256 devices in a mesh: gx: 16 (over y, z_hi, core), gy: 16 (over x, z_lo).
Axes of the slice: x: 4, y: 4, z: 8 (z_hi: 2, z_lo: 4; z = z_hi * 4 + z_lo), core: 2. Of those that a mesh axis runs over, the one named last changes fastest.
Arguments:
- template: bfloat16 [512, 512, 256], P('gx', 'gy'), may hold values from -6 to 6
- mismatch: float32 [512, 512, 256], P('gx', 'gy'), may hold values from -6 to 6
- velocity: bfloat16 [2, 3, 512, 512, 256], P(None, None, 'gx', 'gy'), may hold values from -0.29882812 to 0.29882812
- src_ids: int32 [2, 16, 16, 8], P(None, 'gx', 'gy'), may hold values from 0 to 2047, as said below
Outputs:
- velocity_gradient: float32 [2, 3, 512, 512, 256], P(None, None, 'gx', 'gy')
The draws below stay inside these ranges and needn't reach their ends.
Inputs may be any that keep to these rules, and one draw needn't show every extreme that they name: `src_ids`: for a destination block (i, j, l), the source block (a, b, c) has |a - i| <= 1 and |b - j| <= 1; c is any block along the third dimension.
All inputs are finite; a program needn't handle non-finite values.
Results may differ from the reference program's by a relative error of at most 0.0003.
Values may be sent and summed in bfloat16 or wider, within the bound.
No kernel may reach another device: no remote copies, remote signals or barrier semaphores. Data moves between devices by JAX's collectives and lax.ppermute only.
A program may use at most 64 MiB of HBM per device.

```python
import jax
import jax.numpy as jnp

BLK = 32
NZ = 256
NX = 512
NY = 512
NBX = 16
NBY = 16
NBZ = 8


def draw_src_ids(key, part):
    keys = jax.random.split(jax.random.fold_in(key, 71), 3)
    shape = (2, NBX, NBY, NBZ)
    first_home = jnp.arange(NBX, dtype=jnp.int32)[None, :, None, None]
    second_home = jnp.arange(NBY, dtype=jnp.int32)[None, None, :, None]
    step_one = jax.random.randint(keys[0], shape, -1, 2, dtype=jnp.int32)
    step_two = jax.random.randint(keys[1], shape, -1, 2, dtype=jnp.int32)
    first_source = first_home + step_one
    first_source = jnp.where((first_source < 0) | (first_source >= NBX), first_home - step_one, first_source)
    second_source = second_home + step_two
    second_source = jnp.where((second_source < 0) | (second_source >= NBY), second_home - step_two, second_source)
    third_source = jax.random.randint(keys[2], shape, 0, NBZ, dtype=jnp.int32)
    result = (first_source * NBY + second_source) * NBZ + third_source
    result = result.at[0, 0, 0, 0].set(0)
    result = result.at[0, NBX - 1, NBY - 1, NBZ - 1].set(NBX * NBY * NBZ - 1)
    return result.astype(jnp.int32)


def block_scale(key, extent, pieces, smallest, high):
    gain, own = 1.0, jax.random.fold_in(key, 6)
    for axis_at, shards_of in pieces:
        heights = jnp.exp(jax.random.uniform(jax.random.fold_in(own, axis_at), (shards_of,), jnp.float32, smallest / len(pieces), high / len(pieces)))
        gain = gain * jnp.repeat(heights, extent[axis_at] // shards_of).reshape([-1 if axis == axis_at else 1 for axis in range(len(extent))])
    return gain


def bell_draw(own_key, extent, deviation, limit, pieces=(), kind=jnp.bfloat16):
    values = jax.random.normal(own_key, extent, jnp.float32) * deviation
    if len(pieces) > 0:
        values = block_scale(own_key, extent, pieces, -0.22, 0.18) * values
    return jnp.clip(values, min=-limit, max=limit).astype(kind)


def setup_inputs(seed: int = 0) -> dict:
    seeds = jax.random.split(jax.random.key(seed), 5)
    template = bell_draw(seeds[0], (NX, NY, NZ), 1.0, 6.0, ((0, 16), (1, 16)))
    mismatch = bell_draw(seeds[1], (NX, NY, NZ), 1.0, 6.0, ((0, 16), (1, 16)), jnp.float32)
    velocity = jnp.clip(jax.random.uniform(seeds[2], (2, 3, NX, NY, NZ), jnp.float32, -0.29882812, 0.29882812) * block_scale(seeds[2], (2, 3, NX, NY, NZ), ((2, 16), (3, 16)), -0.4, 0.0), -0.29882812, 0.29882812).astype(jnp.bfloat16)
    src_ids = draw_src_ids(jax.random.fold_in(seeds[4], 71), 0)
    return {"template": template, "mismatch": mismatch, "velocity": velocity, "src_ids": src_ids}


def pad_depth(values):
    return jnp.pad(values, [(0, 0)] * (values.ndim - 1) + [(1, 1)])


def pad_plane(values, margin):
    return jnp.pad(values, [(0, 0)] * (values.ndim - 3) + [(margin, margin), (margin, margin), (0, 0)])


def upwind(adjoint, speeds):
    advect = -speeds
    first = adjoint[:, 1:-1]
    speed_one = advect[0, :, 1:-1]
    face_speed = 0.5 * (speed_one[:-1] + speed_one[1:])
    fluxes = jnp.maximum(face_speed, 0.0) * first[:-1] + jnp.minimum(face_speed, 0.0) * first[1:]
    divergence = fluxes[1:] - fluxes[:-1]
    second = adjoint[1:-1]
    speed_two = advect[1, 1:-1]
    face_speed = 0.5 * (speed_two[:, :-1] + speed_two[:, 1:])
    fluxes = jnp.maximum(face_speed, 0.0) * second[:, :-1] + jnp.minimum(face_speed, 0.0) * second[:, 1:]
    divergence = divergence + (fluxes[:, 1:] - fluxes[:, :-1])
    centre = adjoint[1:-1, 1:-1]
    third = pad_depth(centre)
    speed_three = pad_depth(advect[2, 1:-1, 1:-1])
    face_speed = 0.5 * (speed_three[:, :, :-1] + speed_three[:, :, 1:])
    fluxes = jnp.maximum(face_speed, 0.0) * third[:, :, :-1] + jnp.minimum(face_speed, 0.0) * third[:, :, 1:]
    divergence = divergence + (fluxes[:, :, 1:] - fluxes[:, :, :-1])
    return centre - divergence


def slopes(picture):
    along_one = 0.5 * (picture[..., 2:, 1:-1, :] - picture[..., :-2, 1:-1, :])
    along_two = 0.5 * (picture[..., 1:-1, 2:, :] - picture[..., 1:-1, :-2, :])
    centre = pad_depth(picture[..., 1:-1, 1:-1, :])
    along_three = 0.5 * (centre[..., 2:] - centre[..., :-2])
    return jnp.stack([along_one, along_two, along_three], axis=-4)


def smooth(forces):
    centre = forces[..., 1:-1, 1:-1, :]
    deeper = pad_depth(centre)
    beside_all = forces[..., 2:, 1:-1, :] + forces[..., :-2, 1:-1, :]
    beside_all = beside_all + forces[..., 1:-1, 2:, :] + forces[..., 1:-1, :-2, :]
    beside_all = beside_all + deeper[..., 2:] + deeper[..., :-2]
    return 0.25 * centre + 0.125 * beside_all


def displace(template, block_ids):
    blocks = template.reshape(NBX, BLK, NBY, BLK, NBZ, BLK).transpose(0, 2, 4, 1, 3, 5).reshape(-1, BLK, BLK, BLK)
    picked = jnp.take(blocks, block_ids.reshape(-1).astype(jnp.int32), axis=0)
    return picked.reshape(NBX, NBY, NBZ, BLK, BLK, BLK).transpose(0, 3, 1, 4, 2, 5).reshape(NX, NY, NZ)


def reference(template, mismatch, velocity, src_ids):
    adjoint_one = upwind(pad_plane(mismatch, 1), pad_plane(velocity[1].astype(jnp.float32), 1))
    adjoint_zero = upwind(pad_plane(adjoint_one, 1), pad_plane(velocity[0].astype(jnp.float32), 1))
    adjoints = [adjoint_zero, adjoint_one]
    results = []
    for instant in (0, 1):
        picture = displace(template, src_ids[instant]).astype(jnp.float32)
        forces = adjoints[instant][None] * slopes(pad_plane(picture, 1))
        results.append(velocity[instant].astype(jnp.float32) + smooth(pad_plane(forces, 1)))
    return jnp.stack(results)
```

```python
import functools

import jax
import jax.numpy as jnp
from jax import lax
from jax.experimental import pallas as pl
from jax.experimental.pallas import tpu as pltpu
from jax.sharding import PartitionSpec as P

F32 = jnp.float32
BF16 = jnp.bfloat16
VMEM_LIMIT = 48 << 20


def whole(shape):
    return pl.BlockSpec(shape, lambda *_: (0,) * len(shape))


def call(kernel, outs, scratch, name, in_specs, aliases=None, out_specs=None):
    return pl.pallas_call(
        kernel,
        name=name,
        grid=(1,),
        in_specs=in_specs,
        out_specs=out_specs or [whole(o.shape) for o in outs],
        out_shape=outs,
        scratch_shapes=scratch,
        input_output_aliases=aliases or {},
        compiler_params=pltpu.CompilerParams(vmem_limit_bytes=VMEM_LIMIT),
    )


def struct(shape, dtype):
    return jax.ShapeDtypeStruct(shape, dtype)


def face_flux(here, following, speed_here, speed_following):
    total = speed_here + speed_following
    return jnp.minimum(total, 0.0) * here + jnp.maximum(total, 0.0) * following


def upwind_kernel(
    field_at, speed_at,
    p_ref, v_ref, pxl, pxh, pyl, pyh, vxl, vxh, vyl, vyh,
    o_ref, fxl, fxh, fyl, fyh,
    s_pl, s_ph, s_vl, s_vh, s_fl, s_fh,
):
    nx, ny, nz = p_ref.shape
    s_pl[...] = pyl[field_at].astype(F32)
    s_ph[...] = pyh[field_at].astype(F32)
    s_vl[...] = vyl[speed_at].astype(F32)
    s_vh[...] = vyh[speed_at].astype(F32)
    rows = lax.broadcasted_iota(jnp.int32, (ny, nz), 0)
    lanes = lax.broadcasted_iota(jnp.int32, (ny, nz), 1)

    def plane(x, flux_below, p_next, vx_next):
        p = p_ref[x]
        flux_above = face_flux(p, p_next, v_ref[0, 0, x].astype(F32), vx_next)
        change = flux_above - flux_below
        vy = v_ref[0, 1, x].astype(F32)
        at = pl.ds(x, 1)
        p_up = jnp.where(rows == ny - 1, s_ph[at, :], pltpu.roll(p, ny - 1, 0))
        v_up = jnp.where(rows == ny - 1, s_vh[at, :], pltpu.roll(vy, ny - 1, 0))
        upper = face_flux(p, p_up, vy, v_up)
        first = face_flux(s_pl[at, :], p[0:1], s_vl[at, :], vy[0:1])
        change = change + (upper - jnp.where(rows == 0, first, pltpu.roll(upper, 1, 0)))
        vz = v_ref[0, 2, x].astype(F32)
        p_up = jnp.where(lanes == nz - 1, 0.0, pltpu.roll(p, nz - 1, 1))
        v_up = jnp.where(lanes == nz - 1, 0.0, pltpu.roll(vz, nz - 1, 1))
        upper = face_flux(p, p_up, vz, v_up)
        lower = jnp.where(lanes == 0, jnp.maximum(vz, 0.0) * p, pltpu.roll(upper, 1, 1))
        change = change + (upper - lower)
        out = p + 0.5 * change
        o_ref[x] = out
        s_fl[at, :] = out[0:1]
        s_fh[at, :] = out[ny - 1 : ny]
        return flux_above

    flux = face_flux(pxl[field_at].astype(F32), p_ref[0], vxl[speed_at].astype(F32), v_ref[0, 0, 0].astype(F32))
    flux = lax.fori_loop(
        0, nx - 1, lambda x, f: plane(x, f, p_ref[x + 1], v_ref[0, 0, x + 1].astype(F32)), flux
    )
    plane(nx - 1, flux, pxh[field_at].astype(F32), vxh[speed_at].astype(F32))
    fxl[0] = o_ref[0].astype(BF16)
    fxh[0] = o_ref[nx - 1].astype(BF16)
    fyl[0] = s_fl[...].astype(BF16)
    fyh[0] = s_fh[...].astype(BF16)


def upwind(field, velocity, instant, field_halo, field_at, speed_halo, speed_at, name):
    nx, ny, nz = field.shape
    lines = {"x": (1, ny, nz), "y": (1, nx, nz)}
    outs = [struct(field.shape, F32)] + [struct(lines[d], BF16) for d in "xxyy"]
    in_specs = (
        [whole(field.shape), pl.BlockSpec((1, 3, nx, ny, nz), lambda *_: (instant, 0, 0, 0, 0))]
        + [whole(h.shape) for h in field_halo]
        + [whole(h.shape) for h in speed_halo]
    )
    scratch = [pltpu.VMEM((nx, nz), F32)] * 6
    kernel = functools.partial(upwind_kernel, field_at, speed_at)
    return call(kernel, outs, scratch, name, in_specs)(field, velocity, *field_halo, *speed_halo)


def pick_kernel(planes, t_lo, t_own, t_hi, q_ref, *outs):
    nz = t_own.shape[2]
    ny = t_own.shape[1]
    blocks = []
    for ref in (t_lo, t_own, t_hi):
        parts = [ref[a:b].reshape((b - a) * ny, nz) for a, b in planes]
        blocks.append(parts[0] if len(parts) == 1 else jnp.concatenate(parts, axis=0))
    rows = jnp.concatenate(blocks, axis=1)
    count = rows.shape[0] // ny
    for d, out in enumerate(outs):
        got = jnp.dot(rows, q_ref[d], preferred_element_type=F32).astype(BF16)
        out[0] = got[:, :nz].reshape(count, ny, nz)
        out[1] = got[:, nz:].reshape(count, ny, nz)


def pick(columns, choices, planes, name):
    _, ny, nz = columns[0].shape
    count = sum(b - a for a, b in planes)
    outs = [struct((2, count, ny, nz), BF16)] * choices.shape[0]
    in_specs = [whole(c.shape) for c in columns] + [whole(choices.shape)]
    return call(functools.partial(pick_kernel, planes), outs, [], name, in_specs)(*columns, choices)


def edge_kernel(own, la, ra, lb, rb, xlo, xhi, first, last, s_first, s_last):
    _, nx, ny, nz = own.shape

    def put(x, cells):
        at = pl.ds(x, 1)
        for c in range(2):
            s_first[c, at, :] = cells[c : c + 1]
            s_last[c, at, :] = cells[ny - 2 + c : ny - 1 + c]

    put(0, xlo[0, 1].astype(F32))
    put(nx + 1, xhi[0, 0].astype(F32))
    for x, a in ((0, 0), (1, 1), (nx - 2, 2), (nx - 1, 3)):
        put(x + 1, (own[0, x] + la[0, a] + ra[0, a]).astype(F32))

    def step(x, carry):
        put(x + 3, (own[0, x + 2] + lb[0, x] + rb[0, x]).astype(F32))
        return carry

    lax.fori_loop(0, nx - 4, step, 0)
    first[...] = s_first[...].astype(BF16)
    last[...] = s_last[...].astype(BF16)


def at_instant(shape, instant):
    block = (1,) + tuple(shape[1:])
    return pl.BlockSpec(block, lambda *_: (instant,) + (0,) * (len(block) - 1))


def edges(instant, own, la, ra, lb, rb, xlo, xhi):
    _, nx, ny, nz = own.shape
    ins = (own, la, ra, lb, rb, xlo, xhi)
    in_specs = [at_instant(a.shape, instant if a.shape[0] == 2 else 0) for a in ins]
    outs = [struct((2, nx + 2, nz), BF16)] * 2
    scratch = [pltpu.VMEM((2, nx + 2, nz), F32)] * 2
    return call(edge_kernel, outs, scratch, f"edges_{instant}", in_specs)(*ins)


def force_kernel(
    has_old, own, la, ra, lb, rb, xlo, xhi, ylo, yhi, adj, axl, axh, ayl, ayh, vel, *rest
):
    out, img, frc, s_ylo, s_yhi, s_c0, s_c1, s_fl, s_fh, s_al, s_ah = rest[1:] if has_old else rest
    nx, ny, nz = adj.shape
    rows = lax.broadcasted_iota(jnp.int32, (ny, nz), 0)
    lanes = lax.broadcasted_iota(jnp.int32, (ny, nz), 1)

    def fill(x, cells):
        cells = cells.astype(F32)
        img[x + 2] = cells
        return cells

    def fill_inner(x, cells):
        cells = fill(x, cells)
        s_c0[pl.ds(x, 1), :] = cells[0:1]
        s_c1[pl.ds(x, 1), :] = cells[ny - 1 : ny]

    for h in range(2):
        fill(h - 2, xlo[0, h])
        fill(nx + h, xhi[0, h])
    for x, a in ((0, 0), (1, 1), (nx - 2, 2), (nx - 1, 3)):
        fill_inner(x, own[0, x] + la[0, a] + ra[0, a])

    def fill_step(x, carry):
        fill_inner(x + 2, own[0, x + 2] + lb[0, x] + rb[0, x])
        return carry

    lax.fori_loop(0, nx - 4, fill_step, 0)
    s_ylo[...] = ylo[...].astype(F32)
    s_yhi[...] = yhi[...].astype(F32)
    s_al[...] = ayl[0].astype(F32)
    s_ah[...] = ayh[0].astype(F32)

    def along_z(cells, index, length):
        after = jnp.where(index == length - 1, 0.0, pltpu.roll(cells, length - 1, cells.ndim - 1))
        before = jnp.where(index == 0, 0.0, pltpu.roll(cells, 1, cells.ndim - 1))
        return after, before

    def forces(x, half):
        cells = img[x + 2]
        at = pl.ds(x + 1, 1)
        frc[0, x + 1] = half * (img[x + 3] - img[x + 1])
        up = jnp.where(rows == ny - 1, s_yhi[0, at, :], pltpu.roll(cells, ny - 1, 0))
        down = jnp.where(rows == 0, s_ylo[1, at, :], pltpu.roll(cells, 1, 0))
        frc[1, x + 1] = half * (up - down)
        after, before = along_z(cells, lanes, nz)
        frc[2, x + 1] = half * (after - before)

    forces(-1, 0.5 * axl[0].astype(F32))
    forces(nx, 0.5 * axh[0].astype(F32))

    def force_step(x, carry):
        forces(x, 0.5 * adj[x])
        return carry

    lax.fori_loop(0, nx, force_step, 0)
    lines = lax.broadcasted_iota(jnp.int32, (nx, nz), 1)
    for cols, near, far, beside, half, dest, sign in (
        (s_ylo, 1, 0, s_c0, s_al, s_fl, 1.0),
        (s_yhi, 0, 1, s_c1, s_ah, s_fh, -1.0),
    ):
        weight = 0.5 * half[...]
        dest[0] = weight * (cols[near, 2 : nx + 2, :] - cols[near, 0:nx, :])
        dest[1] = (sign * weight) * (beside[...] - cols[far, 1 : nx + 1, :])
        after, before = along_z(cols[near, 1 : nx + 1, :], lines, nz)
        dest[2] = weight * (after - before)

    def smooth_step(x, carry):
        at = pl.ds(x, 1)
        for c in range(3):
            f = frc[c, x + 1]
            up = jnp.where(rows == ny - 1, s_fh[c, at, :], pltpu.roll(f, ny - 1, 0))
            down = jnp.where(rows == 0, s_fl[c, at, :], pltpu.roll(f, 1, 0))
            after, before = along_z(f, lanes, nz)
            beside = (frc[c, x] + frc[c, x + 2]) + (up + down) + (after + before)
            out[0, c, x] = vel[0, c, x].astype(F32) + (0.25 * f + 0.125 * beside)
        return carry

    lax.fori_loop(0, nx, smooth_step, 0)


def force(instant, own, la, ra, lb, rb, xlo, xhi, ylo, yhi, adj, adj_halo, velocity, old):
    nx, ny, nz = adj.shape
    ins = [own, la, ra, lb, rb, xlo, xhi]
    in_specs = [at_instant(a.shape, instant if a.shape[0] == 2 else 0) for a in ins]
    more = [ylo, yhi, adj, *adj_halo]
    in_specs += [whole(a.shape) for a in more]
    block = pl.BlockSpec((1, 3, nx, ny, nz), lambda *_: (instant, 0, 0, 0, 0))
    ins += more + [velocity]
    in_specs += [block]
    aliases = {}
    if old is not None:
        aliases = {len(ins): 0}
        ins += [old]
        in_specs += [pl.BlockSpec(memory_space=pl.ANY)]
    scratch = [
        pltpu.VMEM((nx + 4, ny, nz), F32),
        pltpu.VMEM((3, nx + 2, ny, nz), F32),
        pltpu.VMEM((2, nx + 2, nz), F32),
        pltpu.VMEM((2, nx + 2, nz), F32),
        pltpu.VMEM((nx, nz), F32),
        pltpu.VMEM((nx, nz), F32),
        pltpu.VMEM((3, nx, nz), F32),
        pltpu.VMEM((3, nx, nz), F32),
        pltpu.VMEM((nx, nz), F32),
        pltpu.VMEM((nx, nz), F32),
    ]
    return call(
        functools.partial(force_kernel, old is not None),
        struct((2, 3, nx, ny, nz), F32),
        scratch,
        f"force_{instant}",
        in_specs,
        aliases,
        block,
    )(*ins)


def forward(value, axis):
    ends = lax.axis_size(axis) - 1
    return lax.ppermute(value, axis, [(i, i + 1) for i in range(ends)])


def backward(value, axis):
    ends = lax.axis_size(axis) - 1
    return lax.ppermute(value, axis, [(i + 1, i) for i in range(ends)])


def after(value, *others):
    return lax.optimization_barrier((value,) + others)[0]


def body(template, mismatch, velocity, src_ids):
    nx, ny, nz = template.shape
    depth_blocks = src_ids.shape[3]
    edge = nz // depth_blocks
    index_first = lax.axis_index("gx")
    index_second = lax.axis_index("gy")
    count_second = lax.axis_size("gy")

    t_lo = forward(template, "gx")
    t_hi = backward(template, "gx")
    own_ids = src_ids.reshape(2, depth_blocks)
    left_ids = forward(own_ids, "gy")
    right_ids = backward(own_ids, "gy")

    def face_message(x, y):
        if x is not None:
            parts = [mismatch[x].astype(BF16), velocity[0, 0, x], velocity[1, 0, x]]
        else:
            parts = [mismatch[:, y].astype(BF16), velocity[0, 1, :, y], velocity[1, 1, :, y]]
        return jnp.stack(parts)

    halo = (
        forward(face_message(nx - 1, None), "gx"),
        backward(face_message(0, None), "gx"),
        forward(face_message(None, ny - 1), "gy"),
        backward(face_message(None, 0), "gy"),
    )

    def choice(ids):
        first_block = ids // (count_second * depth_blocks)
        second_block = ids // depth_blocks % count_second
        start = (first_block - index_first + 1) * nz + ids % depth_blocks * edge
        start = jnp.where(second_block == index_second, start, -4 * nz)
        rows = jnp.repeat(start.reshape(-1), edge) + jnp.tile(jnp.arange(edge), 2 * depth_blocks)
        return (jnp.arange(3 * nz)[:, None] == rows[None, :]).astype(BF16)

    send_choice = jnp.stack([choice(left_ids), choice(right_ids)])
    own_choice = choice(own_ids)[None]

    adj_one, *faces = upwind(mismatch, velocity, 1, halo, 0, halo, 2, "upwind_1")

    columns = (t_lo, template, t_hi)
    outer = ((0, 2), (nx - 2, nx))
    inner = ((2, nx - 2),)
    to_left_a, to_right_a = pick(columns, send_choice, outer, "pick_outer")
    from_left_a = forward(to_right_a, "gy")
    from_right_a = backward(to_left_a, "gy")
    to_left_b, to_right_b = pick(columns, send_choice, inner, "pick_inner")
    from_left_b = [forward(to_right_b[k : k + 1], "gy") for k in range(2)]
    from_right_b = [backward(to_left_b[k : k + 1], "gy") for k in range(2)]
    (own,) = pick(columns, own_choice, ((0, nx),), "pick_own")

    def exchange(faces):
        low_x, high_x, low_y, high_y = faces
        return (
            forward(high_x, "gx"),
            backward(low_x, "gx"),
            forward(high_y, "gy"),
            backward(low_y, "gy"),
        )

    adj_one_halo = exchange(faces)
    adj_zero, *faces = upwind(adj_one, velocity, 0, adj_one_halo, 0, halo, 1, "upwind_0")
    adj_zero_halo = exchange(faces)

    own_outer = jnp.concatenate([own[:, :2], own[:, nx - 2 :]], axis=1)
    outer_image = own_outer + from_left_a + from_right_a
    x_lo = forward(outer_image[:, 2:], "gx")
    x_hi = backward(outer_image[:, :2], "gx")

    result = None
    for k, adj, adj_halo in ((0, adj_zero, adj_zero_halo), (1, adj_one, adj_one_halo)):
        parts = (own, from_left_a, from_right_a, from_left_b[k], from_right_b[k], x_lo, x_hi)
        first, last = edges(k, *parts)
        y_lo = forward(last, "gy")
        y_hi = backward(first, "gy")
        result = force(k, *parts, y_lo, y_hi, adj, adj_halo, velocity, result)
    return result


def solution(mesh):
    in_specs = (
        P("gx", "gy", None),
        P("gx", "gy", None),
        P(None, None, "gx", "gy", None),
        P(None, "gx", "gy", None),
    )
    out_specs = P(None, None, "gx", "gy", None)
    return jax.shard_map(body, mesh=mesh, in_specs=in_specs, out_specs=out_specs, check_vma=False)
```

```python
import functools

import jax
import jax.numpy as jnp
from jax import lax
from jax.experimental import pallas as pl
from jax.experimental.pallas import tpu as pltpu
from jax.sharding import PartitionSpec as P

F32 = jnp.float32
BF16 = jnp.bfloat16
VMEM_LIMIT = 48 << 20


def whole(shape):
    return pl.BlockSpec(shape, lambda *_: (0,) * len(shape))


def call(kernel, outs, scratch, name, in_specs, out_specs=None, steps=1):
    return pl.pallas_call(
        kernel,
        name=name,
        grid=(steps,),
        in_specs=in_specs,
        out_specs=out_specs or [whole(o.shape) for o in outs],
        out_shape=outs,
        scratch_shapes=scratch,
        cost_estimate=pl.CostEstimate(flops=0, transcendentals=0, bytes_accessed=0),
        compiler_params=pltpu.CompilerParams(vmem_limit_bytes=VMEM_LIMIT),
    )


def struct(shape, dtype):
    return jax.ShapeDtypeStruct(shape, dtype)


def face_flux(here, following, speed_here, speed_following):
    total = speed_here + speed_following
    return jnp.minimum(total, 0.0) * here + jnp.maximum(total, 0.0) * following


def depth_change(p, vz):
    nz = p.shape[1]
    lanes = lax.broadcasted_iota(jnp.int32, p.shape, 1)
    p_up = jnp.where(lanes == nz - 1, 0.0, pltpu.roll(p, nz - 1, 1))
    v_up = jnp.where(lanes == nz - 1, 0.0, pltpu.roll(vz, nz - 1, 1))
    upper = face_flux(p, p_up, vz, v_up)
    lower = jnp.where(lanes == 0, jnp.maximum(vz, 0.0) * p, pltpu.roll(upper, 1, 1))
    return upper - lower


def plane_change(p, vy, vz, below, above):
    ny = p.shape[0]
    rows = lax.broadcasted_iota(jnp.int32, p.shape, 0)
    p_up = jnp.where(rows == ny - 1, above[0], pltpu.roll(p, ny - 1, 0))
    v_up = jnp.where(rows == ny - 1, above[1], pltpu.roll(vy, ny - 1, 0))
    upper = face_flux(p, p_up, vy, v_up)
    first = face_flux(below[0], p[0:1], below[1], vy[0:1])
    lower = jnp.where(rows == 0, first, pltpu.roll(upper, 1, 0))
    return (upper - lower) + depth_change(p, vz)


NEAR_P, FAR_P, NEAR_N, FAR_N, NEAR_T, NEAR_Z, NEAR_EARLY = range(7)


def rows_kernel(p_ref, v_ref, hxl, hxh, code, lo, hi, s_lo, s_hi):
    nx, ny, _ = p_ref.shape
    s_lo[...] = jnp.zeros(s_lo.shape, F32)
    s_hi[...] = jnp.zeros(s_hi.shape, F32)

    def put(layer, x, cells, width):
        at = pl.ds(x + 1, 1)
        for d in range(width):
            s_lo[layer + d, at, :] = cells[d : d + 1]
            s_hi[layer + d, at, :] = cells[ny - 1 - d : ny - d]

    def step(x, carry):
        put(NEAR_P, x, p_ref[x], 2)
        put(NEAR_N, x, v_ref[1, 1, x].astype(F32), 2)
        put(NEAR_T, x, v_ref[1, 0, x].astype(F32), 1)
        put(NEAR_Z, x, v_ref[1, 2, x].astype(F32), 1)
        put(NEAR_EARLY, x, v_ref[0, 1, x].astype(F32), 1)
        return carry

    lax.fori_loop(0, nx, step, 0)
    for x, halo in ((-1, hxl), (nx, hxh)):
        put(NEAR_P, x, halo[NEAR_P].astype(F32), 1)
        put(NEAR_N, x, halo[NEAR_T].astype(F32), 1)
        put(NEAR_T, x, halo[NEAR_N].astype(F32), 1)
    s_lo[FAR_P, 0:1, :] = code[...]
    s_hi[FAR_P, 0:1, :] = code[...]
    lo[...] = s_lo[...].astype(BF16)
    hi[...] = s_hi[...].astype(BF16)


def upwind_one_kernel(
    inside, p_ref, v_ref, hxl, hxh, hyl, hyh, out, oxl, oxh, oyl, oyh,
    s_yl, s_yh, s_p0, s_p1, s_v0, s_v1,
):
    nx, ny, nz = p_ref.shape
    s_yl[...] = hyl[...].astype(F32)
    s_yh[...] = hyh[...].astype(F32)

    def plane(x, flux_below, p, speeds, p_next, vx_next):
        vx, vy, vz = speeds
        flux_above = face_flux(p, p_next, vx, vx_next)
        at = pl.ds(x + 1, 1)
        below = s_yl[NEAR_P, at, :], s_yl[NEAR_N, at, :]
        above = s_yh[NEAR_P, at, :], s_yh[NEAR_N, at, :]
        change = (flux_above - flux_below) + plane_change(p, vy, vz, below, above)
        return p + 0.5 * change, flux_above

    def speed(c, x):
        return v_ref[0, c, x].astype(F32)

    def halo_plane(halo):
        return [halo[i].astype(F32) for i in (NEAR_P, FAR_P, NEAR_N, FAR_N, NEAR_T, NEAR_Z)]

    p, p_far, vx, vx_far, vy, vz = halo_plane(hxl)
    flux = face_flux(p_far, p, vx_far, vx)
    got, flux = plane(-1, flux, p, (vx, vy, vz), p_ref[0], speed(0, 0))
    oxl[...] = got * inside[0]
    p_high, p_far, vx_high, vx_far, vy_high, vz_high = halo_plane(hxh)

    def inner(x, flux, p_next, vx_next):
        p = p_ref[x]
        vy = speed(1, x)
        got, flux = plane(x, flux, p, (speed(0, x), vy, speed(2, x)), p_next, vx_next)
        out[x] = got
        at = pl.ds(x, 1)
        s_p0[at, :] = p[0:1]
        s_p1[at, :] = p[ny - 1 : ny]
        s_v0[at, :] = vy[0:1]
        s_v1[at, :] = vy[ny - 1 : ny]
        return flux

    flux = lax.fori_loop(0, nx - 1, lambda x, f: inner(x, f, p_ref[x + 1], speed(0, x + 1)), flux)
    flux = inner(nx - 1, flux, p_high, vx_high)
    got, _ = plane(nx, flux, p_high, (vx_high, vy_high, vz_high), p_far, vx_far)
    oxh[...] = got * inside[1]

    for scr, edge_p, edge_v, dest, flag, sign in (
        (s_yl, s_p0, s_v0, oyl, inside[2], 1.0),
        (s_yh, s_p1, s_v1, oyh, inside[3], -1.0),
    ):
        mid = slice(1, nx + 1)
        p, vy = scr[NEAR_P, mid, :], scr[NEAR_N, mid, :]
        flux_x = face_flux(
            scr[NEAR_P, 0 : nx + 1, :], scr[NEAR_P, 1 : nx + 2, :],
            scr[NEAR_T, 0 : nx + 1, :], scr[NEAR_T, 1 : nx + 2, :],
        )
        change = flux_x[1:] - flux_x[:-1]
        far = (scr[FAR_P, mid, :], scr[FAR_N, mid, :])
        near = (edge_p[...], edge_v[...])
        before, following = (far, near) if sign > 0 else (near, far)
        change = change + (
            face_flux(p, following[0], vy, following[1]) - face_flux(before[0], p, before[1], vy)
        )
        change = change + depth_change(p, scr[NEAR_Z, mid, :])
        dest[...] = (p + 0.5 * change) * flag


def upwind_zero_kernel(
    p_ref, v_ref, pxl, pxh, pyl, pyh, hxl, hxh, hyl, hyh, out, fxl, fxh, fyl, fyh,
    s_vl, s_vh, s_fl, s_fh,
):
    nx, ny, nz = p_ref.shape
    s_vl[...] = hyl[NEAR_EARLY].astype(F32)
    s_vh[...] = hyh[NEAR_EARLY].astype(F32)

    def speed(c, x):
        return v_ref[0, c, x].astype(F32)

    def plane(x, flux_below, p_next, vx_next):
        p = p_ref[x]
        flux_above = face_flux(p, p_next, speed(0, x), vx_next)
        at, halo_at = pl.ds(x, 1), pl.ds(x + 1, 1)
        below = pyl[at, :], s_vl[halo_at, :]
        above = pyh[at, :], s_vh[halo_at, :]
        change = (flux_above - flux_below) + plane_change(p, speed(1, x), speed(2, x), below, above)
        got = p + 0.5 * change
        out[x] = got
        s_fl[at, :] = got[0:1]
        s_fh[at, :] = got[ny - 1 : ny]
        return flux_above

    flux = face_flux(pxl[...], p_ref[0], hxl[NEAR_EARLY].astype(F32), speed(0, 0))
    flux = lax.fori_loop(0, nx - 1, lambda x, f: plane(x, f, p_ref[x + 1], speed(0, x + 1)), flux)
    plane(nx - 1, flux, pxh[...], hxh[NEAR_EARLY].astype(F32))
    fxl[0] = out[0].astype(BF16)
    fxh[0] = out[nx - 1].astype(BF16)
    fyl[0] = s_fl[...].astype(BF16)
    fyh[0] = s_fh[...].astype(BF16)


def speeds_spec(velocity, instant):
    block = (1,) + velocity.shape[1:]
    return pl.BlockSpec(block, lambda *_: (instant,) + (0,) * (len(block) - 1))


def upwind_one(inside, field, velocity, halo):
    nx, ny, nz = field.shape
    line = struct((ny, nz), F32)
    in_specs = [pl.BlockSpec(memory_space=pltpu.SMEM), whole(field.shape), speeds_spec(velocity, 1)]
    in_specs += [whole(h.shape) for h in halo]
    scratch = [pltpu.VMEM(halo[2].shape, F32)] * 2 + [pltpu.VMEM((nx, nz), F32)] * 4
    outs = [struct(field.shape, F32)] + [line] * 4
    return call(upwind_one_kernel, outs, scratch, "upwind_one", in_specs)(inside, field, velocity, *halo)


def upwind_zero(field, velocity, field_halo, halo):
    nx, ny, nz = field.shape
    in_specs = [whole(field.shape), speeds_spec(velocity, 0)]
    in_specs += [whole(h.shape) for h in (*field_halo, *halo)]
    scratch = [pltpu.VMEM((nx + 2, nz), F32)] * 2 + [pltpu.VMEM((nx, nz), F32)] * 2
    outs = [struct(field.shape, F32)] + [struct((1, ny, nz), BF16)] * 4
    return call(upwind_zero_kernel, outs, scratch, "upwind_zero", in_specs)(
        field, velocity, *field_halo, *halo
    )


def pick_kernel(planes, t_lo, t_own, t_hi, q_ref, *outs):
    nz = t_own.shape[2]
    ny = t_own.shape[1]
    blocks = []
    for ref in (t_lo, t_own, t_hi):
        parts = [ref[a:b].reshape((b - a) * ny, nz) for a, b in planes]
        blocks.append(parts[0] if len(parts) == 1 else jnp.concatenate(parts, axis=0))
    rows = jnp.concatenate(blocks, axis=1)
    count = rows.shape[0] // ny
    for d, out in enumerate(outs):
        got = jnp.dot(rows, q_ref[d], preferred_element_type=F32).astype(BF16)
        out[0] = got[:, :nz].reshape(count, ny, nz)
        out[1] = got[:, nz:].reshape(count, ny, nz)


def pick(columns, choices, planes, name):
    _, ny, nz = columns[0].shape
    count = sum(b - a for a, b in planes)
    outs = [struct((2, count, ny, nz), BF16)] * choices.shape[0]
    in_specs = [whole(c.shape) for c in columns] + [whole(choices.shape)]
    return call(functools.partial(pick_kernel, planes), outs, [], name, in_specs)(*columns, choices)


def outer_kernel(own, la, ra, face_lo, face_hi, low, high):
    nx, count = own.shape[1], la.shape[1]
    for k in range(2):
        for c in range(2):
            low[2 * k + c] = own[k, c] + la[k, c] + ra[k, c]
            x, a = nx - 2 + c, count - 2 + c
            high[2 * k + c] = own[k, x] + la[k, a] + ra[k, a]
    low[4] = face_lo[0]
    high[4] = face_hi[0]


def each_plane(groups, own, la, ra, lb, rb, k, visit):
    for planes, lefts, rights in ((groups[0], la, ra), (groups[1], lb, rb)):
        at = 0
        for a, b in planes:

            def step(x, carry, shift=at - a, lefts=lefts, rights=rights):
                visit(x, own[k, x] + lefts[k, x + shift] + rights[k, x + shift])
                return carry

            lax.fori_loop(a, b, step, 0)
            at += b - a


def edge_kernel(
    groups, own, la, ra, lb, rb, xlo, xhi, face_lo, face_hi, first, final, s_first, s_final
):
    _, nx, ny, nz = own.shape
    for k in range(2):

        def put(x, cells, k=k):
            at = pl.ds(x + 1, 1)
            cells = cells.astype(F32)
            for c in range(2):
                s_first[2 * k + c, at, :] = cells[c : c + 1]
                s_final[2 * k + c, at, :] = cells[ny - 2 + c : ny - 1 + c]

        put(-1, xlo[2 * k + 1])
        put(nx, xhi[2 * k])
        each_plane(groups, own, la, ra, lb, rb, k, put)
    for faces, scr, msg in ((face_lo, s_first, first), (face_hi, s_final, final)):
        msg[0:4] = scr[...].astype(BF16)
        msg[4] = jnp.zeros(msg.shape[1:], BF16)
        msg[4, 0:nx] = faces[0]


def force_kernel(
    groups, own, la, ra, lb, rb, band, xlo, xhi, ylo, yhi, adj0, adj1, bxl, bxh, byl, byh, vel,
    out, img, packed, frc, s_ylo, s_yhi, s_c0, s_c1, s_fl, s_fh, s_al, s_ah,
):
    k = pl.program_id(0)
    nx, ny, nz = adj0.shape
    rows = lax.broadcasted_iota(jnp.int32, (ny, nz), 0)
    lanes = lax.broadcasted_iota(jnp.int32, (ny, nz), 1)
    first_image = k == 0

    def this(zero, one):
        return jnp.where(first_image, zero.astype(F32), one.astype(F32))

    for h in range(2):
        img[h] = xlo[2 * k + h].astype(F32)
        img[nx + 2 + h] = xhi[2 * k + h].astype(F32)

    def fill(x, cells):
        packed[x] = cells
        cells = cells.astype(F32)
        img[x + 2] = cells
        s_c0[pl.ds(x, 1), :] = cells[0:1]
        s_c1[pl.ds(x, 1), :] = cells[ny - 1 : ny]

    each_plane(groups, own, la, ra, lb, rb, 0, fill)
    every = packed[...].reshape(nx * ny, nz)
    frc[2, 1 : nx + 1] = jnp.dot(every, band[...], preferred_element_type=F32).reshape(nx, ny, nz)
    for h in range(2):
        s_ylo[h] = ylo[2 * k + h].astype(F32)
        s_yhi[h] = yhi[2 * k + h].astype(F32)
    s_al[...] = this(ylo[4, 0:nx], byl[...])
    s_ah[...] = this(yhi[4, 0:nx], byh[...])

    def along_z(cells, index, length):
        following = jnp.where(index == length - 1, 0.0, pltpu.roll(cells, length - 1, 1))
        before = jnp.where(index == 0, 0.0, pltpu.roll(cells, 1, 1))
        return following, before

    def forces(x, half, slope_z):
        cells = img[x + 2]
        at = pl.ds(x + 1, 1)
        frc[0, x + 1] = half * (img[x + 3] - img[x + 1])
        up = jnp.where(rows == ny - 1, s_yhi[0, at, :], pltpu.roll(cells, ny - 1, 0))
        down = jnp.where(rows == 0, s_ylo[1, at, :], pltpu.roll(cells, 1, 0))
        frc[1, x + 1] = half * (up - down)
        frc[2, x + 1] = half * slope_z

    for x, half in ((-1, 0.5 * this(xlo[4], bxl[...])), (nx, 0.5 * this(xhi[4], bxh[...]))):
        following, before = along_z(img[x + 2], lanes, nz)
        forces(x, half, following - before)

    def force_step(x, carry):
        forces(x, 0.5 * this(adj0[x], adj1[x]), frc[2, x + 1])
        return carry

    lax.fori_loop(0, nx, force_step, 0)
    lines = lax.broadcasted_iota(jnp.int32, (nx, nz), 1)
    for cols, near, far, beside, half, dest, sign in (
        (s_ylo, 1, 0, s_c0, s_al, s_fl, 1.0),
        (s_yhi, 0, 1, s_c1, s_ah, s_fh, -1.0),
    ):
        weight = 0.5 * half[...]
        dest[0] = weight * (cols[near, 2 : nx + 2, :] - cols[near, 0:nx, :])
        dest[1] = (sign * weight) * (beside[...] - cols[far, 1 : nx + 1, :])
        following, before = along_z(cols[near, 1 : nx + 1, :], lines, nz)
        dest[2] = weight * (following - before)

    def smooth_step(x, carry):
        at = pl.ds(x, 1)
        for c in range(3):
            f = frc[c, x + 1]
            up = jnp.where(rows == ny - 1, s_fh[c, at, :], pltpu.roll(f, ny - 1, 0))
            down = jnp.where(rows == 0, s_fl[c, at, :], pltpu.roll(f, 1, 0))
            following, before = along_z(f, lanes, nz)
            beside = (frc[c, x] + frc[c, x + 2]) + (up + down) + (following + before)
            out[0, c, x] = vel[0, c, x].astype(F32) + (0.25 * f + 0.125 * beside)
        return carry

    lax.fori_loop(0, nx, smooth_step, 0)


def force(groups, images, band, x_lo, x_hi, y_lo, y_hi, adj_zero, adj_one, halo_one, velocity):
    nx, ny, nz = adj_zero.shape
    block = pl.BlockSpec((1, 3, nx, ny, nz), lambda k: (k, 0, 0, 0, 0))
    middle = [band, x_lo, x_hi, y_lo, y_hi, adj_zero, adj_one, *halo_one]
    in_specs = [pl.BlockSpec((1,) + a.shape[1:], lambda k: (k, 0, 0, 0)) for a in images]
    in_specs += [whole(a.shape) for a in middle] + [block]
    scratch = [
        pltpu.VMEM((nx + 4, ny, nz), F32),
        pltpu.VMEM((nx, ny, nz), BF16),
        pltpu.VMEM((3, nx + 2, ny, nz), F32),
        pltpu.VMEM((2, nx + 2, nz), F32),
        pltpu.VMEM((2, nx + 2, nz), F32),
        pltpu.VMEM((nx, nz), F32),
        pltpu.VMEM((nx, nz), F32),
        pltpu.VMEM((3, nx, nz), F32),
        pltpu.VMEM((3, nx, nz), F32),
        pltpu.VMEM((nx, nz), F32),
        pltpu.VMEM((nx, nz), F32),
    ]
    return call(
        functools.partial(force_kernel, groups),
        struct((2, 3, nx, ny, nz), F32),
        scratch,
        "force",
        in_specs,
        block,
        2,
    )(*images, *middle, velocity)


def forward(value, axis):
    ends = lax.axis_size(axis) - 1
    return lax.ppermute(value, axis, [(i, i + 1) for i in range(ends)])


def backward(value, axis):
    ends = lax.axis_size(axis) - 1
    return lax.ppermute(value, axis, [(i + 1, i) for i in range(ends)])


def body(template, mismatch, velocity, src_ids):
    nx, ny, nz = template.shape
    depth_blocks = src_ids.shape[3]
    edge = nz // depth_blocks
    slots = 2 * depth_blocks
    index_first = lax.axis_index("gx")
    index_second = lax.axis_index("gy")
    count_first = lax.axis_size("gx")
    count_second = lax.axis_size("gy")

    def x_message(near, far):
        parts = [mismatch[near].astype(BF16), mismatch[far].astype(BF16)]
        parts += [velocity[1, 0, near], velocity[1, 0, far], velocity[1, 1, near]]
        return jnp.stack(parts + [velocity[1, 2, near], velocity[0, 0, near]])

    halo_xl = forward(x_message(nx - 1, nx - 2), "gx")
    halo_xh = backward(x_message(0, 1), "gx")
    t_lo = forward(template, "gx")
    t_hi = backward(template, "gx")

    ids = src_ids.reshape(slots)
    first_block = ids // (count_second * depth_blocks)
    second_block = ids // depth_blocks % count_second
    start = (first_block - index_first + 1) * depth_blocks + ids % depth_blocks
    side = second_block - index_second + 1
    code = (side * (3 * depth_blocks) + start).astype(F32)
    code = jnp.pad(code.reshape(1, slots), ((0, 0), (0, nz - slots)))
    ins = (mismatch, velocity, halo_xl, halo_xh, code)
    rows = struct((7, nx + 2, nz), BF16)
    low, high = call(
        rows_kernel,
        [rows] * 2,
        [pltpu.VMEM(rows.shape, F32)] * 2,
        "rows",
        [whole(a.shape) for a in ins],
    )(*ins)
    halo_yl = forward(high, "gy")
    halo_yh = backward(low, "gy")
    halo = (halo_xl, halo_xh, halo_yl, halo_yh)

    within = jnp.arange(edge)[None, :]

    def choice(wanted, start):
        rows = (jnp.where(wanted, start, -4 * depth_blocks)[:, None] * edge + within).reshape(1, -1)
        return (jnp.arange(3 * nz)[:, None] == rows).astype(BF16)

    def far_choice(message, side):
        code = message[FAR_P, 0, :slots].astype(jnp.int32)
        return choice(code // (3 * depth_blocks) == side, code % (3 * depth_blocks))

    send_choice = jnp.stack([far_choice(halo_yl, 2), far_choice(halo_yh, 0)])
    own_choice = choice(side == 1, start)[None]
    z = jnp.arange(nz)
    band = (z[:, None] == z[None] + 1).astype(BF16) - (z[:, None] == z[None] - 1).astype(BF16)

    columns = (t_lo, template, t_hi)
    margin = nx // 8
    groups = (((0, margin), (nx - margin, nx)), ((margin, nx - margin),))
    to_left_a, to_right_a = pick(columns, send_choice, groups[0], "pick_outer")
    from_left_a = forward(to_right_a, "gy")
    from_right_a = backward(to_left_a, "gy")
    columns, _ = lax.optimization_barrier((columns, to_left_a))
    to_left_b, to_right_b = pick(columns, send_choice, groups[1], "pick_inner")
    from_left_b = forward(to_right_b, "gy")
    from_right_b = backward(to_left_b, "gy")

    late_mismatch, late_choice, _ = lax.optimization_barrier((mismatch, own_choice, to_left_b))
    (own,) = pick(columns, late_choice, ((0, nx),), "pick_own")
    inside = jnp.stack(
        [index_first > 0, index_first < count_first - 1, index_second > 0, index_second < count_second - 1]
    ).astype(F32)
    adj_one, *halo_one = upwind_one(inside, late_mismatch, velocity, halo)
    adj_zero, low_x, high_x, low_y, high_y = upwind_zero(adj_one, velocity, halo_one, halo)

    ins = (own, from_left_a, from_right_a, low_x, high_x)
    low, high = call(
        outer_kernel, [struct((5, ny, nz), BF16)] * 2, [], "outer", [whole(a.shape) for a in ins]
    )(*ins)
    x_lo = forward(high, "gx")
    x_hi = backward(low, "gx")

    images = (own, from_left_a, from_right_a, from_left_b, from_right_b)
    ins = (*images, x_lo, x_hi, low_y, high_y)
    first, final = call(
        functools.partial(edge_kernel, groups),
        [struct((5, nx + 2, nz), BF16)] * 2,
        [pltpu.VMEM((4, nx + 2, nz), F32)] * 2,
        "edges",
        [whole(a.shape) for a in ins],
    )(*ins)
    y_lo = forward(final, "gy")
    y_hi = backward(first, "gy")
    return force(groups, images, band, x_lo, x_hi, y_lo, y_hi, adj_zero, adj_one, halo_one, velocity)


def solution(mesh):
    in_specs = (
        P("gx", "gy", None),
        P("gx", "gy", None),
        P(None, None, "gx", "gy", None),
        P(None, "gx", "gy", None),
    )
    out_specs = P(None, None, "gx", "gy", None)
    return jax.shard_map(body, mesh=mesh, in_specs=in_specs, out_specs=out_specs, check_vma=False)
```

```python
import functools

import jax
import jax.numpy as jnp
from jax import lax
from jax.experimental import pallas as pl
from jax.experimental.pallas import tpu as pltpu
from jax.sharding import PartitionSpec as P

F32 = jnp.float32
BF16 = jnp.bfloat16
VMEM_LIMIT = 48 << 20


def whole(shape):
    return pl.BlockSpec(shape, lambda *_: (0,) * len(shape))


def call(kernel, outs, scratch, name, in_specs, out_specs=None, steps=1):
    return pl.pallas_call(
        kernel,
        name=name,
        grid=(steps,),
        in_specs=in_specs,
        out_specs=out_specs or [whole(o.shape) for o in outs],
        out_shape=outs,
        scratch_shapes=scratch,
        cost_estimate=pl.CostEstimate(flops=0, transcendentals=0, bytes_accessed=0),
        compiler_params=pltpu.CompilerParams(vmem_limit_bytes=VMEM_LIMIT),
    )


def struct(shape, dtype):
    return jax.ShapeDtypeStruct(shape, dtype)


def face_flux(here, following, speed_here, speed_following):
    total = speed_here + speed_following
    return jnp.minimum(total, 0.0) * here + jnp.maximum(total, 0.0) * following


def depth_change(p, vz):
    nz = p.shape[1]
    lanes = lax.broadcasted_iota(jnp.int32, p.shape, 1)
    p_up = jnp.where(lanes == nz - 1, 0.0, pltpu.roll(p, nz - 1, 1))
    v_up = jnp.where(lanes == nz - 1, 0.0, pltpu.roll(vz, nz - 1, 1))
    upper = face_flux(p, p_up, vz, v_up)
    lower = jnp.where(lanes == 0, jnp.maximum(vz, 0.0) * p, pltpu.roll(upper, 1, 1))
    return upper - lower


def plane_change(p, vy, vz, below, above):
    ny = p.shape[0]
    rows = lax.broadcasted_iota(jnp.int32, p.shape, 0)
    p_up = jnp.where(rows == ny - 1, above[0], pltpu.roll(p, ny - 1, 0))
    v_up = jnp.where(rows == ny - 1, above[1], pltpu.roll(vy, ny - 1, 0))
    upper = face_flux(p, p_up, vy, v_up)
    first = face_flux(below[0], p[0:1], below[1], vy[0:1])
    lower = jnp.where(rows == 0, first, pltpu.roll(upper, 1, 0))
    return (upper - lower) + depth_change(p, vz)


NEAR_P, FAR_P, NEAR_N, FAR_N, NEAR_T, NEAR_Z, NEAR_EARLY = range(7)


def column_kernel(p_lo, p_hi, v_lo, v_hi, low, high):
    for msg, p, v, near, far in ((low, p_lo, v_lo, 0, 1), (high, p_hi, v_hi, 1, 0)):
        msg[NEAR_P] = p[near].astype(BF16)
        msg[FAR_P] = p[far].astype(BF16)
        msg[NEAR_N] = v[1, 0, near]
        msg[FAR_N] = v[1, 0, far]
        msg[NEAR_T] = v[1, 1, near]
        msg[NEAR_Z] = v[1, 2, near]
        msg[NEAR_EARLY] = v[0, 0, near]


def column_messages(field, velocity):
    nx, ny, nz = field.shape
    in_specs = [pl.BlockSpec((2, ny, nz), lambda *_, b=b: (b, 0, 0)) for b in (0, nx // 2 - 1)]
    in_specs += [
        pl.BlockSpec((2, 3, 2, ny, nz), lambda *_, b=b: (0, 0, b, 0, 0)) for b in (0, nx // 2 - 1)
    ]
    outs = [struct((7, ny, nz), BF16)] * 2
    return call(column_kernel, outs, [], "columns", in_specs)(
        field, field, velocity, velocity
    )


def rows_kernel(p_ref, v_ref, lo, hi):
    nx, ny, _ = p_ref.shape
    lo[...] = jnp.zeros(lo.shape, F32)
    hi[...] = jnp.zeros(hi.shape, F32)

    def put(layer, x, cells, width):
        for d in range(width):
            at = pl.ds((layer + d) * (nx + 2) + x + 1, 1)
            lo[at, :] = cells[d : d + 1]
            hi[at, :] = cells[ny - 1 - d : ny - d]

    def step(x, carry):
        put(NEAR_P, x, p_ref[x], 2)
        put(NEAR_N, x, v_ref[1, 1, x].astype(F32), 2)
        put(NEAR_T, x, v_ref[1, 0, x].astype(F32), 1)
        put(NEAR_Z, x, v_ref[1, 2, x].astype(F32), 1)
        put(NEAR_EARLY, x, v_ref[0, 1, x].astype(F32), 1)
        return carry

    lax.fori_loop(0, nx, step, 0)


def unpack(ref, flat, layers):
    flat[...] = ref[...].reshape(flat.shape).astype(F32)
    count = layers.shape[1]
    for layer in range(layers.shape[0]):
        layers[layer] = flat[layer * count : (layer + 1) * count, :]


def upwind_one_kernel(
    inside, p_ref, v_ref, hxl, hxh, hyl, hyh, out, oxl, oxh, oyl, oyh,
    s_flat, s_yl, s_yh, s_p0, s_p1, s_v0, s_v1,
):
    nx, ny, nz = p_ref.shape
    unpack(hyl, s_flat, s_yl)
    unpack(hyh, s_flat, s_yh)

    def plane(x, flux_below, p, speeds, p_next, vx_next):
        vx, vy, vz = speeds
        flux_above = face_flux(p, p_next, vx, vx_next)
        at = pl.ds(x + 1, 1)
        below = s_yl[NEAR_P, at, :], s_yl[NEAR_N, at, :]
        above = s_yh[NEAR_P, at, :], s_yh[NEAR_N, at, :]
        change = (flux_above - flux_below) + plane_change(p, vy, vz, below, above)
        return p + 0.5 * change, flux_above

    def speed(c, x):
        return v_ref[0, c, x].astype(F32)

    def halo_plane(halo):
        return [halo[i].astype(F32) for i in (NEAR_P, FAR_P, NEAR_N, FAR_N, NEAR_T, NEAR_Z)]

    p, p_far, vx, vx_far, vy, vz = halo_plane(hxl)
    flux = face_flux(p_far, p, vx_far, vx)
    got, flux = plane(-1, flux, p, (vx, vy, vz), p_ref[0], speed(0, 0))
    oxl[...] = got * inside[0]
    p_high, p_far, vx_high, vx_far, vy_high, vz_high = halo_plane(hxh)

    def inner(x, flux, p_next, vx_next):
        p = p_ref[x]
        vy = speed(1, x)
        got, flux = plane(x, flux, p, (speed(0, x), vy, speed(2, x)), p_next, vx_next)
        out[x] = got
        at = pl.ds(x, 1)
        s_p0[at, :] = p[0:1]
        s_p1[at, :] = p[ny - 1 : ny]
        s_v0[at, :] = vy[0:1]
        s_v1[at, :] = vy[ny - 1 : ny]
        return flux

    flux = lax.fori_loop(0, nx - 1, lambda x, f: inner(x, f, p_ref[x + 1], speed(0, x + 1)), flux)
    flux = inner(nx - 1, flux, p_high, vx_high)
    got, _ = plane(nx, flux, p_high, (vx_high, vy_high, vz_high), p_far, vx_far)
    oxh[...] = got * inside[1]

    for scr, edge_p, edge_v, dest, flag, sign in (
        (s_yl, s_p0, s_v0, oyl, inside[2], 1.0),
        (s_yh, s_p1, s_v1, oyh, inside[3], -1.0),
    ):
        mid = slice(1, nx + 1)
        p, vy = scr[NEAR_P, mid, :], scr[NEAR_N, mid, :]
        flux_x = face_flux(
            scr[NEAR_P, 0 : nx + 1, :], scr[NEAR_P, 1 : nx + 2, :],
            scr[NEAR_T, 0 : nx + 1, :], scr[NEAR_T, 1 : nx + 2, :],
        )
        change = flux_x[1:] - flux_x[:-1]
        far = (scr[FAR_P, mid, :], scr[FAR_N, mid, :])
        near = (edge_p[...], edge_v[...])
        before, following = (far, near) if sign > 0 else (near, far)
        change = change + (
            face_flux(p, following[0], vy, following[1]) - face_flux(before[0], p, before[1], vy)
        )
        change = change + depth_change(p, scr[NEAR_Z, mid, :])
        dest[...] = (p + 0.5 * change) * flag


def upwind_zero_kernel(
    p_ref, v_ref, pxl, pxh, pyl, pyh, hxl, hxh, hyl, hyh, out, fxl, fxh, fyl, fyh,
    s_flat, s_vl, s_vh, s_fl, s_fh,
):
    nx, ny, nz = p_ref.shape
    unpack(hyl, s_flat, s_vl)
    unpack(hyh, s_flat, s_vh)

    def speed(c, x):
        return v_ref[0, c, x].astype(F32)

    def plane(x, flux_below, p_next, vx_next):
        p = p_ref[x]
        flux_above = face_flux(p, p_next, speed(0, x), vx_next)
        at, halo_at = pl.ds(x, 1), pl.ds(x + 1, 1)
        below = pyl[at, :], s_vl[NEAR_EARLY, halo_at, :]
        above = pyh[at, :], s_vh[NEAR_EARLY, halo_at, :]
        change = (flux_above - flux_below) + plane_change(p, speed(1, x), speed(2, x), below, above)
        got = p + 0.5 * change
        out[x] = got
        s_fl[at, :] = got[0:1]
        s_fh[at, :] = got[ny - 1 : ny]
        return flux_above

    flux = face_flux(pxl[...], p_ref[0], hxl[NEAR_EARLY].astype(F32), speed(0, 0))
    flux = lax.fori_loop(0, nx - 1, lambda x, f: plane(x, f, p_ref[x + 1], speed(0, x + 1)), flux)
    plane(nx - 1, flux, pxh[...], hxh[NEAR_EARLY].astype(F32))
    fxl[0] = out[0].astype(BF16)
    fxh[0] = out[nx - 1].astype(BF16)
    fyl[0] = s_fl[...].astype(BF16)
    fyh[0] = s_fh[...].astype(BF16)


def speeds_spec(velocity, instant):
    block = (1,) + velocity.shape[1:]
    return pl.BlockSpec(block, lambda *_: (instant,) + (0,) * (len(block) - 1))


def halo_specs(field, halo):
    nx, ny, nz = field.shape
    planes = halo[2].shape[0] - 8
    return [whole(halo[0].shape)] * 2 + [pl.BlockSpec((8, ny, nz), lambda *_: (planes // 8, 0, 0))] * 2


def halo_scratch(field):
    nx, ny, nz = field.shape
    return [pltpu.VMEM((8 * ny, nz), F32)] + [pltpu.VMEM((7, nx + 2, nz), F32)] * 2


def upwind_one(inside, field, velocity, halo):
    nx, ny, nz = field.shape
    line = struct((ny, nz), F32)
    in_specs = [pl.BlockSpec(memory_space=pltpu.SMEM), whole(field.shape), speeds_spec(velocity, 1)]
    in_specs += halo_specs(field, halo)
    scratch = halo_scratch(field) + [pltpu.VMEM((nx, nz), F32)] * 4
    outs = [struct(field.shape, F32)] + [line] * 4
    return call(upwind_one_kernel, outs, scratch, "upwind_one", in_specs)(inside, field, velocity, *halo)


def upwind_zero(field, velocity, field_halo, halo):
    nx, ny, nz = field.shape
    in_specs = [whole(field.shape), speeds_spec(velocity, 0)]
    in_specs += [whole(h.shape) for h in field_halo] + halo_specs(field, halo)
    scratch = halo_scratch(field) + [pltpu.VMEM((nx, nz), F32)] * 2
    outs = [struct(field.shape, F32)] + [struct((1, ny, nz), BF16)] * 4
    return call(upwind_zero_kernel, outs, scratch, "upwind_zero", in_specs)(
        field, velocity, *field_halo, *halo
    )


def choice_kernel(edge, blocks, left, right, own, send, keep):
    _, height, width = keep.shape
    slots = width // edge
    lane = lax.broadcasted_iota(jnp.int32, (slots, width), 1)
    slot = lax.broadcasted_iota(jnp.int32, (slots, width), 0)
    spread = jnp.where(lane // edge == slot, 1.0, 0.0).astype(BF16)
    row = lax.broadcasted_iota(jnp.int32, (height, width), 0)
    within = lax.broadcasted_iota(jnp.int32, (8, width), 1) % edge
    for code, side, out, d in ((left, 2, send, 0), (right, 0, send, 1), (own, 1, keep, 0)):
        codes = jnp.broadcast_to(code[...], (8, slots)).astype(BF16)
        code = jnp.dot(codes, spread, preferred_element_type=F32).astype(jnp.int32)
        start = (code - side * blocks) * edge
        good = (start >= 0) & (start < height)
        wanted = jnp.where(good, start + within, -1)[0:1]
        out[d] = jnp.where(row == wanted, 1.0, 0.0).astype(BF16)


def choices(left, right, own, edge, nz):
    slots = own.shape[1]
    width = slots * edge
    outs = [struct((count, 3 * nz, width), BF16) for count in (2, 1)]
    kernel = functools.partial(choice_kernel, edge, 3 * nz // edge)
    in_specs = [whole(own.shape)] * 3
    return call(kernel, outs, [], "choices", in_specs)(left, right, own)


def planes_of(ref, planes):
    ny, width = ref.shape[1:]
    parts = [ref[a:b].reshape((b - a) * ny, width) for a, b in planes]
    return parts[0] if len(parts) == 1 else jnp.concatenate(parts, axis=0)


def pick_kernel(planes, t_lo, t_own, t_hi, q_ref, *rest):
    ny, nz = t_own.shape[1:]
    nx = t_own.shape[0]
    rows = jnp.concatenate([planes_of(ref, planes) for ref in (t_lo, t_own, t_hi)], axis=1)
    count = rows.shape[0] // ny
    outs = rest[-q_ref.shape[0] :]
    lines, halos = rest[:2], rest[2:4]
    if len(rest) == len(outs):
        lines = ()
    for d, out in enumerate(outs):
        got = jnp.dot(rows, q_ref[d], preferred_element_type=F32).astype(BF16)
        out[0:count] = got[:, :nz].reshape(count, ny, nz)
        out[count : 2 * count] = got[:, nz:].reshape(count, ny, nz)
    for d, ref in enumerate(lines):
        row = 0 if d == 0 else ny - 1
        for halo, x in ((halos[0], 0), (halos[1], nx + 1)):
            for layer, source in ((NEAR_P, NEAR_P), (NEAR_N, NEAR_T), (NEAR_T, NEAR_N)):
                at = layer * (nx + 2) + x
                ref[at : at + 1, :] = halo[source].astype(F32)[row : row + 1]
        outs[d][2 * count :] = ref[...].astype(BF16).reshape(-1, ny, nz)


def pick(columns, choices, planes, name, lines=()):
    _, ny, nz = columns[1].shape
    count = 2 * sum(b - a for a, b in planes)
    extra = lines[0].shape[0] // ny if lines else 0
    outs = [struct((count + extra, ny, nz), BF16)] * choices.shape[0]
    ins = (*columns, choices, *lines)
    in_specs = [whole(a.shape) for a in ins]
    return call(functools.partial(pick_kernel, planes), outs, [], name, in_specs)(*ins)


def outer_kernel(nx, count, own, la, ra, low, high):
    for k in range(2):
        for c in range(2):
            x, a = k * nx + c, k * count + c
            low[2 * k + c] = own[x] + la[a] + ra[a]
            x, a = (k + 1) * nx - 2 + c, (k + 1) * count - 2 + c
            high[2 * k + c] = own[x] + la[a] + ra[a]


def each_plane(groups, images, k, visit):
    own, la, ra, lb, rb = images
    nx = sum(b - a for planes in groups for a, b in planes)
    for planes, lefts, rights in ((groups[0], la, ra), (groups[1], lb, rb)):
        at = k * sum(b - a for a, b in planes)
        for a, b in planes:

            def step(x, carry, shift=at - a, lefts=lefts, rights=rights):
                visit(x, own[k * nx + x] + lefts[x + shift] + rights[x + shift])
                return carry

            lax.fori_loop(a, b, step, 0)
            at += b - a


def edge_kernel(
    groups, own, la, ra, lb, rb, xlo, xhi, face_lo, face_hi, first, final, s_first, s_final
):
    nx, (ny, nz) = own.shape[0] // 2, own.shape[1:]
    for k in range(2):

        def put(x, cells, k=k):
            at = pl.ds(x + 1, 1)
            cells = cells.astype(F32)
            for c in range(2):
                s_first[2 * k + c, at, :] = cells[c : c + 1]
                s_final[2 * k + c, at, :] = cells[ny - 2 + c : ny - 1 + c]

        put(-1, xlo[2 * k + 1])
        put(nx, xhi[2 * k])
        each_plane(groups, (own, la, ra, lb, rb), k, put)
    for faces, scr, msg in ((face_lo, s_first, first), (face_hi, s_final, final)):
        msg[0:4] = scr[...].astype(BF16)
        msg[4] = jnp.zeros(msg.shape[1:], BF16)
        msg[4, 0:nx] = faces[0]


def force_kernel(
    groups, own, la, ra, lb, rb, band, xlo, xhi, zxl, zxh, ylo, yhi, adj0, adj1, bxl, bxh, byl, byh, vel,
    out, img, packed, frc, s_ylo, s_yhi, s_c0, s_c1, s_fl, s_fh, s_al, s_ah,
):
    k = pl.program_id(0)
    nx, ny, nz = adj0.shape
    rows = lax.broadcasted_iota(jnp.int32, (ny, nz), 0)
    lanes = lax.broadcasted_iota(jnp.int32, (ny, nz), 1)
    first_image = k == 0

    def this(zero, one):
        return jnp.where(first_image, zero.astype(F32), one.astype(F32))

    for h in range(2):
        img[h] = xlo[2 * k + h].astype(F32)
        img[nx + 2 + h] = xhi[2 * k + h].astype(F32)

    def fill(x, cells):
        packed[x] = cells
        cells = cells.astype(F32)
        img[x + 2] = cells
        s_c0[pl.ds(x, 1), :] = cells[0:1]
        s_c1[pl.ds(x, 1), :] = cells[ny - 1 : ny]

    each_plane(groups, (own, la, ra, lb, rb), 0, fill)
    every = packed[...].reshape(nx * ny, nz)
    frc[2, 1 : nx + 1] = jnp.dot(every, band[...], preferred_element_type=F32).reshape(nx, ny, nz)
    for h in range(2):
        s_ylo[h] = ylo[2 * k + h].astype(F32)
        s_yhi[h] = yhi[2 * k + h].astype(F32)
    s_al[...] = this(ylo[4, 0:nx], byl[...])
    s_ah[...] = this(yhi[4, 0:nx], byh[...])

    def along_z(cells, index, length):
        following = jnp.where(index == length - 1, 0.0, pltpu.roll(cells, length - 1, 1))
        before = jnp.where(index == 0, 0.0, pltpu.roll(cells, 1, 1))
        return following, before

    def forces(x, half, slope_z):
        cells = img[x + 2]
        at = pl.ds(x + 1, 1)
        frc[0, x + 1] = half * (img[x + 3] - img[x + 1])
        up = jnp.where(rows == ny - 1, s_yhi[0, at, :], pltpu.roll(cells, ny - 1, 0))
        down = jnp.where(rows == 0, s_ylo[1, at, :], pltpu.roll(cells, 1, 0))
        frc[1, x + 1] = half * (up - down)
        frc[2, x + 1] = half * slope_z

    for x, half in ((-1, 0.5 * this(zxl[0], bxl[...])), (nx, 0.5 * this(zxh[0], bxh[...]))):
        following, before = along_z(img[x + 2], lanes, nz)
        forces(x, half, following - before)

    def force_step(x, carry):
        forces(x, 0.5 * this(adj0[x], adj1[x]), frc[2, x + 1])
        return carry

    lax.fori_loop(0, nx, force_step, 0)
    lines = lax.broadcasted_iota(jnp.int32, (nx, nz), 1)
    for cols, near, far, beside, half, dest, sign in (
        (s_ylo, 1, 0, s_c0, s_al, s_fl, 1.0),
        (s_yhi, 0, 1, s_c1, s_ah, s_fh, -1.0),
    ):
        weight = 0.5 * half[...]
        dest[0] = weight * (cols[near, 2 : nx + 2, :] - cols[near, 0:nx, :])
        dest[1] = (sign * weight) * (beside[...] - cols[far, 1 : nx + 1, :])
        following, before = along_z(cols[near, 1 : nx + 1, :], lines, nz)
        dest[2] = weight * (following - before)

    def smooth_step(x, carry):
        at = pl.ds(x, 1)
        for c in range(3):
            f = frc[c, x + 1]
            up = jnp.where(rows == ny - 1, s_fh[c, at, :], pltpu.roll(f, ny - 1, 0))
            down = jnp.where(rows == 0, s_fl[c, at, :], pltpu.roll(f, 1, 0))
            following, before = along_z(f, lanes, nz)
            beside = (frc[c, x] + frc[c, x + 2]) + (up + down) + (following + before)
            out[0, c, x] = vel[0, c, x].astype(F32) + (0.25 * f + 0.125 * beside)
        return carry

    lax.fori_loop(0, nx, smooth_step, 0)


def force(groups, images, band, x_lo, x_hi, face_lo, face_hi, y_lo, y_hi, adj_zero, adj_one, halo_one, velocity):
    nx, ny, nz = adj_zero.shape
    block = pl.BlockSpec((1, 3, nx, ny, nz), lambda k: (k, 0, 0, 0, 0))
    middle = [band, x_lo, x_hi, face_lo, face_hi, y_lo, y_hi, adj_zero, adj_one, *halo_one]
    counts = [nx] + [sum(b - a for a, b in planes) for planes in groups for _ in range(2)]
    in_specs = [pl.BlockSpec((count, ny, nz), lambda k: (k, 0, 0)) for count in counts]
    in_specs += [whole(a.shape) for a in middle] + [block]
    scratch = [
        pltpu.VMEM((nx + 4, ny, nz), F32),
        pltpu.VMEM((nx, ny, nz), BF16),
        pltpu.VMEM((3, nx + 2, ny, nz), F32),
        pltpu.VMEM((2, nx + 2, nz), F32),
        pltpu.VMEM((2, nx + 2, nz), F32),
        pltpu.VMEM((nx, nz), F32),
        pltpu.VMEM((nx, nz), F32),
        pltpu.VMEM((3, nx, nz), F32),
        pltpu.VMEM((3, nx, nz), F32),
        pltpu.VMEM((nx, nz), F32),
        pltpu.VMEM((nx, nz), F32),
    ]
    return call(
        functools.partial(force_kernel, groups),
        struct((2, 3, nx, ny, nz), F32),
        scratch,
        "force",
        in_specs,
        block,
        2,
    )(*images, *middle, velocity)


def forward(value, axis):
    ends = lax.axis_size(axis) - 1
    return lax.ppermute(value, axis, [(i, i + 1) for i in range(ends)])


def backward(value, axis):
    ends = lax.axis_size(axis) - 1
    return lax.ppermute(value, axis, [(i + 1, i) for i in range(ends)])


def body(template, mismatch, velocity, src_ids):
    nx, ny, nz = template.shape
    depth_blocks = src_ids.shape[3]
    edge = nz // depth_blocks
    slots = 2 * depth_blocks
    index_first = lax.axis_index("gx")
    index_second = lax.axis_index("gy")
    count_first = lax.axis_size("gx")
    count_second = lax.axis_size("gy")

    t_lo = forward(template, "gx")
    t_hi = backward(template, "gx")
    low, high = column_messages(mismatch, velocity)
    halo_xl = forward(high, "gx")
    halo_xh = backward(low, "gx")

    ids = src_ids.reshape(slots)
    first_block = ids // (count_second * depth_blocks)
    second_block = ids // depth_blocks % count_second
    start = (first_block - index_first + 1) * depth_blocks + ids % depth_blocks
    side = second_block - index_second + 1
    code = (side * (3 * depth_blocks) + start).astype(BF16).reshape(1, slots)
    left_code = forward(code, "gy")
    right_code = backward(code, "gy")
    lines = call(
        rows_kernel,
        [struct((8 * ny, nz), F32)] * 2,
        [],
        "rows",
        [whole(a.shape) for a in (mismatch, velocity)],
    )(mismatch, velocity)

    send_choice, own_choice = choices(left_code, right_code, code, edge, nz)
    z = jnp.arange(nz)
    band = (z[:, None] == z[None] + 1).astype(BF16) - (z[:, None] == z[None] - 1).astype(BF16)

    columns = (t_lo, template, t_hi)
    margin = nx // 4
    groups = (((0, margin), (nx - margin, nx)), ((margin, nx - margin),))
    to_left_a, to_right_a = pick(columns, send_choice, groups[0], "pick_outer", (*lines, halo_xl, halo_xh))
    columns, _ = lax.optimization_barrier((columns, to_left_a))
    to_left_b, to_right_b = pick(columns, send_choice, groups[1], "pick_inner")
    from_left_b = forward(to_right_b, "gy")
    from_right_b = backward(to_left_b, "gy")
    from_left_a = forward(to_right_a, "gy")
    from_right_a = backward(to_left_a, "gy")

    late_mismatch, late_choice, _ = lax.optimization_barrier((mismatch, own_choice, to_left_b))
    (own,) = pick(columns, late_choice, ((0, nx),), "pick_own")
    inside = jnp.stack(
        [index_first > 0, index_first < count_first - 1, index_second > 0, index_second < count_second - 1]
    ).astype(F32)
    halo = (halo_xl, halo_xh, from_left_a, from_right_a)
    adj_one, *halo_one = upwind_one(inside, late_mismatch, velocity, halo)
    adj_zero, low_x, high_x, low_y, high_y = upwind_zero(adj_one, velocity, halo_one, halo)

    ins = (own, from_left_a, from_right_a)
    low, high = call(
        functools.partial(outer_kernel, nx, 2 * margin),
        [struct((4, ny, nz), BF16)] * 2, [], "outer", [whole(a.shape) for a in ins]
    )(*ins)
    x_lo = forward(high, "gx")
    x_hi = backward(low, "gx")
    face_lo = forward(high_x, "gx")
    face_hi = backward(low_x, "gx")

    images = (own, from_left_a, from_right_a, from_left_b, from_right_b)
    ins = (*images, x_lo, x_hi, low_y, high_y)
    first, final = call(
        functools.partial(edge_kernel, groups),
        [struct((5, nx + 2, nz), BF16)] * 2,
        [pltpu.VMEM((4, nx + 2, nz), F32)] * 2,
        "edges",
        [whole(a.shape) for a in ins],
    )(*ins)
    y_lo = forward(final, "gy")
    y_hi = backward(first, "gy")
    return force(
        groups, images, band, x_lo, x_hi, face_lo, face_hi, y_lo, y_hi, adj_zero, adj_one, halo_one, velocity
    )


def solution(mesh):
    in_specs = (
        P("gx", "gy", None),
        P("gx", "gy", None),
        P(None, None, "gx", "gy", None),
        P(None, "gx", "gy", None),
    )
    out_specs = P(None, None, "gx", "gy", None)
    return jax.shard_map(body, mesh=mesh, in_specs=in_specs, out_specs=out_specs, check_vma=False)
```

```python
import functools

import jax
import jax.numpy as jnp
from jax import lax
from jax.experimental import pallas as pl
from jax.experimental.pallas import tpu as pltpu
from jax.sharding import PartitionSpec as P

F32 = jnp.float32
BF16 = jnp.bfloat16
VMEM_LIMIT = 48 << 20


def whole(shape):
    return pl.BlockSpec(shape, lambda *_: (0,) * len(shape))


def call(kernel, outs, scratch, name, in_specs, out_specs=None, steps=1):
    return pl.pallas_call(
        kernel,
        name=name,
        grid=(steps,),
        in_specs=in_specs,
        out_specs=out_specs or [whole(o.shape) for o in outs],
        out_shape=outs,
        scratch_shapes=scratch,
        cost_estimate=pl.CostEstimate(flops=0, transcendentals=0, bytes_accessed=0),
        compiler_params=pltpu.CompilerParams(vmem_limit_bytes=VMEM_LIMIT),
    )


def struct(shape, dtype):
    return jax.ShapeDtypeStruct(shape, dtype)


def face_flux(here, following, speed_here, speed_following):
    total = speed_here + speed_following
    return jnp.minimum(total, 0.0) * here + jnp.maximum(total, 0.0) * following


def depth_change(p, vz):
    nz = p.shape[1]
    lanes = lax.broadcasted_iota(jnp.int32, p.shape, 1)
    p_up = jnp.where(lanes == nz - 1, 0.0, pltpu.roll(p, nz - 1, 1))
    v_up = jnp.where(lanes == nz - 1, 0.0, pltpu.roll(vz, nz - 1, 1))
    upper = face_flux(p, p_up, vz, v_up)
    lower = jnp.where(lanes == 0, jnp.maximum(vz, 0.0) * p, pltpu.roll(upper, 1, 1))
    return upper - lower


def plane_change(p, vy, vz, below, above):
    ny = p.shape[0]
    rows = lax.broadcasted_iota(jnp.int32, p.shape, 0)
    p_up = jnp.where(rows == ny - 1, above[0], pltpu.roll(p, ny - 1, 0))
    v_up = jnp.where(rows == ny - 1, above[1], pltpu.roll(vy, ny - 1, 0))
    upper = face_flux(p, p_up, vy, v_up)
    first = face_flux(below[0], p[0:1], below[1], vy[0:1])
    lower = jnp.where(rows == 0, first, pltpu.roll(upper, 1, 0))
    return (upper - lower) + depth_change(p, vz)


NEAR_P, FAR_P, NEAR_N, FAR_N, NEAR_T, NEAR_Z, NEAR_EARLY = range(7)


def column_kernel(p_any, v_any, low, high, p_lo, p_hi, v_lo, v_hi, sem):
    nx = p_any.shape[0]
    copies = []
    for at, (p, v, x) in enumerate(((p_lo, v_lo, 0), (p_hi, v_hi, nx - 2))):
        copies.append(pltpu.make_async_copy(p_any.at[pl.ds(x, 2)], p, sem.at[2 * at]))
        copies.append(pltpu.make_async_copy(v_any.at[:, :, pl.ds(x, 2)], v, sem.at[2 * at + 1]))
    for copy in copies:
        copy.start()
    for copy in copies:
        copy.wait()
    for msg, p, v, near, far in ((low, p_lo, v_lo, 0, 1), (high, p_hi, v_hi, 1, 0)):
        msg[NEAR_P] = p[near].astype(BF16)
        msg[FAR_P] = p[far].astype(BF16)
        msg[NEAR_N] = v[1, 0, near]
        msg[FAR_N] = v[1, 0, far]
        msg[NEAR_T] = v[1, 1, near]
        msg[NEAR_Z] = v[1, 2, near]
        msg[NEAR_EARLY] = v[0, 0, near]


def column_messages(field, velocity):
    nx, ny, nz = field.shape
    outs = [struct((7, ny, nz), BF16)] * 2
    scratch = [pltpu.VMEM((2, ny, nz), F32)] * 2
    scratch += [pltpu.VMEM((2, 3, 2, ny, nz), BF16)] * 2 + [pltpu.SemaphoreType.DMA((4,))]
    in_specs = [pl.BlockSpec(memory_space=pltpu.HBM)] * 2
    return call(column_kernel, outs, scratch, "columns", in_specs)(field, velocity)


def rows_kernel(p_ref, v_ref, hxl, hxh, code, lo, hi, s_lo, s_hi):
    nx, ny, _ = p_ref.shape
    s_lo[...] = jnp.zeros(s_lo.shape, F32)
    s_hi[...] = jnp.zeros(s_hi.shape, F32)

    def put(layer, x, cells, width):
        at = pl.ds(x + 1, 1)
        for d in range(width):
            s_lo[layer + d, at, :] = cells[d : d + 1]
            s_hi[layer + d, at, :] = cells[ny - 1 - d : ny - d]

    def step(x, carry):
        put(NEAR_P, x, p_ref[x], 2)
        put(NEAR_N, x, v_ref[1, 1, x].astype(F32), 2)
        put(NEAR_T, x, v_ref[1, 0, x].astype(F32), 1)
        put(NEAR_Z, x, v_ref[1, 2, x].astype(F32), 1)
        put(NEAR_EARLY, x, v_ref[0, 1, x].astype(F32), 1)
        return carry

    lax.fori_loop(0, nx, step, 0)
    for x, halo in ((-1, hxl), (nx, hxh)):
        put(NEAR_P, x, halo[NEAR_P].astype(F32), 1)
        put(NEAR_N, x, halo[NEAR_T].astype(F32), 1)
        put(NEAR_T, x, halo[NEAR_N].astype(F32), 1)
    s_lo[FAR_P, 0:1, :] = code[...]
    s_hi[FAR_P, 0:1, :] = code[...]
    lo[...] = s_lo[...].astype(BF16)
    hi[...] = s_hi[...].astype(BF16)


def upwind_one_kernel(
    inside, p_ref, v_ref, hxl, hxh, hyl, hyh, out, oxl, oxh, oyl, oyh,
    s_yl, s_yh, s_p0, s_p1, s_v0, s_v1,
):
    nx, ny, nz = p_ref.shape
    s_yl[...] = hyl[...].astype(F32)
    s_yh[...] = hyh[...].astype(F32)

    def plane(x, flux_below, p, speeds, p_next, vx_next):
        vx, vy, vz = speeds
        flux_above = face_flux(p, p_next, vx, vx_next)
        at = pl.ds(x + 1, 1)
        below = s_yl[NEAR_P, at, :], s_yl[NEAR_N, at, :]
        above = s_yh[NEAR_P, at, :], s_yh[NEAR_N, at, :]
        change = (flux_above - flux_below) + plane_change(p, vy, vz, below, above)
        return p + 0.5 * change, flux_above

    def speed(c, x):
        return v_ref[0, c, x].astype(F32)

    def halo_plane(halo):
        return [halo[i].astype(F32) for i in (NEAR_P, FAR_P, NEAR_N, FAR_N, NEAR_T, NEAR_Z)]

    p, p_far, vx, vx_far, vy, vz = halo_plane(hxl)
    flux = face_flux(p_far, p, vx_far, vx)
    got, flux = plane(-1, flux, p, (vx, vy, vz), p_ref[0], speed(0, 0))
    oxl[...] = got * inside[0]
    p_high, p_far, vx_high, vx_far, vy_high, vz_high = halo_plane(hxh)

    def inner(x, flux, p_next, vx_next):
        p = p_ref[x]
        vy = speed(1, x)
        got, flux = plane(x, flux, p, (speed(0, x), vy, speed(2, x)), p_next, vx_next)
        out[x] = got
        at = pl.ds(x, 1)
        s_p0[at, :] = p[0:1]
        s_p1[at, :] = p[ny - 1 : ny]
        s_v0[at, :] = vy[0:1]
        s_v1[at, :] = vy[ny - 1 : ny]
        return flux

    flux = lax.fori_loop(0, nx - 1, lambda x, f: inner(x, f, p_ref[x + 1], speed(0, x + 1)), flux)
    flux = inner(nx - 1, flux, p_high, vx_high)
    got, _ = plane(nx, flux, p_high, (vx_high, vy_high, vz_high), p_far, vx_far)
    oxh[...] = got * inside[1]

    for scr, edge_p, edge_v, dest, flag, sign in (
        (s_yl, s_p0, s_v0, oyl, inside[2], 1.0),
        (s_yh, s_p1, s_v1, oyh, inside[3], -1.0),
    ):
        mid = slice(1, nx + 1)
        p, vy = scr[NEAR_P, mid, :], scr[NEAR_N, mid, :]
        flux_x = face_flux(
            scr[NEAR_P, 0 : nx + 1, :], scr[NEAR_P, 1 : nx + 2, :],
            scr[NEAR_T, 0 : nx + 1, :], scr[NEAR_T, 1 : nx + 2, :],
        )
        change = flux_x[1:] - flux_x[:-1]
        far = (scr[FAR_P, mid, :], scr[FAR_N, mid, :])
        near = (edge_p[...], edge_v[...])
        before, following = (far, near) if sign > 0 else (near, far)
        change = change + (
            face_flux(p, following[0], vy, following[1]) - face_flux(before[0], p, before[1], vy)
        )
        change = change + depth_change(p, scr[NEAR_Z, mid, :])
        dest[...] = (p + 0.5 * change) * flag


def upwind_zero_kernel(
    p_ref, v_ref, pxl, pxh, pyl, pyh, hxl, hxh, hyl, hyh, out, fxl, fxh, fyl, fyh,
    s_vl, s_vh, s_fl, s_fh,
):
    nx, ny, nz = p_ref.shape
    s_vl[...] = hyl[NEAR_EARLY].astype(F32)
    s_vh[...] = hyh[NEAR_EARLY].astype(F32)

    def speed(c, x):
        return v_ref[0, c, x].astype(F32)

    def plane(x, flux_below, p_next, vx_next):
        p = p_ref[x]
        flux_above = face_flux(p, p_next, speed(0, x), vx_next)
        at, halo_at = pl.ds(x, 1), pl.ds(x + 1, 1)
        below = pyl[at, :], s_vl[halo_at, :]
        above = pyh[at, :], s_vh[halo_at, :]
        change = (flux_above - flux_below) + plane_change(p, speed(1, x), speed(2, x), below, above)
        got = p + 0.5 * change
        out[x] = got
        s_fl[at, :] = got[0:1]
        s_fh[at, :] = got[ny - 1 : ny]
        return flux_above

    flux = face_flux(pxl[...], p_ref[0], hxl[NEAR_EARLY].astype(F32), speed(0, 0))
    flux = lax.fori_loop(0, nx - 1, lambda x, f: plane(x, f, p_ref[x + 1], speed(0, x + 1)), flux)
    plane(nx - 1, flux, pxh[...], hxh[NEAR_EARLY].astype(F32))
    fxl[0] = out[0].astype(BF16)
    fxh[0] = out[nx - 1].astype(BF16)
    fyl[0] = s_fl[...].astype(BF16)
    fyh[0] = s_fh[...].astype(BF16)


def speeds_spec(velocity, instant):
    block = (1,) + velocity.shape[1:]
    return pl.BlockSpec(block, lambda *_: (instant,) + (0,) * (len(block) - 1))


def upwind_one(inside, field, velocity, halo):
    nx, ny, nz = field.shape
    line = struct((ny, nz), F32)
    in_specs = [pl.BlockSpec(memory_space=pltpu.SMEM), whole(field.shape), speeds_spec(velocity, 1)]
    in_specs += [whole(h.shape) for h in halo]
    scratch = [pltpu.VMEM(halo[2].shape, F32)] * 2 + [pltpu.VMEM((nx, nz), F32)] * 4
    outs = [struct(field.shape, F32)] + [line] * 4
    return call(upwind_one_kernel, outs, scratch, "upwind_one", in_specs)(inside, field, velocity, *halo)


def upwind_zero(field, velocity, field_halo, halo):
    nx, ny, nz = field.shape
    in_specs = [whole(field.shape), speeds_spec(velocity, 0)]
    in_specs += [whole(h.shape) for h in (*field_halo, *halo)]
    scratch = [pltpu.VMEM((nx + 2, nz), F32)] * 2 + [pltpu.VMEM((nx, nz), F32)] * 2
    outs = [struct(field.shape, F32)] + [struct((1, ny, nz), BF16)] * 4
    return call(upwind_zero_kernel, outs, scratch, "upwind_zero", in_specs)(
        field, velocity, *field_halo, *halo
    )


def choice_kernel(edge, blocks, left, right, own, send, keep):
    _, height, width = keep.shape
    nz = own.shape[1]
    lane = lax.broadcasted_iota(jnp.int32, (nz, width), 1)
    slot = lax.broadcasted_iota(jnp.int32, (nz, width), 0)
    spread = jnp.where(lane // edge == slot, 1.0, 0.0).astype(BF16)
    row = lax.broadcasted_iota(jnp.int32, (height, width), 0)
    within = lax.broadcasted_iota(jnp.int32, (8, width), 1) % edge
    codes = (left[FAR_P, 0:1, :].astype(F32), right[FAR_P, 0:1, :].astype(F32), own[...])
    for code, side, out, d in zip(codes, (2, 0, 1), (send, send, keep), (0, 1, 0)):
        code = jnp.broadcast_to(code, (8, nz)).astype(BF16)
        code = jnp.dot(code, spread, preferred_element_type=F32).astype(jnp.int32)
        start = (code - side * blocks) * edge
        good = (start >= 0) & (start < height)
        wanted = jnp.where(good, start + within, -1)[0:1]
        out[d] = jnp.where(row == wanted, 1.0, 0.0).astype(BF16)


def choices(left, right, own, edge, slots):
    nz = own.shape[1]
    outs = [struct((count, 3 * nz, slots * edge), BF16) for count in (2, 1)]
    kernel = functools.partial(choice_kernel, edge, 3 * nz // edge)
    in_specs = [whole(a.shape) for a in (left, right, own)]
    return call(kernel, outs, [], "choices", in_specs)(left, right, own)


def planes_of(ref, planes):
    ny, width = ref.shape[1:]
    parts = [ref[a:b].reshape((b - a) * ny, width) for a, b in planes]
    return parts[0] if len(parts) == 1 else jnp.concatenate(parts, axis=0)


def pick_kernel(planes, t_lo, t_own, t_hi, q_ref, *outs):
    ny, nz = t_own.shape[1:]
    rows = jnp.concatenate([planes_of(ref, planes) for ref in (t_lo, t_own, t_hi)], axis=1)
    count = rows.shape[0] // ny
    for d, out in enumerate(outs):
        got = jnp.dot(rows, q_ref[d], preferred_element_type=F32).astype(BF16)
        out[0:count] = got[:, :nz].reshape(count, ny, nz)
        out[count : 2 * count] = got[:, nz:].reshape(count, ny, nz)


def pick(columns, choices, planes, name):
    _, ny, nz = columns[1].shape
    count = 2 * sum(b - a for a, b in planes)
    outs = [struct((count, ny, nz), BF16)] * choices.shape[0]
    ins = (*columns, choices)
    in_specs = [whole(a.shape) for a in ins]
    return call(functools.partial(pick_kernel, planes), outs, [], name, in_specs)(*ins)


def outer_kernel(nx, count, own, la, ra, face_lo, face_hi, low, high):
    for k in range(2):
        for c in range(2):
            x, a = k * nx + c, k * count + c
            low[2 * k + c] = own[x] + la[a] + ra[a]
            x, a = (k + 1) * nx - 2 + c, (k + 1) * count - 2 + c
            high[2 * k + c] = own[x] + la[a] + ra[a]
    low[4] = face_lo[0]
    high[4] = face_hi[0]


def each_plane(groups, images, k, visit):
    own, la, ra, lb, rb = images
    nx = sum(b - a for planes in groups for a, b in planes)
    for planes, lefts, rights in ((groups[0], la, ra), (groups[1], lb, rb)):
        at = k * sum(b - a for a, b in planes)
        for a, b in planes:

            def step(x, carry, shift=at - a, lefts=lefts, rights=rights):
                visit(x, own[k * nx + x] + lefts[x + shift] + rights[x + shift])
                return carry

            lax.fori_loop(a, b, step, 0)
            at += b - a


def edge_kernel(
    groups, own, la, ra, lb, rb, xlo, xhi, face_lo, face_hi, first, final, s_first, s_final
):
    nx, (ny, nz) = own.shape[0] // 2, own.shape[1:]
    for k in range(2):

        def put(x, cells, k=k):
            at = pl.ds(x + 1, 1)
            cells = cells.astype(F32)
            for c in range(2):
                s_first[2 * k + c, at, :] = cells[c : c + 1]
                s_final[2 * k + c, at, :] = cells[ny - 2 + c : ny - 1 + c]

        put(-1, xlo[2 * k + 1])
        put(nx, xhi[2 * k])
        each_plane(groups, (own, la, ra, lb, rb), k, put)
    for faces, scr, msg in ((face_lo, s_first, first), (face_hi, s_final, final)):
        msg[0:4] = scr[...].astype(BF16)
        msg[4] = jnp.zeros(msg.shape[1:], BF16)
        msg[4, 0:nx] = faces[0]


def force_kernel(
    groups, own, la, ra, lb, rb, band, xlo, xhi, ylo, yhi, adj0, adj1, bxl, bxh, byl, byh, vel,
    out, img, packed, frc, s_ylo, s_yhi, s_c0, s_c1, s_fl, s_fh, s_al, s_ah,
):
    k = pl.program_id(0)
    nx, ny, nz = adj0.shape
    rows = lax.broadcasted_iota(jnp.int32, (ny, nz), 0)
    lanes = lax.broadcasted_iota(jnp.int32, (ny, nz), 1)
    first_image = k == 0

    def this(zero, one):
        return jnp.where(first_image, zero.astype(F32), one.astype(F32))

    for h in range(2):
        img[h] = xlo[2 * k + h].astype(F32)
        img[nx + 2 + h] = xhi[2 * k + h].astype(F32)

    def fill(x, cells):
        packed[x] = cells
        cells = cells.astype(F32)
        img[x + 2] = cells
        s_c0[pl.ds(x, 1), :] = cells[0:1]
        s_c1[pl.ds(x, 1), :] = cells[ny - 1 : ny]

    each_plane(groups, (own, la, ra, lb, rb), 0, fill)
    every = packed[...].reshape(nx * ny, nz)
    frc[2, 1 : nx + 1] = jnp.dot(every, band[...], preferred_element_type=F32).reshape(nx, ny, nz)
    for h in range(2):
        s_ylo[h] = ylo[2 * k + h].astype(F32)
        s_yhi[h] = yhi[2 * k + h].astype(F32)
    s_al[...] = this(ylo[4, 0:nx], byl[...])
    s_ah[...] = this(yhi[4, 0:nx], byh[...])

    def along_z(cells, index, length):
        following = jnp.where(index == length - 1, 0.0, pltpu.roll(cells, length - 1, 1))
        before = jnp.where(index == 0, 0.0, pltpu.roll(cells, 1, 1))
        return following, before

    def forces(x, half, slope_z):
        cells = img[x + 2]
        at = pl.ds(x + 1, 1)
        frc[0, x + 1] = half * (img[x + 3] - img[x + 1])
        up = jnp.where(rows == ny - 1, s_yhi[0, at, :], pltpu.roll(cells, ny - 1, 0))
        down = jnp.where(rows == 0, s_ylo[1, at, :], pltpu.roll(cells, 1, 0))
        frc[1, x + 1] = half * (up - down)
        frc[2, x + 1] = half * slope_z

    for x, half in ((-1, 0.5 * this(xlo[4], bxl[...])), (nx, 0.5 * this(xhi[4], bxh[...]))):
        following, before = along_z(img[x + 2], lanes, nz)
        forces(x, half, following - before)

    def force_step(x, carry):
        forces(x, 0.5 * this(adj0[x], adj1[x]), frc[2, x + 1])
        return carry

    lax.fori_loop(0, nx, force_step, 0)
    lines = lax.broadcasted_iota(jnp.int32, (nx, nz), 1)
    for cols, near, far, beside, half, dest, sign in (
        (s_ylo, 1, 0, s_c0, s_al, s_fl, 1.0),
        (s_yhi, 0, 1, s_c1, s_ah, s_fh, -1.0),
    ):
        weight = 0.5 * half[...]
        dest[0] = weight * (cols[near, 2 : nx + 2, :] - cols[near, 0:nx, :])
        dest[1] = (sign * weight) * (beside[...] - cols[far, 1 : nx + 1, :])
        following, before = along_z(cols[near, 1 : nx + 1, :], lines, nz)
        dest[2] = weight * (following - before)

    def smooth_step(x, carry):
        at = pl.ds(x, 1)
        for c in range(3):
            f = frc[c, x + 1]
            up = jnp.where(rows == ny - 1, s_fh[c, at, :], pltpu.roll(f, ny - 1, 0))
            down = jnp.where(rows == 0, s_fl[c, at, :], pltpu.roll(f, 1, 0))
            following, before = along_z(f, lanes, nz)
            beside = (frc[c, x] + frc[c, x + 2]) + (up + down) + (following + before)
            out[0, c, x] = vel[0, c, x].astype(F32) + (0.25 * f + 0.125 * beside)
        return carry

    lax.fori_loop(0, nx, smooth_step, 0)


def force(groups, images, band, x_lo, x_hi, y_lo, y_hi, adj_zero, adj_one, halo_one, velocity):
    nx, ny, nz = adj_zero.shape
    block = pl.BlockSpec((1, 3, nx, ny, nz), lambda k: (k, 0, 0, 0, 0))
    middle = [band, x_lo, x_hi, y_lo, y_hi, adj_zero, adj_one, *halo_one]
    counts = [nx] + [sum(b - a for a, b in planes) for planes in groups for _ in range(2)]
    in_specs = [pl.BlockSpec((count, ny, nz), lambda k: (k, 0, 0)) for count in counts]
    in_specs += [whole(a.shape) for a in middle] + [block]
    scratch = [
        pltpu.VMEM((nx + 4, ny, nz), F32),
        pltpu.VMEM((nx, ny, nz), BF16),
        pltpu.VMEM((3, nx + 2, ny, nz), F32),
        pltpu.VMEM((2, nx + 2, nz), F32),
        pltpu.VMEM((2, nx + 2, nz), F32),
        pltpu.VMEM((nx, nz), F32),
        pltpu.VMEM((nx, nz), F32),
        pltpu.VMEM((3, nx, nz), F32),
        pltpu.VMEM((3, nx, nz), F32),
        pltpu.VMEM((nx, nz), F32),
        pltpu.VMEM((nx, nz), F32),
    ]
    return call(
        functools.partial(force_kernel, groups),
        struct((2, 3, nx, ny, nz), F32),
        scratch,
        "force",
        in_specs,
        block,
        2,
    )(*images, *middle, velocity)


def forward(value, axis):
    ends = lax.axis_size(axis) - 1
    return lax.ppermute(value, axis, [(i, i + 1) for i in range(ends)])


def backward(value, axis):
    ends = lax.axis_size(axis) - 1
    return lax.ppermute(value, axis, [(i + 1, i) for i in range(ends)])


def body(template, mismatch, velocity, src_ids):
    nx, ny, nz = template.shape
    depth_blocks = src_ids.shape[3]
    edge = nz // depth_blocks
    slots = 2 * depth_blocks
    index_first = lax.axis_index("gx")
    index_second = lax.axis_index("gy")
    count_first = lax.axis_size("gx")
    count_second = lax.axis_size("gy")

    low, high = column_messages(
        pltpu.with_memory_space_constraint(mismatch, pltpu.HBM),
        pltpu.with_memory_space_constraint(velocity, pltpu.HBM),
    )
    halo_xl = forward(high, "gx")
    halo_xh = backward(low, "gx")
    late_template, _ = lax.optimization_barrier((template, low))
    t_lo = forward(late_template, "gx")
    t_hi = backward(late_template, "gx")

    ids = src_ids.reshape(slots)
    first_block = ids // (count_second * depth_blocks)
    second_block = ids // depth_blocks % count_second
    start = (first_block - index_first + 1) * depth_blocks + ids % depth_blocks
    side = second_block - index_second + 1
    code = (side * (3 * depth_blocks) + start).astype(F32)
    code = jnp.pad(code.reshape(1, slots), ((0, 0), (0, nz - slots)))
    ins = (mismatch, velocity, halo_xl, halo_xh, code)
    rows = struct((7, nx + 2, nz), BF16)
    low, high = call(
        rows_kernel,
        [rows] * 2,
        [pltpu.VMEM(rows.shape, F32)] * 2,
        "rows",
        [whole(a.shape) for a in ins],
    )(*ins)
    halo_yl = forward(high, "gy")
    halo_yh = backward(low, "gy")
    halo = (halo_xl, halo_xh, halo_yl, halo_yh)
    inside = jnp.stack(
        [index_first > 0, index_first < count_first - 1, index_second > 0, index_second < count_second - 1]
    ).astype(F32)

    send_choice, own_choice = choices(halo_yl, halo_yh, code, edge, slots)
    z = jnp.arange(nz)
    band = (z[:, None] == z[None] + 1).astype(BF16) - (z[:, None] == z[None] - 1).astype(BF16)

    columns = (t_lo, template, t_hi)
    half = nx // 4
    groups = (((0, half), (nx - half, nx)), ((half, nx - half),))
    to_left_a, to_right_a = pick(columns, send_choice, groups[0], "pick_outer")
    from_left_a = forward(to_right_a, "gy")
    from_right_a = backward(to_left_a, "gy")
    columns, _ = lax.optimization_barrier((columns, to_left_a))
    to_left_b, to_right_b = pick(columns, send_choice, groups[1], "pick_inner")
    from_left_b = forward(to_right_b, "gy")
    from_right_b = backward(to_left_b, "gy")
    late_choice, late_mismatch, _ = lax.optimization_barrier((own_choice, mismatch, to_left_b))
    adj_one, *halo_one = upwind_one(inside, late_mismatch, velocity, halo)
    adj_zero, low_x, high_x, low_y, high_y = upwind_zero(adj_one, velocity, halo_one, halo)
    (own,) = pick(columns, late_choice, ((0, nx),), "pick_own")

    ins = (own, from_left_a, from_right_a, low_x, high_x)
    low, high = call(
        functools.partial(outer_kernel, nx, 2 * half),
        [struct((5, ny, nz), BF16)] * 2, [], "outer", [whole(a.shape) for a in ins]
    )(*ins)
    x_lo = forward(high, "gx")
    x_hi = backward(low, "gx")

    images = (own, from_left_a, from_right_a, from_left_b, from_right_b)
    ins = (*images, x_lo, x_hi, low_y, high_y)
    first, final = call(
        functools.partial(edge_kernel, groups),
        [struct((5, nx + 2, nz), BF16)] * 2,
        [pltpu.VMEM((4, nx + 2, nz), F32)] * 2,
        "edges",
        [whole(a.shape) for a in ins],
    )(*ins)
    y_lo = forward(final, "gy")
    y_hi = backward(first, "gy")
    return force(
        groups, images, band, x_lo, x_hi, y_lo, y_hi, adj_zero, adj_one, halo_one, velocity
    )


def solution(mesh):
    in_specs = (
        P("gx", "gy", None),
        P("gx", "gy", None),
        P(None, None, "gx", "gy", None),
        P(None, "gx", "gy", None),
    )
    out_specs = P(None, None, "gx", "gy", None)
    return jax.shard_map(body, mesh=mesh, in_specs=in_specs, out_specs=out_specs, check_vma=False)
```

```python
import functools

import jax
import jax.numpy as jnp
from jax import lax
from jax.experimental import pallas as pl
from jax.experimental.pallas import tpu as pltpu
from jax.sharding import PartitionSpec as P

F32 = jnp.float32
BF16 = jnp.bfloat16
VMEM_LIMIT = 48 << 20


def whole(shape):
    return pl.BlockSpec(shape, lambda *_: (0,) * len(shape))


def call(kernel, outs, scratch, name, in_specs, out_specs=None, steps=(1,)):
    return pl.pallas_call(
        kernel,
        name=name,
        grid=steps,
        in_specs=in_specs,
        out_specs=out_specs or [whole(o.shape) for o in outs],
        out_shape=outs,
        scratch_shapes=scratch,
        cost_estimate=pl.CostEstimate(flops=0, transcendentals=0, bytes_accessed=0),
        compiler_params=pltpu.CompilerParams(vmem_limit_bytes=VMEM_LIMIT),
    )


def struct(shape, dtype):
    return jax.ShapeDtypeStruct(shape, dtype)


def face_flux(here, following, speed_here, speed_following):
    total = speed_here + speed_following
    return jnp.minimum(total, 0.0) * here + jnp.maximum(total, 0.0) * following


def depth_change(p, vz):
    nz = p.shape[1]
    lanes = lax.broadcasted_iota(jnp.int32, p.shape, 1)
    p_up = jnp.where(lanes == nz - 1, 0.0, pltpu.roll(p, nz - 1, 1))
    v_up = jnp.where(lanes == nz - 1, 0.0, pltpu.roll(vz, nz - 1, 1))
    upper = face_flux(p, p_up, vz, v_up)
    lower = jnp.where(lanes == 0, jnp.maximum(vz, 0.0) * p, pltpu.roll(upper, 1, 1))
    return upper - lower


def plane_change(p, vy, vz, below, above):
    ny = p.shape[0]
    rows = lax.broadcasted_iota(jnp.int32, p.shape, 0)
    p_up = jnp.where(rows == ny - 1, above[0], pltpu.roll(p, ny - 1, 0))
    v_up = jnp.where(rows == ny - 1, above[1], pltpu.roll(vy, ny - 1, 0))
    upper = face_flux(p, p_up, vy, v_up)
    first = face_flux(below[0], p[0:1], below[1], vy[0:1])
    lower = jnp.where(rows == 0, first, pltpu.roll(upper, 1, 0))
    return (upper - lower) + depth_change(p, vz)


NEAR_P, FAR_P, NEAR_N, FAR_N, NEAR_T, NEAR_Z, NEAR_EARLY = range(7)


def column_kernel(p_any, v_any, low, high, p_lo, p_hi, v_lo, v_hi, sem):
    nx = p_any.shape[0]
    copies = []
    for at, (p, v, x) in enumerate(((p_lo, v_lo, 0), (p_hi, v_hi, nx - 2))):
        copies.append(pltpu.make_async_copy(p_any.at[pl.ds(x, 2)], p, sem.at[2 * at]))
        copies.append(pltpu.make_async_copy(v_any.at[:, :, pl.ds(x, 2)], v, sem.at[2 * at + 1]))
    for copy in copies:
        copy.start()
    for copy in copies:
        copy.wait()
    for msg, p, v, near, far in ((low, p_lo, v_lo, 0, 1), (high, p_hi, v_hi, 1, 0)):
        msg[NEAR_P] = p[near].astype(BF16)
        msg[FAR_P] = p[far].astype(BF16)
        msg[NEAR_N] = v[1, 0, near]
        msg[FAR_N] = v[1, 0, far]
        msg[NEAR_T] = v[1, 1, near]
        msg[NEAR_Z] = v[1, 2, near]
        msg[NEAR_EARLY] = v[0, 0, near]


def column_messages(field, velocity):
    nx, ny, nz = field.shape
    outs = [struct((7, ny, nz), BF16)] * 2
    scratch = [pltpu.VMEM((2, ny, nz), F32)] * 2
    scratch += [pltpu.VMEM((2, 3, 2, ny, nz), BF16)] * 2 + [pltpu.SemaphoreType.DMA((4,))]
    in_specs = [pl.BlockSpec(memory_space=pltpu.HBM)] * 2
    return call(column_kernel, outs, scratch, "columns", in_specs)(field, velocity)


def rows_kernel(p_ref, v_ref, hxl, hxh, code, lo, hi, s_lo, s_hi):
    nx, ny, _ = p_ref.shape
    s_lo[...] = jnp.zeros(s_lo.shape, F32)
    s_hi[...] = jnp.zeros(s_hi.shape, F32)

    def put(layer, x, cells, width):
        at = pl.ds(x + 1, 1)
        for d in range(width):
            s_lo[layer + d, at, :] = cells[d : d + 1]
            s_hi[layer + d, at, :] = cells[ny - 1 - d : ny - d]

    def step(x, carry):
        put(NEAR_P, x, p_ref[x], 2)
        put(NEAR_N, x, v_ref[1, 1, x].astype(F32), 2)
        put(NEAR_T, x, v_ref[1, 0, x].astype(F32), 1)
        put(NEAR_Z, x, v_ref[1, 2, x].astype(F32), 1)
        put(NEAR_EARLY, x, v_ref[0, 1, x].astype(F32), 1)
        return carry

    lax.fori_loop(0, nx, step, 0)
    for x, halo in ((-1, hxl), (nx, hxh)):
        put(NEAR_P, x, halo[NEAR_P].astype(F32), 1)
        put(NEAR_N, x, halo[NEAR_T].astype(F32), 1)
        put(NEAR_T, x, halo[NEAR_N].astype(F32), 1)
    s_lo[FAR_P, 0:1, :] = code[...]
    s_hi[FAR_P, 0:1, :] = code[...]
    lo[...] = s_lo[...].astype(BF16)
    hi[...] = s_hi[...].astype(BF16)


def upwind_one_kernel(
    inside, p_ref, v_ref, hxl, hxh, hyl, hyh, out, oxl, oxh, oyl, oyh,
    s_yl, s_yh, s_p0, s_p1, s_v0, s_v1,
):
    nx, ny, nz = p_ref.shape
    s_yl[...] = hyl[...].astype(F32)
    s_yh[...] = hyh[...].astype(F32)

    def plane(x, flux_below, p, speeds, p_next, vx_next):
        vx, vy, vz = speeds
        flux_above = face_flux(p, p_next, vx, vx_next)
        at = pl.ds(x + 1, 1)
        below = s_yl[NEAR_P, at, :], s_yl[NEAR_N, at, :]
        above = s_yh[NEAR_P, at, :], s_yh[NEAR_N, at, :]
        change = (flux_above - flux_below) + plane_change(p, vy, vz, below, above)
        return p + 0.5 * change, flux_above

    def speed(c, x):
        return v_ref[0, c, x].astype(F32)

    def halo_plane(halo):
        return [halo[i].astype(F32) for i in (NEAR_P, FAR_P, NEAR_N, FAR_N, NEAR_T, NEAR_Z)]

    p, p_far, vx, vx_far, vy, vz = halo_plane(hxl)
    flux = face_flux(p_far, p, vx_far, vx)
    got, flux = plane(-1, flux, p, (vx, vy, vz), p_ref[0], speed(0, 0))
    oxl[...] = got * inside[0]
    p_high, p_far, vx_high, vx_far, vy_high, vz_high = halo_plane(hxh)

    def inner(x, flux, p_next, vx_next):
        p = p_ref[x]
        vy = speed(1, x)
        got, flux = plane(x, flux, p, (speed(0, x), vy, speed(2, x)), p_next, vx_next)
        out[x] = got
        at = pl.ds(x, 1)
        s_p0[at, :] = p[0:1]
        s_p1[at, :] = p[ny - 1 : ny]
        s_v0[at, :] = vy[0:1]
        s_v1[at, :] = vy[ny - 1 : ny]
        return flux

    flux = lax.fori_loop(0, nx - 1, lambda x, f: inner(x, f, p_ref[x + 1], speed(0, x + 1)), flux)
    flux = inner(nx - 1, flux, p_high, vx_high)
    got, _ = plane(nx, flux, p_high, (vx_high, vy_high, vz_high), p_far, vx_far)
    oxh[...] = got * inside[1]

    for scr, edge_p, edge_v, dest, flag, sign in (
        (s_yl, s_p0, s_v0, oyl, inside[2], 1.0),
        (s_yh, s_p1, s_v1, oyh, inside[3], -1.0),
    ):
        mid = slice(1, nx + 1)
        p, vy = scr[NEAR_P, mid, :], scr[NEAR_N, mid, :]
        flux_x = face_flux(
            scr[NEAR_P, 0 : nx + 1, :], scr[NEAR_P, 1 : nx + 2, :],
            scr[NEAR_T, 0 : nx + 1, :], scr[NEAR_T, 1 : nx + 2, :],
        )
        change = flux_x[1:] - flux_x[:-1]
        far = (scr[FAR_P, mid, :], scr[FAR_N, mid, :])
        near = (edge_p[...], edge_v[...])
        before, following = (far, near) if sign > 0 else (near, far)
        change = change + (
            face_flux(p, following[0], vy, following[1]) - face_flux(before[0], p, before[1], vy)
        )
        change = change + depth_change(p, scr[NEAR_Z, mid, :])
        dest[...] = (p + 0.5 * change) * flag


def upwind_zero_kernel(
    p_ref, v_ref, pxl, pxh, pyl, pyh, hxl, hxh, hyl, hyh, out, fxl, fxh, fyl, fyh,
    s_vl, s_vh, s_fl, s_fh,
):
    nx, ny, nz = p_ref.shape
    s_vl[...] = hyl[NEAR_EARLY].astype(F32)
    s_vh[...] = hyh[NEAR_EARLY].astype(F32)

    def speed(c, x):
        return v_ref[0, c, x].astype(F32)

    def plane(x, flux_below, p_next, vx_next):
        p = p_ref[x]
        flux_above = face_flux(p, p_next, speed(0, x), vx_next)
        at, halo_at = pl.ds(x, 1), pl.ds(x + 1, 1)
        below = pyl[at, :], s_vl[halo_at, :]
        above = pyh[at, :], s_vh[halo_at, :]
        change = (flux_above - flux_below) + plane_change(p, speed(1, x), speed(2, x), below, above)
        got = p + 0.5 * change
        out[x] = got
        s_fl[at, :] = got[0:1]
        s_fh[at, :] = got[ny - 1 : ny]
        return flux_above

    flux = face_flux(pxl[...], p_ref[0], hxl[NEAR_EARLY].astype(F32), speed(0, 0))
    flux = lax.fori_loop(0, nx - 1, lambda x, f: plane(x, f, p_ref[x + 1], speed(0, x + 1)), flux)
    plane(nx - 1, flux, pxh[...], hxh[NEAR_EARLY].astype(F32))
    fxl[0] = out[0].astype(BF16)
    fxh[0] = out[nx - 1].astype(BF16)
    fyl[0] = s_fl[...].astype(BF16)
    fyh[0] = s_fh[...].astype(BF16)


def speeds_spec(velocity, instant):
    block = (1,) + velocity.shape[1:]
    return pl.BlockSpec(block, lambda *_: (instant,) + (0,) * (len(block) - 1))


def upwind_one(inside, field, velocity, halo):
    nx, ny, nz = field.shape
    line = struct((ny, nz), F32)
    in_specs = [pl.BlockSpec(memory_space=pltpu.SMEM), whole(field.shape), speeds_spec(velocity, 1)]
    in_specs += [whole(h.shape) for h in halo]
    scratch = [pltpu.VMEM(halo[2].shape, F32)] * 2 + [pltpu.VMEM((nx, nz), F32)] * 4
    outs = [struct(field.shape, F32)] + [line] * 4
    return call(upwind_one_kernel, outs, scratch, "upwind_one", in_specs)(inside, field, velocity, *halo)


def upwind_zero(field, velocity, field_halo, halo):
    nx, ny, nz = field.shape
    in_specs = [whole(field.shape), speeds_spec(velocity, 0)]
    in_specs += [whole(h.shape) for h in (*field_halo, *halo)]
    scratch = [pltpu.VMEM((nx + 2, nz), F32)] * 2 + [pltpu.VMEM((nx, nz), F32)] * 2
    outs = [struct(field.shape, F32)] + [struct((1, ny, nz), BF16)] * 4
    return call(upwind_zero_kernel, outs, scratch, "upwind_zero", in_specs)(
        field, velocity, *field_halo, *halo
    )


def choice_kernel(edge, blocks, left, right, own, send, keep):
    _, height, width = keep.shape
    nz = own.shape[1]
    lane = lax.broadcasted_iota(jnp.int32, (nz, width), 1)
    slot = lax.broadcasted_iota(jnp.int32, (nz, width), 0)
    spread = jnp.where(lane // edge == slot, 1.0, 0.0).astype(BF16)
    row = lax.broadcasted_iota(jnp.int32, (height, width), 0)
    within = lax.broadcasted_iota(jnp.int32, (8, width), 1) % edge
    codes = (left[FAR_P, 0:1, :].astype(F32), right[FAR_P, 0:1, :].astype(F32), own[...])
    for code, side, out, d in zip(codes, (2, 0, 1), (send, send, keep), (0, 1, 0)):
        code = jnp.broadcast_to(code, (8, nz)).astype(BF16)
        code = jnp.dot(code, spread, preferred_element_type=F32).astype(jnp.int32)
        start = (code - side * blocks) * edge
        good = (start >= 0) & (start < height)
        wanted = jnp.where(good, start + within, -1)[0:1]
        out[d] = jnp.where(row == wanted, 1.0, 0.0).astype(BF16)


def choices(left, right, own, edge, slots):
    nz = own.shape[1]
    outs = [struct((count, 3 * nz, slots * edge), BF16) for count in (2, 1)]
    kernel = functools.partial(choice_kernel, edge, 3 * nz // edge)
    in_specs = [whole(a.shape) for a in (left, right, own)]
    return call(kernel, outs, [], "choices", in_specs)(left, right, own)


def planes_of(ref, planes):
    ny, width = ref.shape[1:]
    parts = [ref[a:b].reshape((b - a) * ny, width) for a, b in planes]
    return parts[0] if len(parts) == 1 else jnp.concatenate(parts, axis=0)


def pick_kernel(planes, t_lo, t_own, t_hi, q_ref, *outs):
    ny, nz = t_own.shape[1:]
    rows = jnp.concatenate([planes_of(ref, planes) for ref in (t_lo, t_own, t_hi)], axis=1)
    count = rows.shape[0] // ny
    for d, out in enumerate(outs):
        got = jnp.dot(rows, q_ref[d], preferred_element_type=F32).astype(BF16)
        out[0:count] = got[:, :nz].reshape(count, ny, nz)
        out[count : 2 * count] = got[:, nz:].reshape(count, ny, nz)


def pick(columns, choices, planes, name):
    _, ny, nz = columns[1].shape
    count = 2 * sum(b - a for a, b in planes)
    outs = [struct((count, ny, nz), BF16)] * choices.shape[0]
    ins = (*columns, choices)
    in_specs = [whole(a.shape) for a in ins]
    return call(functools.partial(pick_kernel, planes), outs, [], name, in_specs)(*ins)


def outer_kernel(nx, count, own, la, ra, face_lo, face_hi, low, high):
    for k in range(2):
        for c in range(2):
            x, a = k * nx + c, k * count + c
            low[2 * k + c] = own[x] + la[a] + ra[a]
            x, a = (k + 1) * nx - 2 + c, (k + 1) * count - 2 + c
            high[2 * k + c] = own[x] + la[a] + ra[a]
    low[4] = face_lo[0]
    high[4] = face_hi[0]


def each_plane(groups, images, k, visit):
    own, la, ra, lb, rb = images
    nx = sum(b - a for planes in groups for a, b in planes)
    for planes, lefts, rights in ((groups[0], la, ra), (groups[1], lb, rb)):
        at = k * sum(b - a for a, b in planes)
        for a, b in planes:

            def step(x, carry, shift=at - a, lefts=lefts, rights=rights):
                visit(x, own[k * nx + x] + lefts[x + shift] + rights[x + shift])
                return carry

            lax.fori_loop(a, b, step, 0, unroll=8)
            at += b - a


def edge_kernel(
    groups, own, la, ra, lb, rb, xlo, xhi, face_lo, face_hi, first, final, s_first, s_final
):
    nx, (ny, nz) = own.shape[0] // 2, own.shape[1:]
    for k in range(2):

        def put(x, cells, k=k):
            at = pl.ds(x + 1, 1)
            cells = cells.astype(F32)
            for c in range(2):
                s_first[2 * k + c, at, :] = cells[c : c + 1]
                s_final[2 * k + c, at, :] = cells[ny - 2 + c : ny - 1 + c]

        put(-1, xlo[2 * k + 1])
        put(nx, xhi[2 * k])
        each_plane(groups, (own, la, ra, lb, rb), k, put)
    for faces, scr, msg in ((face_lo, s_first, first), (face_hi, s_final, final)):
        msg[0:4] = scr[...].astype(BF16)
        msg[4] = jnp.zeros(msg.shape[1:], BF16)
        msg[4, 0:nx] = faces[0]


def force_kernel(
    groups, own, la, ra, lb, rb, band, xlo, xhi, ylo, yhi, adj0, adj1, bxl, bxh, byl, byh, vel,
    out, img, packed, frc, s_ylo, s_yhi, s_c0, s_c1, s_fl, s_fh, s_al, s_ah,
):
    k = pl.program_id(0)
    chunk = pl.program_id(1)
    deep = out.shape[2]
    nx, ny, nz = adj0.shape
    rows = lax.broadcasted_iota(jnp.int32, (ny, nz), 0)
    lanes = lax.broadcasted_iota(jnp.int32, (ny, nz), 1)
    first_image = k == 0

    def this(zero, one):
        return jnp.where(first_image, zero.astype(F32), one.astype(F32))

    def along_z(cells, index, length):
        following = jnp.where(index == length - 1, 0.0, pltpu.roll(cells, length - 1, 1))
        before = jnp.where(index == 0, 0.0, pltpu.roll(cells, 1, 1))
        return following, before

    @pl.when(chunk == 0)
    def _():
        for h in range(2):
            img[h] = xlo[2 * k + h].astype(F32)
            img[nx + 2 + h] = xhi[2 * k + h].astype(F32)

        def fill(x, cells):
            packed[x] = cells
            cells = cells.astype(F32)
            img[x + 2] = cells
            s_c0[pl.ds(x, 1), :] = cells[0:1]
            s_c1[pl.ds(x, 1), :] = cells[ny - 1 : ny]

        each_plane(groups, (own, la, ra, lb, rb), 0, fill)
        every = packed[...].reshape(nx * ny, nz)
        frc[2, 1 : nx + 1] = jnp.dot(every, band[...], preferred_element_type=F32).reshape(nx, ny, nz)
        for h in range(2):
            s_ylo[h] = ylo[2 * k + h].astype(F32)
            s_yhi[h] = yhi[2 * k + h].astype(F32)
        s_al[...] = this(ylo[4, 0:nx], byl[...])
        s_ah[...] = this(yhi[4, 0:nx], byh[...])

        def forces(x, half, slope_z):
            cells = img[x + 2]
            at = pl.ds(x + 1, 1)
            frc[0, x + 1] = half * (img[x + 3] - img[x + 1])
            up = jnp.where(rows == ny - 1, s_yhi[0, at, :], pltpu.roll(cells, ny - 1, 0))
            down = jnp.where(rows == 0, s_ylo[1, at, :], pltpu.roll(cells, 1, 0))
            frc[1, x + 1] = half * (up - down)
            frc[2, x + 1] = half * slope_z

        for x, half in ((-1, 0.5 * this(xlo[4], bxl[...])), (nx, 0.5 * this(xhi[4], bxh[...]))):
            following, before = along_z(img[x + 2], lanes, nz)
            forces(x, half, following - before)

        def force_step(x, carry):
            forces(x, 0.5 * this(adj0[x], adj1[x]), frc[2, x + 1])
            return carry

        lax.fori_loop(0, nx, force_step, 0, unroll=8)
        lines = lax.broadcasted_iota(jnp.int32, (nx, nz), 1)
        for cols, near, far, beside, half, dest, sign in (
            (s_ylo, 1, 0, s_c0, s_al, s_fl, 1.0),
            (s_yhi, 0, 1, s_c1, s_ah, s_fh, -1.0),
        ):
            weight = 0.5 * half[...]
            dest[0] = weight * (cols[near, 2 : nx + 2, :] - cols[near, 0:nx, :])
            dest[1] = (sign * weight) * (beside[...] - cols[far, 1 : nx + 1, :])
            following, before = along_z(cols[near, 1 : nx + 1, :], lines, nz)
            dest[2] = weight * (following - before)

    def smooth_step(i, carry):
        x = chunk * deep + i
        at = pl.ds(x, 1)
        for c in range(3):
            f = frc[c, x + 1]
            up = jnp.where(rows == ny - 1, s_fh[c, at, :], pltpu.roll(f, ny - 1, 0))
            down = jnp.where(rows == 0, s_fl[c, at, :], pltpu.roll(f, 1, 0))
            following, before = along_z(f, lanes, nz)
            beside = (frc[c, x] + frc[c, x + 2]) + (up + down) + (following + before)
            out[0, c, i] = vel[0, c, i].astype(F32) + (0.25 * f + 0.125 * beside)
        return carry

    lax.fori_loop(0, deep, smooth_step, 0, unroll=8)


def force(groups, images, band, x_lo, x_hi, y_lo, y_hi, adj_zero, adj_one, halo_one, velocity):
    nx, ny, nz = adj_zero.shape
    deep = nx // 2
    block = pl.BlockSpec((1, 3, deep, ny, nz), lambda k, i: (k, 0, i, 0, 0))
    middle = [band, x_lo, x_hi, y_lo, y_hi, adj_zero, adj_one, *halo_one]
    counts = [nx] + [sum(b - a for a, b in planes) for planes in groups for _ in range(2)]
    in_specs = [pl.BlockSpec((count, ny, nz), lambda k, i: (k, 0, 0)) for count in counts]
    in_specs += [whole(a.shape) for a in middle] + [block]
    scratch = [
        pltpu.VMEM((nx + 4, ny, nz), F32),
        pltpu.VMEM((nx, ny, nz), BF16),
        pltpu.VMEM((3, nx + 2, ny, nz), F32),
        pltpu.VMEM((2, nx + 2, nz), F32),
        pltpu.VMEM((2, nx + 2, nz), F32),
        pltpu.VMEM((nx, nz), F32),
        pltpu.VMEM((nx, nz), F32),
        pltpu.VMEM((3, nx, nz), F32),
        pltpu.VMEM((3, nx, nz), F32),
        pltpu.VMEM((nx, nz), F32),
        pltpu.VMEM((nx, nz), F32),
    ]
    return call(
        functools.partial(force_kernel, groups),
        struct((2, 3, nx, ny, nz), F32),
        scratch,
        "force",
        in_specs,
        block,
        (2, 2),
    )(*images, *middle, velocity)


def forward(value, axis):
    ends = lax.axis_size(axis) - 1
    return lax.ppermute(value, axis, [(i, i + 1) for i in range(ends)])


def backward(value, axis):
    ends = lax.axis_size(axis) - 1
    return lax.ppermute(value, axis, [(i + 1, i) for i in range(ends)])


def body(template, mismatch, velocity, src_ids):
    nx, ny, nz = template.shape
    depth_blocks = src_ids.shape[3]
    edge = nz // depth_blocks
    slots = 2 * depth_blocks
    index_first = lax.axis_index("gx")
    index_second = lax.axis_index("gy")
    count_first = lax.axis_size("gx")
    count_second = lax.axis_size("gy")

    low, high = column_messages(
        pltpu.with_memory_space_constraint(mismatch, pltpu.HBM),
        pltpu.with_memory_space_constraint(velocity, pltpu.HBM),
    )
    halo_xl = forward(high, "gx")
    halo_xh = backward(low, "gx")
    late_template, _ = lax.optimization_barrier((template, low))
    t_lo = forward(late_template, "gx")
    t_hi = backward(late_template, "gx")

    ids = src_ids.reshape(slots)
    first_block = ids // (count_second * depth_blocks)
    second_block = ids // depth_blocks % count_second
    start = (first_block - index_first + 1) * depth_blocks + ids % depth_blocks
    side = second_block - index_second + 1
    code = (side * (3 * depth_blocks) + start).astype(F32)
    code = jnp.pad(code.reshape(1, slots), ((0, 0), (0, nz - slots)))
    ins = (mismatch, velocity, halo_xl, halo_xh, code)
    rows = struct((7, nx + 2, nz), BF16)
    low, high = call(
        rows_kernel,
        [rows] * 2,
        [pltpu.VMEM(rows.shape, F32)] * 2,
        "rows",
        [whole(a.shape) for a in ins],
    )(*ins)
    halo_yl = forward(high, "gy")
    halo_yh = backward(low, "gy")
    halo = (halo_xl, halo_xh, halo_yl, halo_yh)
    inside = jnp.stack(
        [index_first > 0, index_first < count_first - 1, index_second > 0, index_second < count_second - 1]
    ).astype(F32)

    send_choice, own_choice = choices(halo_yl, halo_yh, code, edge, slots)
    z = jnp.arange(nz)
    band = (z[:, None] == z[None] + 1).astype(BF16) - (z[:, None] == z[None] - 1).astype(BF16)

    columns = (t_lo, template, t_hi)
    half = nx // 4
    groups = (((0, half), (nx - half, nx)), ((half, nx - half),))
    to_left_a, to_right_a = pick(columns, send_choice, groups[0], "pick_outer")
    from_left_a = forward(to_right_a, "gy")
    from_right_a = backward(to_left_a, "gy")
    columns, _ = lax.optimization_barrier((columns, to_left_a))
    to_left_b, to_right_b = pick(columns, send_choice, groups[1], "pick_inner")
    from_left_b = forward(to_right_b, "gy")
    from_right_b = backward(to_left_b, "gy")
    late_choice, late_mismatch, _ = lax.optimization_barrier((own_choice, mismatch, to_left_b))
    adj_one, *halo_one = upwind_one(inside, late_mismatch, velocity, halo)
    adj_zero, low_x, high_x, low_y, high_y = upwind_zero(adj_one, velocity, halo_one, halo)
    (own,) = pick(columns, late_choice, ((0, nx),), "pick_own")

    ins = (own, from_left_a, from_right_a, low_x, high_x)
    low, high = call(
        functools.partial(outer_kernel, nx, 2 * half),
        [struct((5, ny, nz), BF16)] * 2, [], "outer", [whole(a.shape) for a in ins]
    )(*ins)
    x_lo = forward(high, "gx")
    x_hi = backward(low, "gx")

    images = (own, from_left_a, from_right_a, from_left_b, from_right_b)
    ins = (*images, x_lo, x_hi, low_y, high_y)
    first, final = call(
        functools.partial(edge_kernel, groups),
        [struct((5, nx + 2, nz), BF16)] * 2,
        [pltpu.VMEM((4, nx + 2, nz), F32)] * 2,
        "edges",
        [whole(a.shape) for a in ins],
    )(*ins)
    y_lo = forward(final, "gy")
    y_hi = backward(first, "gy")
    return force(
        groups, images, band, x_lo, x_hi, y_lo, y_hi, adj_zero, adj_one, halo_one, velocity
    )


def solution(mesh):
    in_specs = (
        P("gx", "gy", None),
        P("gx", "gy", None),
        P(None, None, "gx", "gy", None),
        P(None, "gx", "gy", None),
    )
    out_specs = P(None, None, "gx", "gy", None)
    return jax.shard_map(body, mesh=mesh, in_specs=in_specs, out_specs=out_specs, check_vma=False)
```

```python
import functools

import jax
import jax.numpy as jnp
from jax import lax
from jax.experimental import pallas as pl
from jax.experimental.pallas import tpu as pltpu
from jax.sharding import PartitionSpec as P

F32 = jnp.float32
BF16 = jnp.bfloat16
VMEM_LIMIT = 48 << 20


def whole(shape):
    return pl.BlockSpec(shape, lambda *_: (0,) * len(shape))


def call(kernel, outs, scratch, name, in_specs, out_specs=None, steps=(1,)):
    return pl.pallas_call(
        kernel,
        name=name,
        grid=steps,
        in_specs=in_specs,
        out_specs=out_specs or [whole(o.shape) for o in outs],
        out_shape=outs,
        scratch_shapes=scratch,
        cost_estimate=pl.CostEstimate(flops=0, transcendentals=0, bytes_accessed=0),
        compiler_params=pltpu.CompilerParams(vmem_limit_bytes=VMEM_LIMIT),
    )


def struct(shape, dtype):
    return jax.ShapeDtypeStruct(shape, dtype)


def face_flux(here, following, speed_here, speed_following):
    total = speed_here + speed_following
    return jnp.minimum(total, 0.0) * here + jnp.maximum(total, 0.0) * following


def depth_change(p, vz):
    nz = p.shape[1]
    lanes = lax.broadcasted_iota(jnp.int32, p.shape, 1)
    p_up = jnp.where(lanes == nz - 1, 0.0, pltpu.roll(p, nz - 1, 1))
    v_up = jnp.where(lanes == nz - 1, 0.0, pltpu.roll(vz, nz - 1, 1))
    upper = face_flux(p, p_up, vz, v_up)
    lower = jnp.where(lanes == 0, jnp.maximum(vz, 0.0) * p, pltpu.roll(upper, 1, 1))
    return upper - lower


def plane_change(p, vy, vz, below, above):
    ny = p.shape[0]
    rows = lax.broadcasted_iota(jnp.int32, p.shape, 0)
    p_up = jnp.where(rows == ny - 1, above[0], pltpu.roll(p, ny - 1, 0))
    v_up = jnp.where(rows == ny - 1, above[1], pltpu.roll(vy, ny - 1, 0))
    upper = face_flux(p, p_up, vy, v_up)
    first = face_flux(below[0], p[0:1], below[1], vy[0:1])
    lower = jnp.where(rows == 0, first, pltpu.roll(upper, 1, 0))
    return (upper - lower) + depth_change(p, vz)


NEAR_P, FAR_P, NEAR_N, FAR_N, NEAR_T, NEAR_Z, NEAR_EARLY = range(7)


def column_kernel(p_any, v_any, low, high, p_lo, p_hi, v_lo, v_hi, sem):
    nx = p_any.shape[0]
    copies = []
    for at, (p, v, x) in enumerate(((p_lo, v_lo, 0), (p_hi, v_hi, nx - 2))):
        copies.append(pltpu.make_async_copy(p_any.at[pl.ds(x, 2)], p, sem.at[2 * at]))
        copies.append(pltpu.make_async_copy(v_any.at[:, :, pl.ds(x, 2)], v, sem.at[2 * at + 1]))
    for copy in copies:
        copy.start()
    for copy in copies:
        copy.wait()
    for msg, p, v, near, far in ((low, p_lo, v_lo, 0, 1), (high, p_hi, v_hi, 1, 0)):
        msg[NEAR_P] = p[near].astype(BF16)
        msg[FAR_P] = p[far].astype(BF16)
        msg[NEAR_N] = v[1, 0, near]
        msg[FAR_N] = v[1, 0, far]
        msg[NEAR_T] = v[1, 1, near]
        msg[NEAR_Z] = v[1, 2, near]
        msg[NEAR_EARLY] = v[0, 0, near]


def column_messages(field, velocity):
    nx, ny, nz = field.shape
    outs = [struct((7, ny, nz), BF16)] * 2
    scratch = [pltpu.VMEM((2, ny, nz), F32)] * 2
    scratch += [pltpu.VMEM((2, 3, 2, ny, nz), BF16)] * 2 + [pltpu.SemaphoreType.DMA((4,))]
    in_specs = [pl.BlockSpec(memory_space=pltpu.HBM)] * 2
    return call(column_kernel, outs, scratch, "columns", in_specs)(field, velocity)


def rows_kernel(p_ref, v_ref, lo, hi):
    nx, ny, _ = p_ref.shape
    lo[...] = jnp.zeros(lo.shape, F32)
    hi[...] = jnp.zeros(hi.shape, F32)

    def put(layer, x, cells, width):
        for d in range(width):
            at = pl.ds((layer + d) * (nx + 2) + x + 1, 1)
            lo[at, :] = cells[d : d + 1]
            hi[at, :] = cells[ny - 1 - d : ny - d]

    def step(x, carry):
        put(NEAR_P, x, p_ref[x], 2)
        put(NEAR_N, x, v_ref[1, 1, x].astype(F32), 2)
        put(NEAR_T, x, v_ref[1, 0, x].astype(F32), 1)
        put(NEAR_Z, x, v_ref[1, 2, x].astype(F32), 1)
        put(NEAR_EARLY, x, v_ref[0, 1, x].astype(F32), 1)
        return carry

    lax.fori_loop(0, nx, step, 0)


def unpack(ref, flat, layers):
    flat[...] = ref[...].reshape(flat.shape).astype(F32)
    count = layers.shape[1]
    for layer in range(layers.shape[0]):
        layers[layer] = flat[layer * count : (layer + 1) * count, :]


def upwind_one_kernel(
    inside, p_ref, v_ref, hxl, hxh, hyl, hyh, out, oxl, oxh, oyl, oyh,
    s_flat, s_yl, s_yh, s_p0, s_p1, s_v0, s_v1,
):
    nx, ny, nz = p_ref.shape
    unpack(hyl, s_flat, s_yl)
    unpack(hyh, s_flat, s_yh)

    def plane(x, flux_below, p, speeds, p_next, vx_next):
        vx, vy, vz = speeds
        flux_above = face_flux(p, p_next, vx, vx_next)
        at = pl.ds(x + 1, 1)
        below = s_yl[NEAR_P, at, :], s_yl[NEAR_N, at, :]
        above = s_yh[NEAR_P, at, :], s_yh[NEAR_N, at, :]
        change = (flux_above - flux_below) + plane_change(p, vy, vz, below, above)
        return p + 0.5 * change, flux_above

    def speed(c, x):
        return v_ref[0, c, x].astype(F32)

    def halo_plane(halo):
        return [halo[i].astype(F32) for i in (NEAR_P, FAR_P, NEAR_N, FAR_N, NEAR_T, NEAR_Z)]

    p, p_far, vx, vx_far, vy, vz = halo_plane(hxl)
    flux = face_flux(p_far, p, vx_far, vx)
    got, flux = plane(-1, flux, p, (vx, vy, vz), p_ref[0], speed(0, 0))
    oxl[...] = got * inside[0]
    p_high, p_far, vx_high, vx_far, vy_high, vz_high = halo_plane(hxh)

    def inner(x, flux, p_next, vx_next):
        p = p_ref[x]
        vy = speed(1, x)
        got, flux = plane(x, flux, p, (speed(0, x), vy, speed(2, x)), p_next, vx_next)
        out[x] = got
        at = pl.ds(x, 1)
        s_p0[at, :] = p[0:1]
        s_p1[at, :] = p[ny - 1 : ny]
        s_v0[at, :] = vy[0:1]
        s_v1[at, :] = vy[ny - 1 : ny]
        return flux

    flux = lax.fori_loop(0, nx - 1, lambda x, f: inner(x, f, p_ref[x + 1], speed(0, x + 1)), flux)
    flux = inner(nx - 1, flux, p_high, vx_high)
    got, _ = plane(nx, flux, p_high, (vx_high, vy_high, vz_high), p_far, vx_far)
    oxh[...] = got * inside[1]

    for scr, edge_p, edge_v, dest, flag, sign in (
        (s_yl, s_p0, s_v0, oyl, inside[2], 1.0),
        (s_yh, s_p1, s_v1, oyh, inside[3], -1.0),
    ):
        mid = slice(1, nx + 1)
        p, vy = scr[NEAR_P, mid, :], scr[NEAR_N, mid, :]
        flux_x = face_flux(
            scr[NEAR_P, 0 : nx + 1, :], scr[NEAR_P, 1 : nx + 2, :],
            scr[NEAR_T, 0 : nx + 1, :], scr[NEAR_T, 1 : nx + 2, :],
        )
        change = flux_x[1:] - flux_x[:-1]
        far = (scr[FAR_P, mid, :], scr[FAR_N, mid, :])
        near = (edge_p[...], edge_v[...])
        before, following = (far, near) if sign > 0 else (near, far)
        change = change + (
            face_flux(p, following[0], vy, following[1]) - face_flux(before[0], p, before[1], vy)
        )
        change = change + depth_change(p, scr[NEAR_Z, mid, :])
        dest[...] = (p + 0.5 * change) * flag


def upwind_zero_kernel(
    p_ref, v_ref, pxl, pxh, pyl, pyh, hxl, hxh, hyl, hyh, out, fxl, fxh, fyl, fyh,
    s_flat, s_vl, s_vh, s_fl, s_fh,
):
    nx, ny, nz = p_ref.shape
    unpack(hyl, s_flat, s_vl)
    unpack(hyh, s_flat, s_vh)

    def speed(c, x):
        return v_ref[0, c, x].astype(F32)

    def plane(x, flux_below, p_next, vx_next):
        p = p_ref[x]
        flux_above = face_flux(p, p_next, speed(0, x), vx_next)
        at, halo_at = pl.ds(x, 1), pl.ds(x + 1, 1)
        below = pyl[at, :], s_vl[NEAR_EARLY, halo_at, :]
        above = pyh[at, :], s_vh[NEAR_EARLY, halo_at, :]
        change = (flux_above - flux_below) + plane_change(p, speed(1, x), speed(2, x), below, above)
        got = p + 0.5 * change
        out[x] = got
        s_fl[at, :] = got[0:1]
        s_fh[at, :] = got[ny - 1 : ny]
        return flux_above

    flux = face_flux(pxl[...], p_ref[0], hxl[NEAR_EARLY].astype(F32), speed(0, 0))
    flux = lax.fori_loop(0, nx - 1, lambda x, f: plane(x, f, p_ref[x + 1], speed(0, x + 1)), flux)
    plane(nx - 1, flux, pxh[...], hxh[NEAR_EARLY].astype(F32))
    fxl[0] = out[0].astype(BF16)
    fxh[0] = out[nx - 1].astype(BF16)
    fyl[0] = s_fl[...].astype(BF16)
    fyh[0] = s_fh[...].astype(BF16)


def speeds_spec(velocity, instant):
    block = (1,) + velocity.shape[1:]
    return pl.BlockSpec(block, lambda *_: (instant,) + (0,) * (len(block) - 1))


def halo_specs(field, halo):
    nx, ny, nz = field.shape
    planes = halo[2].shape[0] - 8
    return [whole(halo[0].shape)] * 2 + [pl.BlockSpec((8, ny, nz), lambda *_: (planes // 8, 0, 0))] * 2


def halo_scratch(field):
    nx, ny, nz = field.shape
    return [pltpu.VMEM((8 * ny, nz), F32)] + [pltpu.VMEM((7, nx + 2, nz), F32)] * 2


def upwind_one(inside, field, velocity, halo):
    nx, ny, nz = field.shape
    line = struct((ny, nz), F32)
    in_specs = [pl.BlockSpec(memory_space=pltpu.SMEM), whole(field.shape), speeds_spec(velocity, 1)]
    in_specs += halo_specs(field, halo)
    scratch = halo_scratch(field) + [pltpu.VMEM((nx, nz), F32)] * 4
    outs = [struct(field.shape, F32)] + [line] * 4
    return call(upwind_one_kernel, outs, scratch, "upwind_one", in_specs)(inside, field, velocity, *halo)


def upwind_zero(field, velocity, field_halo, halo):
    nx, ny, nz = field.shape
    in_specs = [whole(field.shape), speeds_spec(velocity, 0)]
    in_specs += [whole(h.shape) for h in field_halo] + halo_specs(field, halo)
    scratch = halo_scratch(field) + [pltpu.VMEM((nx, nz), F32)] * 2
    outs = [struct(field.shape, F32)] + [struct((1, ny, nz), BF16)] * 4
    return call(upwind_zero_kernel, outs, scratch, "upwind_zero", in_specs)(
        field, velocity, *field_halo, *halo
    )


def choice_kernel(edge, blocks, left, right, own, send, keep):
    _, height, width = keep.shape
    slots = width // edge
    lane = lax.broadcasted_iota(jnp.int32, (slots, width), 1)
    slot = lax.broadcasted_iota(jnp.int32, (slots, width), 0)
    spread = jnp.where(lane // edge == slot, 1.0, 0.0).astype(BF16)
    row = lax.broadcasted_iota(jnp.int32, (height, width), 0)
    within = lax.broadcasted_iota(jnp.int32, (8, width), 1) % edge
    for code, side, out, d in ((left, 2, send, 0), (right, 0, send, 1), (own, 1, keep, 0)):
        codes = jnp.broadcast_to(code[...], (8, slots)).astype(BF16)
        code = jnp.dot(codes, spread, preferred_element_type=F32).astype(jnp.int32)
        start = (code - side * blocks) * edge
        good = (start >= 0) & (start < height)
        wanted = jnp.where(good, start + within, -1)[0:1]
        out[d] = jnp.where(row == wanted, 1.0, 0.0).astype(BF16)


def choices(left, right, own, edge, nz):
    slots = own.shape[1]
    width = slots * edge
    outs = [struct((count, 3 * nz, width), BF16) for count in (2, 1)]
    kernel = functools.partial(choice_kernel, edge, 3 * nz // edge)
    in_specs = [whole(own.shape)] * 3
    return call(kernel, outs, [], "choices", in_specs)(left, right, own)


def planes_of(ref, planes):
    ny, width = ref.shape[1:]
    parts = [ref[a:b].reshape((b - a) * ny, width) for a, b in planes]
    return parts[0] if len(parts) == 1 else jnp.concatenate(parts, axis=0)


def pick_kernel(planes, t_lo, t_own, t_hi, q_ref, *rest):
    ny, nz = t_own.shape[1:]
    nx = t_own.shape[0]
    rows = jnp.concatenate([planes_of(ref, planes) for ref in (t_lo, t_own, t_hi)], axis=1)
    count = rows.shape[0] // ny
    outs = rest[-q_ref.shape[0] :]
    lines, halos = rest[:2], rest[2:4]
    if len(rest) == len(outs):
        lines = ()
    for d, out in enumerate(outs):
        got = jnp.dot(rows, q_ref[d], preferred_element_type=F32).astype(BF16)
        out[0:count] = got[:, :nz].reshape(count, ny, nz)
        out[count : 2 * count] = got[:, nz:].reshape(count, ny, nz)
    for d, ref in enumerate(lines):
        row = 0 if d == 0 else ny - 1
        for halo, x in ((halos[0], 0), (halos[1], nx + 1)):
            for layer, source in ((NEAR_P, NEAR_P), (NEAR_N, NEAR_T), (NEAR_T, NEAR_N)):
                at = layer * (nx + 2) + x
                ref[at : at + 1, :] = halo[source].astype(F32)[row : row + 1]
        outs[d][2 * count :] = ref[...].astype(BF16).reshape(-1, ny, nz)


def pick(columns, choices, planes, name, lines=()):
    _, ny, nz = columns[1].shape
    count = 2 * sum(b - a for a, b in planes)
    extra = lines[0].shape[0] // ny if lines else 0
    outs = [struct((count + extra, ny, nz), BF16)] * choices.shape[0]
    ins = (*columns, choices, *lines)
    in_specs = [whole(a.shape) for a in ins]
    return call(functools.partial(pick_kernel, planes), outs, [], name, in_specs)(*ins)


def outer_kernel(nx, count, own, la, ra, face_lo, face_hi, low, high):
    for k in range(2):
        for c in range(2):
            x, a = k * nx + c, k * count + c
            low[2 * k + c] = own[x] + la[a] + ra[a]
            x, a = (k + 1) * nx - 2 + c, (k + 1) * count - 2 + c
            high[2 * k + c] = own[x] + la[a] + ra[a]
    low[4] = face_lo[0]
    high[4] = face_hi[0]


def each_plane(groups, images, k, visit):
    own, la, ra, lb, rb = images
    nx = sum(b - a for planes in groups for a, b in planes)
    for planes, lefts, rights in ((groups[0], la, ra), (groups[1], lb, rb)):
        at = k * sum(b - a for a, b in planes)
        for a, b in planes:

            def step(x, carry, shift=at - a, lefts=lefts, rights=rights):
                visit(x, own[k * nx + x] + lefts[x + shift] + rights[x + shift])
                return carry

            lax.fori_loop(a, b, step, 0, unroll=8)
            at += b - a


def edge_kernel(
    groups, own, la, ra, lb, rb, xlo, xhi, face_lo, face_hi, first, final, s_first, s_final
):
    nx, (ny, nz) = own.shape[0] // 2, own.shape[1:]
    for k in range(2):

        def put(x, cells, k=k):
            at = pl.ds(x + 1, 1)
            cells = cells.astype(F32)
            for c in range(2):
                s_first[2 * k + c, at, :] = cells[c : c + 1]
                s_final[2 * k + c, at, :] = cells[ny - 2 + c : ny - 1 + c]

        put(-1, xlo[2 * k + 1])
        put(nx, xhi[2 * k])
        each_plane(groups, (own, la, ra, lb, rb), k, put)
    for faces, scr, msg in ((face_lo, s_first, first), (face_hi, s_final, final)):
        msg[0:4] = scr[...].astype(BF16)
        msg[4] = jnp.zeros(msg.shape[1:], BF16)
        msg[4, 0:nx] = faces[0]


def force_kernel(
    groups, own, la, ra, lb, rb, band, xlo, xhi, ylo, yhi, adj0, adj1, bxl, bxh, byl, byh, vel,
    out, img, packed, frc, s_ylo, s_yhi, s_c0, s_c1, s_fl, s_fh, s_al, s_ah,
):
    k = pl.program_id(0)
    chunk = pl.program_id(1)
    deep = out.shape[2]
    nx, ny, nz = adj0.shape
    rows = lax.broadcasted_iota(jnp.int32, (ny, nz), 0)
    lanes = lax.broadcasted_iota(jnp.int32, (ny, nz), 1)
    first_image = k == 0

    def this(zero, one):
        return jnp.where(first_image, zero.astype(F32), one.astype(F32))

    def along_z(cells, index, length):
        following = jnp.where(index == length - 1, 0.0, pltpu.roll(cells, length - 1, 1))
        before = jnp.where(index == 0, 0.0, pltpu.roll(cells, 1, 1))
        return following, before

    @pl.when(chunk == 0)
    def _():
        for h in range(2):
            img[h] = xlo[2 * k + h].astype(F32)
            img[nx + 2 + h] = xhi[2 * k + h].astype(F32)

        def fill(x, cells):
            packed[x] = cells
            cells = cells.astype(F32)
            img[x + 2] = cells
            s_c0[pl.ds(x, 1), :] = cells[0:1]
            s_c1[pl.ds(x, 1), :] = cells[ny - 1 : ny]

        each_plane(groups, (own, la, ra, lb, rb), 0, fill)
        every = packed[...].reshape(nx * ny, nz)
        frc[2, 1 : nx + 1] = jnp.dot(every, band[...], preferred_element_type=F32).reshape(nx, ny, nz)
        for h in range(2):
            s_ylo[h] = ylo[2 * k + h].astype(F32)
            s_yhi[h] = yhi[2 * k + h].astype(F32)
        s_al[...] = this(ylo[4, 0:nx], byl[...])
        s_ah[...] = this(yhi[4, 0:nx], byh[...])

        def forces(x, half, slope_z):
            cells = img[x + 2]
            at = pl.ds(x + 1, 1)
            frc[0, x + 1] = half * (img[x + 3] - img[x + 1])
            up = jnp.where(rows == ny - 1, s_yhi[0, at, :], pltpu.roll(cells, ny - 1, 0))
            down = jnp.where(rows == 0, s_ylo[1, at, :], pltpu.roll(cells, 1, 0))
            frc[1, x + 1] = half * (up - down)
            frc[2, x + 1] = half * slope_z

        for x, half in ((-1, 0.5 * this(xlo[4], bxl[...])), (nx, 0.5 * this(xhi[4], bxh[...]))):
            following, before = along_z(img[x + 2], lanes, nz)
            forces(x, half, following - before)

        def force_step(x, carry):
            forces(x, 0.5 * this(adj0[x], adj1[x]), frc[2, x + 1])
            return carry

        lax.fori_loop(0, nx, force_step, 0, unroll=8)
        lines = lax.broadcasted_iota(jnp.int32, (nx, nz), 1)
        for cols, near, far, beside, half, dest, sign in (
            (s_ylo, 1, 0, s_c0, s_al, s_fl, 1.0),
            (s_yhi, 0, 1, s_c1, s_ah, s_fh, -1.0),
        ):
            weight = 0.5 * half[...]
            dest[0] = weight * (cols[near, 2 : nx + 2, :] - cols[near, 0:nx, :])
            dest[1] = (sign * weight) * (beside[...] - cols[far, 1 : nx + 1, :])
            following, before = along_z(cols[near, 1 : nx + 1, :], lines, nz)
            dest[2] = weight * (following - before)

    def smooth_step(i, carry):
        x = chunk * deep + i
        at = pl.ds(x, 1)
        for c in range(3):
            f = frc[c, x + 1]
            up = jnp.where(rows == ny - 1, s_fh[c, at, :], pltpu.roll(f, ny - 1, 0))
            down = jnp.where(rows == 0, s_fl[c, at, :], pltpu.roll(f, 1, 0))
            following, before = along_z(f, lanes, nz)
            beside = (frc[c, x] + frc[c, x + 2]) + (up + down) + (following + before)
            out[0, c, i] = vel[0, c, i].astype(F32) + (0.25 * f + 0.125 * beside)
        return carry

    lax.fori_loop(0, deep, smooth_step, 0, unroll=8)


def force(groups, images, band, x_lo, x_hi, y_lo, y_hi, adj_zero, adj_one, halo_one, velocity):
    nx, ny, nz = adj_zero.shape
    deep = nx // 2
    block = pl.BlockSpec((1, 3, deep, ny, nz), lambda k, i: (k, 0, i, 0, 0))
    middle = [band, x_lo, x_hi, y_lo, y_hi, adj_zero, adj_one, *halo_one]
    counts = [nx] + [sum(b - a for a, b in planes) for planes in groups for _ in range(2)]
    in_specs = [pl.BlockSpec((count, ny, nz), lambda k, i: (k, 0, 0)) for count in counts]
    in_specs += [whole(a.shape) for a in middle] + [block]
    scratch = [
        pltpu.VMEM((nx + 4, ny, nz), F32),
        pltpu.VMEM((nx, ny, nz), BF16),
        pltpu.VMEM((3, nx + 2, ny, nz), F32),
        pltpu.VMEM((2, nx + 2, nz), F32),
        pltpu.VMEM((2, nx + 2, nz), F32),
        pltpu.VMEM((nx, nz), F32),
        pltpu.VMEM((nx, nz), F32),
        pltpu.VMEM((3, nx, nz), F32),
        pltpu.VMEM((3, nx, nz), F32),
        pltpu.VMEM((nx, nz), F32),
        pltpu.VMEM((nx, nz), F32),
    ]
    return call(
        functools.partial(force_kernel, groups),
        struct((2, 3, nx, ny, nz), F32),
        scratch,
        "force",
        in_specs,
        block,
        (2, 2),
    )(*images, *middle, velocity)


def forward(value, axis):
    ends = lax.axis_size(axis) - 1
    return lax.ppermute(value, axis, [(i, i + 1) for i in range(ends)])


def backward(value, axis):
    ends = lax.axis_size(axis) - 1
    return lax.ppermute(value, axis, [(i + 1, i) for i in range(ends)])


def body(template, mismatch, velocity, src_ids):
    nx, ny, nz = template.shape
    depth_blocks = src_ids.shape[3]
    edge = nz // depth_blocks
    slots = 2 * depth_blocks
    index_first = lax.axis_index("gx")
    index_second = lax.axis_index("gy")
    count_first = lax.axis_size("gx")
    count_second = lax.axis_size("gy")

    t_lo = forward(template, "gx")
    t_hi = backward(template, "gx")
    ids = src_ids.reshape(slots)
    first_block = ids // (count_second * depth_blocks)
    second_block = ids // depth_blocks % count_second
    start = (first_block - index_first + 1) * depth_blocks + ids % depth_blocks
    side = second_block - index_second + 1
    code = (side * (3 * depth_blocks) + start).astype(BF16).reshape(1, slots)
    left_code = forward(code, "gy")
    right_code = backward(code, "gy")
    left_code, right_code, late_mismatch, late_velocity = lax.optimization_barrier(
        (left_code, right_code, mismatch, velocity)
    )
    low, high = column_messages(
        pltpu.with_memory_space_constraint(late_mismatch, pltpu.HBM),
        pltpu.with_memory_space_constraint(late_velocity, pltpu.HBM),
    )
    halo_xl = forward(high, "gx")
    halo_xh = backward(low, "gx")
    lines = call(
        rows_kernel,
        [struct((8 * ny, nz), F32)] * 2,
        [],
        "rows",
        [whole(a.shape) for a in (mismatch, velocity)],
    )(late_mismatch, late_velocity)

    send_choice, own_choice = choices(left_code, right_code, code, edge, nz)
    z = jnp.arange(nz)
    band = (z[:, None] == z[None] + 1).astype(BF16) - (z[:, None] == z[None] - 1).astype(BF16)

    columns = (t_lo, template, t_hi)
    margin = nx // 4
    groups = (((0, margin), (nx - margin, nx)), ((margin, nx - margin),))
    to_left_a, to_right_a = pick(columns, send_choice, groups[0], "pick_outer", (*lines, halo_xl, halo_xh))
    columns, _ = lax.optimization_barrier((columns, to_left_a))
    to_left_b, to_right_b = pick(columns, send_choice, groups[1], "pick_inner")
    from_left_b = forward(to_right_b, "gy")
    from_right_b = backward(to_left_b, "gy")
    from_left_a = forward(to_right_a, "gy")
    from_right_a = backward(to_left_a, "gy")

    late_mismatch, late_choice, _ = lax.optimization_barrier((mismatch, own_choice, to_left_b))
    (own,) = pick(columns, late_choice, ((0, nx),), "pick_own")
    inside = jnp.stack(
        [index_first > 0, index_first < count_first - 1, index_second > 0, index_second < count_second - 1]
    ).astype(F32)
    halo = (halo_xl, halo_xh, from_left_a, from_right_a)
    adj_one, *halo_one = upwind_one(inside, late_mismatch, velocity, halo)
    adj_zero, low_x, high_x, low_y, high_y = upwind_zero(adj_one, velocity, halo_one, halo)

    ins = (own, from_left_a, from_right_a, low_x, high_x)
    low, high = call(
        functools.partial(outer_kernel, nx, 2 * margin),
        [struct((5, ny, nz), BF16)] * 2, [], "outer", [whole(a.shape) for a in ins]
    )(*ins)
    x_lo = forward(high, "gx")
    x_hi = backward(low, "gx")

    images = (own, from_left_a, from_right_a, from_left_b, from_right_b)
    ins = (*images, x_lo, x_hi, low_y, high_y)
    first, final = call(
        functools.partial(edge_kernel, groups),
        [struct((5, nx + 2, nz), BF16)] * 2,
        [pltpu.VMEM((4, nx + 2, nz), F32)] * 2,
        "edges",
        [whole(a.shape) for a in ins],
    )(*ins)
    y_lo = forward(final, "gy")
    y_hi = backward(first, "gy")
    return force(
        groups, images, band, x_lo, x_hi, y_lo, y_hi, adj_zero, adj_one, halo_one, velocity
    )


def solution(mesh):
    in_specs = (
        P("gx", "gy", None),
        P("gx", "gy", None),
        P(None, None, "gx", "gy", None),
        P(None, "gx", "gy", None),
    )
    out_specs = P(None, None, "gx", "gy", None)
    return jax.shard_map(body, mesh=mesh, in_specs=in_specs, out_specs=out_specs, check_vma=False)
```

```python
import functools

import jax
import jax.numpy as jnp
from jax import lax
from jax.experimental import pallas as pl
from jax.experimental.pallas import tpu as pltpu
from jax.sharding import PartitionSpec as P

F32 = jnp.float32
BF16 = jnp.bfloat16
VMEM_LIMIT = 48 << 20


def whole(shape):
    return pl.BlockSpec(shape, lambda *_: (0,) * len(shape))


def call(kernel, outs, scratch, name, in_specs, out_specs=None, steps=(1,)):
    return pl.pallas_call(
        kernel,
        name=name,
        grid=steps,
        in_specs=in_specs,
        out_specs=out_specs or [whole(o.shape) for o in outs],
        out_shape=outs,
        scratch_shapes=scratch,
        cost_estimate=pl.CostEstimate(flops=0, transcendentals=0, bytes_accessed=0),
        compiler_params=pltpu.CompilerParams(vmem_limit_bytes=VMEM_LIMIT),
    )


def struct(shape, dtype):
    return jax.ShapeDtypeStruct(shape, dtype)


def face_flux(here, following, speed_here, speed_following):
    total = speed_here + speed_following
    return jnp.minimum(total, 0.0) * here + jnp.maximum(total, 0.0) * following


def depth_change(p, vz):
    nz = p.shape[1]
    lanes = lax.broadcasted_iota(jnp.int32, p.shape, 1)
    p_up = jnp.where(lanes == nz - 1, 0.0, pltpu.roll(p, nz - 1, 1))
    v_up = jnp.where(lanes == nz - 1, 0.0, pltpu.roll(vz, nz - 1, 1))
    upper = face_flux(p, p_up, vz, v_up)
    lower = jnp.where(lanes == 0, jnp.maximum(vz, 0.0) * p, pltpu.roll(upper, 1, 1))
    return upper - lower


def plane_change(p, vy, vz, below, above):
    ny = p.shape[0]
    rows = lax.broadcasted_iota(jnp.int32, p.shape, 0)
    p_up = jnp.where(rows == ny - 1, above[0], pltpu.roll(p, ny - 1, 0))
    v_up = jnp.where(rows == ny - 1, above[1], pltpu.roll(vy, ny - 1, 0))
    upper = face_flux(p, p_up, vy, v_up)
    first = face_flux(below[0], p[0:1], below[1], vy[0:1])
    lower = jnp.where(rows == 0, first, pltpu.roll(upper, 1, 0))
    return (upper - lower) + depth_change(p, vz)


NEAR_P, FAR_P, NEAR_N, FAR_N, NEAR_T, NEAR_Z, NEAR_EARLY = range(7)


def column_kernel(p_any, v_any, low, high, p_lo, p_hi, v_lo, v_hi, sem):
    nx = p_any.shape[0]
    copies = []
    for at, (p, v, x) in enumerate(((p_lo, v_lo, 0), (p_hi, v_hi, nx - 2))):
        copies.append(pltpu.make_async_copy(p_any.at[pl.ds(x, 2)], p, sem.at[2 * at]))
        copies.append(pltpu.make_async_copy(v_any.at[:, :, pl.ds(x, 2)], v, sem.at[2 * at + 1]))
    for copy in copies:
        copy.start()
    for copy in copies:
        copy.wait()
    for msg, p, v, near, far in ((low, p_lo, v_lo, 0, 1), (high, p_hi, v_hi, 1, 0)):
        msg[NEAR_P] = p[near].astype(BF16)
        msg[FAR_P] = p[far].astype(BF16)
        msg[NEAR_N] = v[1, 0, near]
        msg[FAR_N] = v[1, 0, far]
        msg[NEAR_T] = v[1, 1, near]
        msg[NEAR_Z] = v[1, 2, near]
        msg[NEAR_EARLY] = v[0, 0, near]


def column_messages(field, velocity):
    nx, ny, nz = field.shape
    outs = [struct((7, ny, nz), BF16)] * 2
    scratch = [pltpu.VMEM((2, ny, nz), F32)] * 2
    scratch += [pltpu.VMEM((2, 3, 2, ny, nz), BF16)] * 2 + [pltpu.SemaphoreType.DMA((4,))]
    in_specs = [pl.BlockSpec(memory_space=pltpu.HBM)] * 2
    return call(column_kernel, outs, scratch, "columns", in_specs)(field, velocity)


def rows_kernel(p_ref, v_ref, hxl, hxh, code, lo, hi, s_lo, s_hi):
    nx, ny, _ = p_ref.shape
    s_lo[...] = jnp.zeros(s_lo.shape, F32)
    s_hi[...] = jnp.zeros(s_hi.shape, F32)

    def put(layer, x, cells, width):
        at = pl.ds(x + 1, 1)
        for d in range(width):
            s_lo[layer + d, at, :] = cells[d : d + 1]
            s_hi[layer + d, at, :] = cells[ny - 1 - d : ny - d]

    def step(x, carry):
        put(NEAR_P, x, p_ref[x], 2)
        put(NEAR_N, x, v_ref[1, 1, x].astype(F32), 2)
        put(NEAR_T, x, v_ref[1, 0, x].astype(F32), 1)
        put(NEAR_Z, x, v_ref[1, 2, x].astype(F32), 1)
        put(NEAR_EARLY, x, v_ref[0, 1, x].astype(F32), 1)
        return carry

    lax.fori_loop(0, nx, step, 0)
    for x, halo in ((-1, hxl), (nx, hxh)):
        put(NEAR_P, x, halo[NEAR_P].astype(F32), 1)
        put(NEAR_N, x, halo[NEAR_T].astype(F32), 1)
        put(NEAR_T, x, halo[NEAR_N].astype(F32), 1)
    s_lo[FAR_P, 0:1, :] = code[...]
    s_hi[FAR_P, 0:1, :] = code[...]
    lo[...] = s_lo[...].astype(BF16)
    hi[...] = s_hi[...].astype(BF16)


def upwind_one_kernel(
    inside, p_ref, v_ref, hxl, hxh, hyl, hyh, out, oxl, oxh, oyl, oyh,
    s_yl, s_yh, s_p0, s_p1, s_v0, s_v1,
):
    nx, ny, nz = p_ref.shape
    s_yl[...] = hyl[...].astype(F32)
    s_yh[...] = hyh[...].astype(F32)

    def plane(x, flux_below, p, speeds, p_next, vx_next):
        vx, vy, vz = speeds
        flux_above = face_flux(p, p_next, vx, vx_next)
        at = pl.ds(x + 1, 1)
        below = s_yl[NEAR_P, at, :], s_yl[NEAR_N, at, :]
        above = s_yh[NEAR_P, at, :], s_yh[NEAR_N, at, :]
        change = (flux_above - flux_below) + plane_change(p, vy, vz, below, above)
        return p + 0.5 * change, flux_above

    def speed(c, x):
        return v_ref[0, c, x].astype(F32)

    def halo_plane(halo):
        return [halo[i].astype(F32) for i in (NEAR_P, FAR_P, NEAR_N, FAR_N, NEAR_T, NEAR_Z)]

    p, p_far, vx, vx_far, vy, vz = halo_plane(hxl)
    flux = face_flux(p_far, p, vx_far, vx)
    got, flux = plane(-1, flux, p, (vx, vy, vz), p_ref[0], speed(0, 0))
    oxl[...] = got * inside[0]
    p_high, p_far, vx_high, vx_far, vy_high, vz_high = halo_plane(hxh)

    def inner(x, flux, p_next, vx_next):
        p = p_ref[x]
        vy = speed(1, x)
        got, flux = plane(x, flux, p, (speed(0, x), vy, speed(2, x)), p_next, vx_next)
        out[x] = got
        at = pl.ds(x, 1)
        s_p0[at, :] = p[0:1]
        s_p1[at, :] = p[ny - 1 : ny]
        s_v0[at, :] = vy[0:1]
        s_v1[at, :] = vy[ny - 1 : ny]
        return flux

    def inner_step(x, f):
        return inner(x, f, p_ref[x + 1], speed(0, x + 1))

    flux = lax.fori_loop(0, nx - 2, inner_step, flux, unroll=5)
    flux = inner_step(nx - 2, flux)
    flux = inner(nx - 1, flux, p_high, vx_high)
    got, _ = plane(nx, flux, p_high, (vx_high, vy_high, vz_high), p_far, vx_far)
    oxh[...] = got * inside[1]

    for scr, edge_p, edge_v, dest, flag, sign in (
        (s_yl, s_p0, s_v0, oyl, inside[2], 1.0),
        (s_yh, s_p1, s_v1, oyh, inside[3], -1.0),
    ):
        mid = slice(1, nx + 1)
        p, vy = scr[NEAR_P, mid, :], scr[NEAR_N, mid, :]
        flux_x = face_flux(
            scr[NEAR_P, 0 : nx + 1, :], scr[NEAR_P, 1 : nx + 2, :],
            scr[NEAR_T, 0 : nx + 1, :], scr[NEAR_T, 1 : nx + 2, :],
        )
        change = flux_x[1:] - flux_x[:-1]
        far = (scr[FAR_P, mid, :], scr[FAR_N, mid, :])
        near = (edge_p[...], edge_v[...])
        before, following = (far, near) if sign > 0 else (near, far)
        change = change + (
            face_flux(p, following[0], vy, following[1]) - face_flux(before[0], p, before[1], vy)
        )
        change = change + depth_change(p, scr[NEAR_Z, mid, :])
        dest[...] = (p + 0.5 * change) * flag


def upwind_zero_kernel(
    p_ref, v_ref, pxl, pxh, pyl, pyh, hxl, hxh, hyl, hyh, out, fxl, fxh, fyl, fyh,
    s_vl, s_vh, s_fl, s_fh,
):
    nx, ny, nz = p_ref.shape
    s_vl[...] = hyl[NEAR_EARLY].astype(F32)
    s_vh[...] = hyh[NEAR_EARLY].astype(F32)

    def speed(c, x):
        return v_ref[0, c, x].astype(F32)

    def plane(x, flux_below, p_next, vx_next):
        p = p_ref[x]
        flux_above = face_flux(p, p_next, speed(0, x), vx_next)
        at, halo_at = pl.ds(x, 1), pl.ds(x + 1, 1)
        below = pyl[at, :], s_vl[halo_at, :]
        above = pyh[at, :], s_vh[halo_at, :]
        change = (flux_above - flux_below) + plane_change(p, speed(1, x), speed(2, x), below, above)
        got = p + 0.5 * change
        out[x] = got
        s_fl[at, :] = got[0:1]
        s_fh[at, :] = got[ny - 1 : ny]
        return flux_above

    flux = face_flux(pxl[...], p_ref[0], hxl[NEAR_EARLY].astype(F32), speed(0, 0))
    def plane_step(x, f):
        return plane(x, f, p_ref[x + 1], speed(0, x + 1))

    flux = lax.fori_loop(0, nx - 2, plane_step, flux, unroll=5)
    flux = plane_step(nx - 2, flux)
    plane(nx - 1, flux, pxh[...], hxh[NEAR_EARLY].astype(F32))
    fxl[0] = out[0].astype(BF16)
    fxh[0] = out[nx - 1].astype(BF16)
    fyl[0] = s_fl[...].astype(BF16)
    fyh[0] = s_fh[...].astype(BF16)


def speeds_spec(velocity, instant):
    block = (1,) + velocity.shape[1:]
    return pl.BlockSpec(block, lambda *_: (instant,) + (0,) * (len(block) - 1))


def upwind_one(inside, field, velocity, halo):
    nx, ny, nz = field.shape
    line = struct((ny, nz), F32)
    in_specs = [pl.BlockSpec(memory_space=pltpu.SMEM), whole(field.shape), speeds_spec(velocity, 1)]
    in_specs += [whole(h.shape) for h in halo]
    scratch = [pltpu.VMEM(halo[2].shape, F32)] * 2 + [pltpu.VMEM((nx, nz), F32)] * 4
    outs = [struct(field.shape, F32)] + [line] * 4
    return call(upwind_one_kernel, outs, scratch, "upwind_one", in_specs)(inside, field, velocity, *halo)


def upwind_zero(field, velocity, field_halo, halo):
    nx, ny, nz = field.shape
    in_specs = [whole(field.shape), speeds_spec(velocity, 0)]
    in_specs += [whole(h.shape) for h in (*field_halo, *halo)]
    scratch = [pltpu.VMEM((nx + 2, nz), F32)] * 2 + [pltpu.VMEM((nx, nz), F32)] * 2
    outs = [struct(field.shape, F32)] + [struct((1, ny, nz), BF16)] * 4
    return call(upwind_zero_kernel, outs, scratch, "upwind_zero", in_specs)(
        field, velocity, *field_halo, *halo
    )


def choice_kernel(edge, blocks, left, right, own, send, keep):
    _, height, width = keep.shape
    nz = own.shape[1]
    lane = lax.broadcasted_iota(jnp.int32, (nz, width), 1)
    slot = lax.broadcasted_iota(jnp.int32, (nz, width), 0)
    spread = jnp.where(lane // edge == slot, 1.0, 0.0).astype(BF16)
    row = lax.broadcasted_iota(jnp.int32, (height, width), 0)
    within = lax.broadcasted_iota(jnp.int32, (8, width), 1) % edge
    codes = (left[FAR_P, 0:1, :].astype(F32), right[FAR_P, 0:1, :].astype(F32), own[...])
    for code, side, out, d in zip(codes, (2, 0, 1), (send, send, keep), (0, 1, 0)):
        code = jnp.broadcast_to(code, (8, nz)).astype(BF16)
        code = jnp.dot(code, spread, preferred_element_type=F32).astype(jnp.int32)
        start = (code - side * blocks) * edge
        good = (start >= 0) & (start < height)
        wanted = jnp.where(good, start + within, -1)[0:1]
        out[d] = jnp.where(row == wanted, 1.0, 0.0).astype(BF16)


def choices(left, right, own, edge, slots):
    nz = own.shape[1]
    outs = [struct((count, 3 * nz, slots * edge), BF16) for count in (2, 1)]
    kernel = functools.partial(choice_kernel, edge, 3 * nz // edge)
    in_specs = [whole(a.shape) for a in (left, right, own)]
    return call(kernel, outs, [], "choices", in_specs)(left, right, own)


def planes_of(ref, planes):
    ny, width = ref.shape[1:]
    parts = [ref[a:b].reshape((b - a) * ny, width) for a, b in planes]
    return parts[0] if len(parts) == 1 else jnp.concatenate(parts, axis=0)


def pick_kernel(planes, t_lo, t_own, t_hi, q_ref, *outs):
    ny, nz = t_own.shape[1:]
    rows = jnp.concatenate([planes_of(ref, planes) for ref in (t_lo, t_own, t_hi)], axis=1)
    count = rows.shape[0] // ny
    for d, out in enumerate(outs):
        got = jnp.dot(rows, q_ref[d], preferred_element_type=F32).astype(BF16)
        out[0:count] = got[:, :nz].reshape(count, ny, nz)
        out[count : 2 * count] = got[:, nz:].reshape(count, ny, nz)


def pick(columns, choices, planes, name):
    _, ny, nz = columns[1].shape
    count = 2 * sum(b - a for a, b in planes)
    outs = [struct((count, ny, nz), BF16)] * choices.shape[0]
    ins = (*columns, choices)
    in_specs = [whole(a.shape) for a in ins]
    return call(functools.partial(pick_kernel, planes), outs, [], name, in_specs)(*ins)


def outer_kernel(nx, count, own, la, ra, face_lo, face_hi, low, high):
    for k in range(2):
        for c in range(2):
            x, a = k * nx + c, k * count + c
            low[2 * k + c] = own[x] + la[a] + ra[a]
            x, a = (k + 1) * nx - 2 + c, (k + 1) * count - 2 + c
            high[2 * k + c] = own[x] + la[a] + ra[a]
    low[4] = face_lo[0]
    high[4] = face_hi[0]


def each_plane(groups, images, k, visit):
    own, la, ra, lb, rb = images
    nx = sum(b - a for planes in groups for a, b in planes)
    for planes, lefts, rights in ((groups[0], la, ra), (groups[1], lb, rb)):
        at = k * sum(b - a for a, b in planes)
        for a, b in planes:

            def step(x, carry, shift=at - a, lefts=lefts, rights=rights):
                visit(x, own[k * nx + x] + lefts[x + shift] + rights[x + shift])
                return carry

            lax.fori_loop(a, b, step, 0, unroll=8)
            at += b - a


def edge_kernel(
    groups, own, la, ra, lb, rb, xlo, xhi, face_lo, face_hi, first, final, s_first, s_final
):
    nx, (ny, nz) = own.shape[0] // 2, own.shape[1:]
    for k in range(2):

        def put(x, cells, k=k):
            at = pl.ds(x + 1, 1)
            cells = cells.astype(F32)
            for c in range(2):
                s_first[2 * k + c, at, :] = cells[c : c + 1]
                s_final[2 * k + c, at, :] = cells[ny - 2 + c : ny - 1 + c]

        put(-1, xlo[2 * k + 1])
        put(nx, xhi[2 * k])
        each_plane(groups, (own, la, ra, lb, rb), k, put)
    for faces, scr, msg in ((face_lo, s_first, first), (face_hi, s_final, final)):
        msg[0:4] = scr[...].astype(BF16)
        msg[4] = jnp.zeros(msg.shape[1:], BF16)
        msg[4, 0:nx] = faces[0]


def force_kernel(
    groups, own, la, ra, lb, rb, band, xlo, xhi, ylo, yhi, adj0, adj1, bxl, bxh, byl, byh, vel,
    out, img, packed, frc, s_ylo, s_yhi, s_c0, s_c1, s_fl, s_fh, s_al, s_ah,
):
    k = pl.program_id(0)
    chunk = pl.program_id(1)
    deep = out.shape[2]
    nx, ny, nz = adj0.shape
    rows = lax.broadcasted_iota(jnp.int32, (ny, nz), 0)
    lanes = lax.broadcasted_iota(jnp.int32, (ny, nz), 1)
    first_image = k == 0

    def this(zero, one):
        return jnp.where(first_image, zero.astype(F32), one.astype(F32))

    def along_z(cells, index, length):
        following = jnp.where(index == length - 1, 0.0, pltpu.roll(cells, length - 1, 1))
        before = jnp.where(index == 0, 0.0, pltpu.roll(cells, 1, 1))
        return following, before

    @pl.when(chunk == 0)
    def _():
        for h in range(2):
            img[h] = xlo[2 * k + h].astype(F32)
            img[nx + 2 + h] = xhi[2 * k + h].astype(F32)

        def fill(x, cells):
            packed[x] = cells
            cells = cells.astype(F32)
            img[x + 2] = cells
            s_c0[pl.ds(x, 1), :] = cells[0:1]
            s_c1[pl.ds(x, 1), :] = cells[ny - 1 : ny]

        each_plane(groups, (own, la, ra, lb, rb), 0, fill)
        every = packed[...].reshape(nx * ny, nz)
        frc[2, 1 : nx + 1] = jnp.dot(every, band[...], preferred_element_type=F32).reshape(nx, ny, nz)
        for h in range(2):
            s_ylo[h] = ylo[2 * k + h].astype(F32)
            s_yhi[h] = yhi[2 * k + h].astype(F32)
        s_al[...] = this(ylo[4, 0:nx], byl[...])
        s_ah[...] = this(yhi[4, 0:nx], byh[...])

        def forces(x, half, slope_z):
            cells = img[x + 2]
            at = pl.ds(x + 1, 1)
            frc[0, x + 1] = half * (img[x + 3] - img[x + 1])
            up = jnp.where(rows == ny - 1, s_yhi[0, at, :], pltpu.roll(cells, ny - 1, 0))
            down = jnp.where(rows == 0, s_ylo[1, at, :], pltpu.roll(cells, 1, 0))
            frc[1, x + 1] = half * (up - down)
            frc[2, x + 1] = half * slope_z

        for x, half in ((-1, 0.5 * this(xlo[4], bxl[...])), (nx, 0.5 * this(xhi[4], bxh[...]))):
            following, before = along_z(img[x + 2], lanes, nz)
            forces(x, half, following - before)

        def force_step(x, carry):
            forces(x, 0.5 * this(adj0[x], adj1[x]), frc[2, x + 1])
            return carry

        lax.fori_loop(0, nx, force_step, 0, unroll=8)
        lines = lax.broadcasted_iota(jnp.int32, (nx, nz), 1)
        for cols, near, far, beside, half, dest, sign in (
            (s_ylo, 1, 0, s_c0, s_al, s_fl, 1.0),
            (s_yhi, 0, 1, s_c1, s_ah, s_fh, -1.0),
        ):
            weight = 0.5 * half[...]
            dest[0] = weight * (cols[near, 2 : nx + 2, :] - cols[near, 0:nx, :])
            dest[1] = (sign * weight) * (beside[...] - cols[far, 1 : nx + 1, :])
            following, before = along_z(cols[near, 1 : nx + 1, :], lines, nz)
            dest[2] = weight * (following - before)

    def smooth_step(i, carry):
        x = chunk * deep + i
        at = pl.ds(x, 1)
        for c in range(3):
            f = frc[c, x + 1]
            up = jnp.where(rows == ny - 1, s_fh[c, at, :], pltpu.roll(f, ny - 1, 0))
            down = jnp.where(rows == 0, s_fl[c, at, :], pltpu.roll(f, 1, 0))
            following, before = along_z(f, lanes, nz)
            beside = (frc[c, x] + frc[c, x + 2]) + (up + down) + (following + before)
            out[0, c, i] = vel[0, c, i].astype(F32) + (0.25 * f + 0.125 * beside)
        return carry

    lax.fori_loop(0, deep, smooth_step, 0, unroll=8)


def force(groups, images, band, x_lo, x_hi, y_lo, y_hi, adj_zero, adj_one, halo_one, velocity):
    nx, ny, nz = adj_zero.shape
    deep = nx // 2
    block = pl.BlockSpec((1, 3, deep, ny, nz), lambda k, i: (k, 0, i, 0, 0))
    middle = [band, x_lo, x_hi, y_lo, y_hi, adj_zero, adj_one, *halo_one]
    counts = [nx] + [sum(b - a for a, b in planes) for planes in groups for _ in range(2)]
    in_specs = [pl.BlockSpec((count, ny, nz), lambda k, i: (k, 0, 0)) for count in counts]
    in_specs += [whole(a.shape) for a in middle] + [block]
    scratch = [
        pltpu.VMEM((nx + 4, ny, nz), F32),
        pltpu.VMEM((nx, ny, nz), BF16),
        pltpu.VMEM((3, nx + 2, ny, nz), F32),
        pltpu.VMEM((2, nx + 2, nz), F32),
        pltpu.VMEM((2, nx + 2, nz), F32),
        pltpu.VMEM((nx, nz), F32),
        pltpu.VMEM((nx, nz), F32),
        pltpu.VMEM((3, nx, nz), F32),
        pltpu.VMEM((3, nx, nz), F32),
        pltpu.VMEM((nx, nz), F32),
        pltpu.VMEM((nx, nz), F32),
    ]
    return call(
        functools.partial(force_kernel, groups),
        struct((2, 3, nx, ny, nz), F32),
        scratch,
        "force",
        in_specs,
        block,
        (2, 2),
    )(*images, *middle, velocity)


def forward(value, axis):
    ends = lax.axis_size(axis) - 1
    return lax.ppermute(value, axis, [(i, i + 1) for i in range(ends)])


def backward(value, axis):
    ends = lax.axis_size(axis) - 1
    return lax.ppermute(value, axis, [(i + 1, i) for i in range(ends)])


def body(template, mismatch, velocity, src_ids):
    nx, ny, nz = template.shape
    depth_blocks = src_ids.shape[3]
    edge = nz // depth_blocks
    slots = 2 * depth_blocks
    index_first = lax.axis_index("gx")
    index_second = lax.axis_index("gy")
    count_first = lax.axis_size("gx")
    count_second = lax.axis_size("gy")

    low, high = column_messages(
        pltpu.with_memory_space_constraint(mismatch, pltpu.HBM),
        pltpu.with_memory_space_constraint(velocity, pltpu.HBM),
    )
    halo_xl = forward(high, "gx")
    halo_xh = backward(low, "gx")
    late_template, _ = lax.optimization_barrier((template, low))
    t_lo = forward(late_template, "gx")
    t_hi = backward(late_template, "gx")

    ids = src_ids.reshape(slots)
    first_block = ids // (count_second * depth_blocks)
    second_block = ids // depth_blocks % count_second
    start = (first_block - index_first + 1) * depth_blocks + ids % depth_blocks
    side = second_block - index_second + 1
    code = (side * (3 * depth_blocks) + start).astype(F32)
    code = jnp.pad(code.reshape(1, slots), ((0, 0), (0, nz - slots)))
    ins = (mismatch, velocity, halo_xl, halo_xh, code)
    rows = struct((7, nx + 2, nz), BF16)
    low, high = call(
        rows_kernel,
        [rows] * 2,
        [pltpu.VMEM(rows.shape, F32)] * 2,
        "rows",
        [whole(a.shape) for a in ins],
    )(*ins)
    halo_yl = forward(high, "gy")
    halo_yh = backward(low, "gy")
    halo = (halo_xl, halo_xh, halo_yl, halo_yh)
    inside = jnp.stack(
        [index_first > 0, index_first < count_first - 1, index_second > 0, index_second < count_second - 1]
    ).astype(F32)

    send_choice, own_choice = choices(halo_yl, halo_yh, code, edge, slots)
    z = jnp.arange(nz)
    band = (z[:, None] == z[None] + 1).astype(BF16) - (z[:, None] == z[None] - 1).astype(BF16)

    columns = (t_lo, template, t_hi)
    half = nx // 4
    groups = (((0, half), (nx - half, nx)), ((half, nx - half),))
    to_left_a, to_right_a = pick(columns, send_choice, groups[0], "pick_outer")
    from_left_a = forward(to_right_a, "gy")
    from_right_a = backward(to_left_a, "gy")
    columns, _ = lax.optimization_barrier((columns, to_left_a))
    to_left_b, to_right_b = pick(columns, send_choice, groups[1], "pick_inner")
    from_left_b = forward(to_right_b, "gy")
    from_right_b = backward(to_left_b, "gy")
    late_choice, late_mismatch, _ = lax.optimization_barrier((own_choice, mismatch, to_left_b))
    adj_one, *halo_one = upwind_one(inside, late_mismatch, velocity, halo)
    adj_zero, low_x, high_x, low_y, high_y = upwind_zero(adj_one, velocity, halo_one, halo)
    (own,) = pick(columns, late_choice, ((0, nx),), "pick_own")

    ins = (own, from_left_a, from_right_a, low_x, high_x)
    low, high = call(
        functools.partial(outer_kernel, nx, 2 * half),
        [struct((5, ny, nz), BF16)] * 2, [], "outer", [whole(a.shape) for a in ins]
    )(*ins)
    x_lo = forward(high, "gx")
    x_hi = backward(low, "gx")

    images = (own, from_left_a, from_right_a, from_left_b, from_right_b)
    ins = (*images, x_lo, x_hi, low_y, high_y)
    first, final = call(
        functools.partial(edge_kernel, groups),
        [struct((5, nx + 2, nz), BF16)] * 2,
        [pltpu.VMEM((4, nx + 2, nz), F32)] * 2,
        "edges",
        [whole(a.shape) for a in ins],
    )(*ins)
    y_lo = forward(final, "gy")
    y_hi = backward(first, "gy")
    return force(
        groups, images, band, x_lo, x_hi, y_lo, y_hi, adj_zero, adj_one, halo_one, velocity
    )


def solution(mesh):
    in_specs = (
        P("gx", "gy", None),
        P("gx", "gy", None),
        P(None, None, "gx", "gy", None),
        P(None, "gx", "gy", None),
    )
    out_specs = P(None, None, "gx", "gy", None)
    return jax.shard_map(body, mesh=mesh, in_specs=in_specs, out_specs=out_specs, check_vma=False)
```

```python
import functools

import jax
import jax.numpy as jnp
from jax import lax
from jax.experimental import pallas as pl
from jax.experimental.pallas import tpu as pltpu
from jax.sharding import PartitionSpec as P

F32 = jnp.float32
BF16 = jnp.bfloat16
VMEM_LIMIT = 48 << 20


def whole(shape):
    return pl.BlockSpec(shape, lambda *_: (0,) * len(shape))


def call(kernel, outs, scratch, name, in_specs, out_specs=None, steps=(1,)):
    return pl.pallas_call(
        kernel,
        name=name,
        grid=steps,
        in_specs=in_specs,
        out_specs=out_specs or [whole(o.shape) for o in outs],
        out_shape=outs,
        scratch_shapes=scratch,
        cost_estimate=pl.CostEstimate(flops=0, transcendentals=0, bytes_accessed=0),
        compiler_params=pltpu.CompilerParams(vmem_limit_bytes=VMEM_LIMIT),
    )


def struct(shape, dtype):
    return jax.ShapeDtypeStruct(shape, dtype)


def face_flux(here, following, speed_here, speed_following):
    total = speed_here + speed_following
    return jnp.minimum(total, 0.0) * here + jnp.maximum(total, 0.0) * following


def depth_change(p, vz):
    nz = p.shape[1]
    lanes = lax.broadcasted_iota(jnp.int32, p.shape, 1)
    p_up = jnp.where(lanes == nz - 1, 0.0, pltpu.roll(p, nz - 1, 1))
    v_up = jnp.where(lanes == nz - 1, 0.0, pltpu.roll(vz, nz - 1, 1))
    upper = face_flux(p, p_up, vz, v_up)
    lower = jnp.where(lanes == 0, jnp.maximum(vz, 0.0) * p, pltpu.roll(upper, 1, 1))
    return upper - lower


def plane_change(p, vy, vz, below, above):
    ny = p.shape[0]
    rows = lax.broadcasted_iota(jnp.int32, p.shape, 0)
    p_up = jnp.where(rows == ny - 1, above[0], pltpu.roll(p, ny - 1, 0))
    v_up = jnp.where(rows == ny - 1, above[1], pltpu.roll(vy, ny - 1, 0))
    upper = face_flux(p, p_up, vy, v_up)
    first = face_flux(below[0], p[0:1], below[1], vy[0:1])
    lower = jnp.where(rows == 0, first, pltpu.roll(upper, 1, 0))
    return (upper - lower) + depth_change(p, vz)


NEAR_P, FAR_P, NEAR_N, FAR_N, NEAR_T, NEAR_Z, NEAR_EARLY = range(7)


def column_kernel(p_any, v_any, low, high, p_lo, p_hi, v_lo, v_hi, sem):
    nx = p_any.shape[0]
    copies = []
    for at, (p, v, x) in enumerate(((p_lo, v_lo, 0), (p_hi, v_hi, nx - 2))):
        copies.append(pltpu.make_async_copy(p_any.at[pl.ds(x, 2)], p, sem.at[2 * at]))
        copies.append(pltpu.make_async_copy(v_any.at[:, :, pl.ds(x, 2)], v, sem.at[2 * at + 1]))
    for copy in copies:
        copy.start()
    for copy in copies:
        copy.wait()
    for msg, p, v, near, far in ((low, p_lo, v_lo, 0, 1), (high, p_hi, v_hi, 1, 0)):
        msg[NEAR_P] = p[near].astype(BF16)
        msg[FAR_P] = p[far].astype(BF16)
        msg[NEAR_N] = v[1, 0, near]
        msg[FAR_N] = v[1, 0, far]
        msg[NEAR_T] = v[1, 1, near]
        msg[NEAR_Z] = v[1, 2, near]
        msg[NEAR_EARLY] = v[0, 0, near]


def column_messages(field, velocity):
    nx, ny, nz = field.shape
    outs = [struct((7, ny, nz), BF16)] * 2
    scratch = [pltpu.VMEM((2, ny, nz), F32)] * 2
    scratch += [pltpu.VMEM((2, 3, 2, ny, nz), BF16)] * 2 + [pltpu.SemaphoreType.DMA((4,))]
    in_specs = [pl.BlockSpec(memory_space=pltpu.HBM)] * 2
    return call(column_kernel, outs, scratch, "columns", in_specs)(field, velocity)


def rows_kernel(p_ref, v_ref, hxl, hxh, code, lo, hi, s_lo, s_hi):
    nx, ny, _ = p_ref.shape
    s_lo[...] = jnp.zeros(s_lo.shape, F32)
    s_hi[...] = jnp.zeros(s_hi.shape, F32)

    def put(layer, x, cells, width):
        at = pl.ds(x + 1, 1)
        for d in range(width):
            s_lo[layer + d, at, :] = cells[d : d + 1]
            s_hi[layer + d, at, :] = cells[ny - 1 - d : ny - d]

    def step(x, carry):
        put(NEAR_P, x, p_ref[x], 2)
        put(NEAR_N, x, v_ref[1, 1, x].astype(F32), 2)
        put(NEAR_T, x, v_ref[1, 0, x].astype(F32), 1)
        put(NEAR_Z, x, v_ref[1, 2, x].astype(F32), 1)
        put(NEAR_EARLY, x, v_ref[0, 1, x].astype(F32), 1)
        return carry

    lax.fori_loop(0, nx, step, 0)
    for x, halo in ((-1, hxl), (nx, hxh)):
        put(NEAR_P, x, halo[NEAR_P].astype(F32), 1)
        put(NEAR_N, x, halo[NEAR_T].astype(F32), 1)
        put(NEAR_T, x, halo[NEAR_N].astype(F32), 1)
    s_lo[FAR_P, 0:1, :] = code[...]
    s_hi[FAR_P, 0:1, :] = code[...]
    lo[...] = s_lo[...].astype(BF16)
    hi[...] = s_hi[...].astype(BF16)


def upwind_one_kernel(
    inside, p_ref, v_ref, hxl, hxh, hyl, hyh, out, oxl, oxh, oyl, oyh,
    s_yl, s_yh, s_p0, s_p1, s_v0, s_v1,
):
    nx, ny, nz = p_ref.shape
    s_yl[...] = hyl[...].astype(F32)
    s_yh[...] = hyh[...].astype(F32)

    def plane(x, flux_below, p, speeds, p_next, vx_next):
        vx, vy, vz = speeds
        flux_above = face_flux(p, p_next, vx, vx_next)
        at = pl.ds(x + 1, 1)
        below = s_yl[NEAR_P, at, :], s_yl[NEAR_N, at, :]
        above = s_yh[NEAR_P, at, :], s_yh[NEAR_N, at, :]
        change = (flux_above - flux_below) + plane_change(p, vy, vz, below, above)
        return p + 0.5 * change, flux_above

    def speed(c, x):
        return v_ref[0, c, x].astype(F32)

    def halo_plane(halo):
        return [halo[i].astype(F32) for i in (NEAR_P, FAR_P, NEAR_N, FAR_N, NEAR_T, NEAR_Z)]

    p, p_far, vx, vx_far, vy, vz = halo_plane(hxl)
    flux = face_flux(p_far, p, vx_far, vx)
    got, flux = plane(-1, flux, p, (vx, vy, vz), p_ref[0], speed(0, 0))
    oxl[...] = got * inside[0]
    p_high, p_far, vx_high, vx_far, vy_high, vz_high = halo_plane(hxh)

    def inner(x, flux, p_next, vx_next):
        p = p_ref[x]
        vy = speed(1, x)
        got, flux = plane(x, flux, p, (speed(0, x), vy, speed(2, x)), p_next, vx_next)
        out[x] = got
        at = pl.ds(x, 1)
        s_p0[at, :] = p[0:1]
        s_p1[at, :] = p[ny - 1 : ny]
        s_v0[at, :] = vy[0:1]
        s_v1[at, :] = vy[ny - 1 : ny]
        return flux

    def inner_step(x, f):
        return inner(x, f, p_ref[x + 1], speed(0, x + 1))

    flux = lax.fori_loop(0, nx - 2, inner_step, flux, unroll=5)
    flux = inner_step(nx - 2, flux)
    flux = inner(nx - 1, flux, p_high, vx_high)
    got, _ = plane(nx, flux, p_high, (vx_high, vy_high, vz_high), p_far, vx_far)
    oxh[...] = got * inside[1]

    for scr, edge_p, edge_v, dest, flag, sign in (
        (s_yl, s_p0, s_v0, oyl, inside[2], 1.0),
        (s_yh, s_p1, s_v1, oyh, inside[3], -1.0),
    ):
        mid = slice(1, nx + 1)
        p, vy = scr[NEAR_P, mid, :], scr[NEAR_N, mid, :]
        flux_x = face_flux(
            scr[NEAR_P, 0 : nx + 1, :], scr[NEAR_P, 1 : nx + 2, :],
            scr[NEAR_T, 0 : nx + 1, :], scr[NEAR_T, 1 : nx + 2, :],
        )
        change = flux_x[1:] - flux_x[:-1]
        far = (scr[FAR_P, mid, :], scr[FAR_N, mid, :])
        near = (edge_p[...], edge_v[...])
        before, following = (far, near) if sign > 0 else (near, far)
        change = change + (
            face_flux(p, following[0], vy, following[1]) - face_flux(before[0], p, before[1], vy)
        )
        change = change + depth_change(p, scr[NEAR_Z, mid, :])
        dest[...] = (p + 0.5 * change) * flag


def upwind_zero_kernel(
    p_ref, v_ref, pxl, pxh, pyl, pyh, hxl, hxh, hyl, hyh, out, fxl, fxh, fyl, fyh,
    s_vl, s_vh, s_fl, s_fh,
):
    nx, ny, nz = p_ref.shape
    s_vl[...] = hyl[NEAR_EARLY].astype(F32)
    s_vh[...] = hyh[NEAR_EARLY].astype(F32)

    def speed(c, x):
        return v_ref[0, c, x].astype(F32)

    def plane(x, flux_below, p_next, vx_next):
        p = p_ref[x]
        flux_above = face_flux(p, p_next, speed(0, x), vx_next)
        at, halo_at = pl.ds(x, 1), pl.ds(x + 1, 1)
        below = pyl[at, :], s_vl[halo_at, :]
        above = pyh[at, :], s_vh[halo_at, :]
        change = (flux_above - flux_below) + plane_change(p, speed(1, x), speed(2, x), below, above)
        got = p + 0.5 * change
        out[x] = got
        s_fl[at, :] = got[0:1]
        s_fh[at, :] = got[ny - 1 : ny]
        return flux_above

    flux = face_flux(pxl[...], p_ref[0], hxl[NEAR_EARLY].astype(F32), speed(0, 0))
    def plane_step(x, f):
        return plane(x, f, p_ref[x + 1], speed(0, x + 1))

    flux = lax.fori_loop(0, nx - 2, plane_step, flux, unroll=5)
    flux = plane_step(nx - 2, flux)
    plane(nx - 1, flux, pxh[...], hxh[NEAR_EARLY].astype(F32))
    fxl[0] = out[0].astype(BF16)
    fxh[0] = out[nx - 1].astype(BF16)
    fyl[0] = s_fl[...].astype(BF16)
    fyh[0] = s_fh[...].astype(BF16)


def speeds_spec(velocity, instant):
    block = (1,) + velocity.shape[1:]
    return pl.BlockSpec(block, lambda *_: (instant,) + (0,) * (len(block) - 1))


def upwind_one(inside, field, velocity, halo):
    nx, ny, nz = field.shape
    line = struct((ny, nz), F32)
    in_specs = [pl.BlockSpec(memory_space=pltpu.SMEM), whole(field.shape), speeds_spec(velocity, 1)]
    in_specs += [whole(h.shape) for h in halo]
    scratch = [pltpu.VMEM(halo[2].shape, F32)] * 2 + [pltpu.VMEM((nx, nz), F32)] * 4
    outs = [struct(field.shape, F32)] + [line] * 4
    return call(upwind_one_kernel, outs, scratch, "upwind_one", in_specs)(inside, field, velocity, *halo)


def upwind_zero(field, velocity, field_halo, halo):
    nx, ny, nz = field.shape
    in_specs = [whole(field.shape), speeds_spec(velocity, 0)]
    in_specs += [whole(h.shape) for h in (*field_halo, *halo)]
    scratch = [pltpu.VMEM((nx + 2, nz), F32)] * 2 + [pltpu.VMEM((nx, nz), F32)] * 2
    outs = [struct(field.shape, F32)] + [struct((1, ny, nz), BF16)] * 4
    return call(upwind_zero_kernel, outs, scratch, "upwind_zero", in_specs)(
        field, velocity, *field_halo, *halo
    )


def choice_kernel(edge, blocks, left, right, own, send, keep):
    _, height, width = keep.shape
    nz = own.shape[1]
    lane = lax.broadcasted_iota(jnp.int32, (nz, width), 1)
    slot = lax.broadcasted_iota(jnp.int32, (nz, width), 0)
    spread = jnp.where(lane // edge == slot, 1.0, 0.0).astype(BF16)
    row = lax.broadcasted_iota(jnp.int32, (height, width), 0)
    within = lax.broadcasted_iota(jnp.int32, (8, width), 1) % edge
    codes = (left[FAR_P, 0:1, :].astype(F32), right[FAR_P, 0:1, :].astype(F32), own[...])
    for code, side, out, d in zip(codes, (2, 0, 1), (send, send, keep), (0, 1, 0)):
        code = jnp.broadcast_to(code, (8, nz)).astype(BF16)
        code = jnp.dot(code, spread, preferred_element_type=F32).astype(jnp.int32)
        start = (code - side * blocks) * edge
        good = (start >= 0) & (start < height)
        wanted = jnp.where(good, start + within, -1)[0:1]
        out[d] = jnp.where(row == wanted, 1.0, 0.0).astype(BF16)


def choices(left, right, own, edge, slots):
    nz = own.shape[1]
    outs = [struct((count, 3 * nz, slots * edge), BF16) for count in (2, 1)]
    kernel = functools.partial(choice_kernel, edge, 3 * nz // edge)
    in_specs = [whole(a.shape) for a in (left, right, own)]
    return call(kernel, outs, [], "choices", in_specs)(left, right, own)


def planes_of(ref, planes):
    ny, width = ref.shape[1:]
    parts = [ref[a:b].reshape((b - a) * ny, width) for a, b in planes]
    return parts[0] if len(parts) == 1 else jnp.concatenate(parts, axis=0)


def pick_kernel(planes, t_lo, t_own, t_hi, q_ref, *outs):
    ny, nz = t_own.shape[1:]
    rows = jnp.concatenate([planes_of(ref, planes) for ref in (t_lo, t_own, t_hi)], axis=1)
    count = rows.shape[0] // ny
    for d, out in enumerate(outs):
        got = jnp.dot(rows, q_ref[d], preferred_element_type=F32).astype(BF16)
        out[0:count] = got[:, :nz].reshape(count, ny, nz)
        out[count : 2 * count] = got[:, nz:].reshape(count, ny, nz)


def pick(columns, choices, planes, name):
    _, ny, nz = columns[1].shape
    count = 2 * sum(b - a for a, b in planes)
    outs = [struct((count, ny, nz), BF16)] * choices.shape[0]
    ins = (*columns, choices)
    in_specs = [whole(a.shape) for a in ins]
    return call(functools.partial(pick_kernel, planes), outs, [], name, in_specs)(*ins)


def outer_kernel(nx, count, own, la, ra, face_lo, face_hi, low, high):
    for k in range(2):
        for c in range(2):
            x, a = k * nx + c, k * count + c
            low[2 * k + c] = own[x] + la[a] + ra[a]
            x, a = (k + 1) * nx - 2 + c, (k + 1) * count - 2 + c
            high[2 * k + c] = own[x] + la[a] + ra[a]
    low[4] = face_lo[0]
    high[4] = face_hi[0]


def each_plane(groups, images, k, visit):
    own, la, ra, lb, rb = images
    nx = sum(b - a for planes in groups for a, b in planes)
    for planes, lefts, rights in ((groups[0], la, ra), (groups[1], lb, rb)):
        at = k * sum(b - a for a, b in planes)
        for a, b in planes:

            def step(x, carry, shift=at - a, lefts=lefts, rights=rights):
                visit(x, own[k * nx + x] + lefts[x + shift] + rights[x + shift])
                return carry

            lax.fori_loop(a, b, step, 0, unroll=8)
            at += b - a


def edge_kernel(
    groups, own, la, ra, lb, rb, xlo, xhi, face_lo, face_hi, first, final, s_first, s_final
):
    nx, (ny, nz) = own.shape[0] // 2, own.shape[1:]
    for k in range(2):

        def put(x, cells, k=k):
            at = pl.ds(x + 1, 1)
            cells = cells.astype(F32)
            for c in range(2):
                s_first[2 * k + c, at, :] = cells[c : c + 1]
                s_final[2 * k + c, at, :] = cells[ny - 2 + c : ny - 1 + c]

        put(-1, xlo[2 * k + 1])
        put(nx, xhi[2 * k])
        each_plane(groups, (own, la, ra, lb, rb), k, put)
    for faces, scr, msg in ((face_lo, s_first, first), (face_hi, s_final, final)):
        msg[0:4] = scr[...].astype(BF16)
        msg[4] = jnp.zeros(msg.shape[1:], BF16)
        msg[4, 0:nx] = faces[0]


def force_kernel(
    groups, own, la, ra, lb, rb, band, xlo, xhi, ylo, yhi, adj0, adj1, bxl, bxh, byl, byh, vel,
    out, img, packed, frc, s_ylo, s_yhi, s_c0, s_c1, s_fl, s_fh, s_al, s_ah,
):
    k = pl.program_id(0)
    chunk = pl.program_id(1)
    deep = out.shape[2]
    nx, ny, nz = adj0.shape
    rows = lax.broadcasted_iota(jnp.int32, (ny, nz), 0)
    lanes = lax.broadcasted_iota(jnp.int32, (ny, nz), 1)
    first_image = k == 0

    def this(zero, one):
        return jnp.where(first_image, zero.astype(F32), one.astype(F32))

    def along_z(cells, index, length):
        following = jnp.where(index == length - 1, 0.0, pltpu.roll(cells, length - 1, 1))
        before = jnp.where(index == 0, 0.0, pltpu.roll(cells, 1, 1))
        return following, before

    @pl.when(chunk == 0)
    def _():
        for h in range(2):
            img[h] = xlo[2 * k + h].astype(F32)
            img[nx + 2 + h] = xhi[2 * k + h].astype(F32)

        def fill(x, cells):
            packed[x] = cells
            cells = cells.astype(F32)
            img[x + 2] = cells
            s_c0[pl.ds(x, 1), :] = cells[0:1]
            s_c1[pl.ds(x, 1), :] = cells[ny - 1 : ny]

        each_plane(groups, (own, la, ra, lb, rb), 0, fill)
        every = packed[...].reshape(nx * ny, nz)
        frc[2, 1 : nx + 1] = jnp.dot(every, band[...], preferred_element_type=F32).reshape(nx, ny, nz)
        for h in range(2):
            s_ylo[h] = ylo[2 * k + h].astype(F32)
            s_yhi[h] = yhi[2 * k + h].astype(F32)
        s_al[...] = this(ylo[4, 0:nx], byl[...])
        s_ah[...] = this(yhi[4, 0:nx], byh[...])

        def forces(x, half, slope_z):
            cells = img[x + 2]
            at = pl.ds(x + 1, 1)
            frc[0, x + 1] = half * (img[x + 3] - img[x + 1])
            up = jnp.where(rows == ny - 1, s_yhi[0, at, :], pltpu.roll(cells, ny - 1, 0))
            down = jnp.where(rows == 0, s_ylo[1, at, :], pltpu.roll(cells, 1, 0))
            frc[1, x + 1] = half * (up - down)
            frc[2, x + 1] = half * slope_z

        for x, half in ((-1, 0.5 * this(xlo[4], bxl[...])), (nx, 0.5 * this(xhi[4], bxh[...]))):
            following, before = along_z(img[x + 2], lanes, nz)
            forces(x, half, following - before)

        def force_step(x, carry):
            forces(x, 0.5 * this(adj0[x], adj1[x]), frc[2, x + 1])
            return carry

        lax.fori_loop(0, nx, force_step, 0, unroll=8)
        lines = lax.broadcasted_iota(jnp.int32, (nx, nz), 1)
        for cols, near, far, beside, half, dest, sign in (
            (s_ylo, 1, 0, s_c0, s_al, s_fl, 1.0),
            (s_yhi, 0, 1, s_c1, s_ah, s_fh, -1.0),
        ):
            weight = 0.5 * half[...]
            dest[0] = weight * (cols[near, 2 : nx + 2, :] - cols[near, 0:nx, :])
            dest[1] = (sign * weight) * (beside[...] - cols[far, 1 : nx + 1, :])
            following, before = along_z(cols[near, 1 : nx + 1, :], lines, nz)
            dest[2] = weight * (following - before)

    def smooth_step(i, carry):
        x = chunk * deep + i
        at = pl.ds(x, 1)
        for c in range(3):
            f = frc[c, x + 1]
            up = jnp.where(rows == ny - 1, s_fh[c, at, :], pltpu.roll(f, ny - 1, 0))
            down = jnp.where(rows == 0, s_fl[c, at, :], pltpu.roll(f, 1, 0))
            following, before = along_z(f, lanes, nz)
            beside = (frc[c, x] + frc[c, x + 2]) + (up + down) + (following + before)
            out[0, c, i] = vel[0, c, i].astype(F32) + (0.25 * f + 0.125 * beside)
        return carry

    lax.fori_loop(0, deep, smooth_step, 0, unroll=8)


def force(groups, images, band, x_lo, x_hi, y_lo, y_hi, adj_zero, adj_one, halo_one, velocity):
    nx, ny, nz = adj_zero.shape
    deep = nx // 2
    block = pl.BlockSpec((1, 3, deep, ny, nz), lambda k, i: (k, 0, i, 0, 0))
    middle = [band, x_lo, x_hi, y_lo, y_hi, adj_zero, adj_one, *halo_one]
    counts = [nx] + [sum(b - a for a, b in planes) for planes in groups for _ in range(2)]
    in_specs = [pl.BlockSpec((count, ny, nz), lambda k, i: (k, 0, 0)) for count in counts]
    in_specs += [whole(a.shape) for a in middle] + [block]
    scratch = [
        pltpu.VMEM((nx + 4, ny, nz), F32),
        pltpu.VMEM((nx, ny, nz), BF16),
        pltpu.VMEM((3, nx + 2, ny, nz), F32),
        pltpu.VMEM((2, nx + 2, nz), F32),
        pltpu.VMEM((2, nx + 2, nz), F32),
        pltpu.VMEM((nx, nz), F32),
        pltpu.VMEM((nx, nz), F32),
        pltpu.VMEM((3, nx, nz), F32),
        pltpu.VMEM((3, nx, nz), F32),
        pltpu.VMEM((nx, nz), F32),
        pltpu.VMEM((nx, nz), F32),
    ]
    return call(
        functools.partial(force_kernel, groups),
        struct((2, 3, nx, ny, nz), F32),
        scratch,
        "force",
        in_specs,
        block,
        (2, 2),
    )(*images, *middle, velocity)


def forward(value, axis):
    ends = lax.axis_size(axis) - 1
    return lax.ppermute(value, axis, [(i, i + 1) for i in range(ends)])


def backward(value, axis):
    ends = lax.axis_size(axis) - 1
    return lax.ppermute(value, axis, [(i + 1, i) for i in range(ends)])


def body(template, mismatch, velocity, src_ids):
    nx, ny, nz = template.shape
    depth_blocks = src_ids.shape[3]
    edge = nz // depth_blocks
    slots = 2 * depth_blocks
    index_first = lax.axis_index("gx")
    index_second = lax.axis_index("gy")
    count_first = lax.axis_size("gx")
    count_second = lax.axis_size("gy")

    low, high = column_messages(
        pltpu.with_memory_space_constraint(mismatch, pltpu.HBM),
        pltpu.with_memory_space_constraint(velocity, pltpu.HBM),
    )
    halo_xl = forward(high, "gx")
    halo_xh = backward(low, "gx")
    t_lo = forward(template, "gx")
    t_hi = backward(template, "gx")

    ids = src_ids.reshape(slots)
    first_block = ids // (count_second * depth_blocks)
    second_block = ids // depth_blocks % count_second
    start = (first_block - index_first + 1) * depth_blocks + ids % depth_blocks
    side = second_block - index_second + 1
    code = (side * (3 * depth_blocks) + start).astype(F32)
    code = jnp.pad(code.reshape(1, slots), ((0, 0), (0, nz - slots)))
    ins = (mismatch, velocity, halo_xl, halo_xh, code)
    rows = struct((7, nx + 2, nz), BF16)
    low, high = call(
        rows_kernel,
        [rows] * 2,
        [pltpu.VMEM(rows.shape, F32)] * 2,
        "rows",
        [whole(a.shape) for a in ins],
    )(*ins)
    halo_yl = forward(high, "gy")
    halo_yh = backward(low, "gy")
    halo = (halo_xl, halo_xh, halo_yl, halo_yh)
    inside = jnp.stack(
        [index_first > 0, index_first < count_first - 1, index_second > 0, index_second < count_second - 1]
    ).astype(F32)

    send_choice, own_choice = choices(halo_yl, halo_yh, code, edge, slots)
    z = jnp.arange(nz)
    band = (z[:, None] == z[None] + 1).astype(BF16) - (z[:, None] == z[None] - 1).astype(BF16)

    columns = (t_lo, template, t_hi)
    half = nx // 4
    groups = (((0, half), (nx - half, nx)), ((half, nx - half),))
    to_left_a, to_right_a = pick(columns, send_choice, groups[0], "pick_outer")
    from_left_a = forward(to_right_a, "gy")
    from_right_a = backward(to_left_a, "gy")
    columns, _ = lax.optimization_barrier((columns, to_left_a))
    to_left_b, to_right_b = pick(columns, send_choice, groups[1], "pick_inner")
    from_left_b = forward(to_right_b, "gy")
    from_right_b = backward(to_left_b, "gy")
    late_choice, late_mismatch, _ = lax.optimization_barrier((own_choice, mismatch, to_left_b))
    adj_one, *halo_one = upwind_one(inside, late_mismatch, velocity, halo)
    adj_zero, low_x, high_x, low_y, high_y = upwind_zero(adj_one, velocity, halo_one, halo)
    (own,) = pick(columns, late_choice, ((0, nx),), "pick_own")

    ins = (own, from_left_a, from_right_a, low_x, high_x)
    low, high = call(
        functools.partial(outer_kernel, nx, 2 * half),
        [struct((5, ny, nz), BF16)] * 2, [], "outer", [whole(a.shape) for a in ins]
    )(*ins)
    x_lo = forward(high, "gx")
    x_hi = backward(low, "gx")

    images = (own, from_left_a, from_right_a, from_left_b, from_right_b)
    ins = (*images, x_lo, x_hi, low_y, high_y)
    first, final = call(
        functools.partial(edge_kernel, groups),
        [struct((5, nx + 2, nz), BF16)] * 2,
        [pltpu.VMEM((4, nx + 2, nz), F32)] * 2,
        "edges",
        [whole(a.shape) for a in ins],
    )(*ins)
    y_lo = forward(final, "gy")
    y_hi = backward(first, "gy")
    return force(
        groups, images, band, x_lo, x_hi, y_lo, y_hi, adj_zero, adj_one, halo_one, velocity
    )


def solution(mesh):
    in_specs = (
        P("gx", "gy", None),
        P("gx", "gy", None),
        P(None, None, "gx", "gy", None),
        P(None, "gx", "gy", None),
    )
    out_specs = P(None, None, "gx", "gy", None)
    return jax.shard_map(body, mesh=mesh, in_specs=in_specs, out_specs=out_specs, check_vma=False)
```
